32 devices in a mesh: leaf: 2 (over x), row: 4 (over z), col: 4 (over y, core).
Axes of the slice: x: 2, y: 2, z: 4, core: 2. Of those that a mesh axis runs over, the one named last changes fastest.
Arguments:
- tokens: bfloat16 [768, 20480], P('col', ('leaf', 'row')), may hold values from -6 to 6
- memory: bfloat16 [128, 768], P('leaf', 'col'), may hold values from -6 to 6
- parents: int32 [80], P('leaf'), may hold values from -1 to 39, as said below
- memory_slots: int32 [80, 20], P('leaf'), may hold values from 0 to 63, as said below
- query_weight: bfloat16 [768, 768], P('col', 'row'), may hold values from -0.21875 to 0.21875
- query_bias: bfloat16 [768], P('row'), may hold values from -3 to 3
- key_weight: bfloat16 [768, 768], P('col', 'row'), may hold values from -0.21875 to 0.21875
- value_weight: bfloat16 [768, 768], P('col', 'row'), may hold values from -0.21875 to 0.21875
- value_bias: bfloat16 [768], P('row'), may hold values from -3 to 3
- out_weight: bfloat16 [768, 768], P('row', 'col'), may hold values from -1.75 to 1.75
- out_bias: bfloat16 [768], P('col'), may hold values from -2 to 2
- norm_gain: bfloat16 [768], P('col'), may hold values from 0.5 to 1.5
- norm_shift: bfloat16 [768], P('col'), may hold values from -2 to 2
- up_weight: bfloat16 [768, 3072], P('col', 'row'), may hold values from -0.21875 to 0.21875
- up_bias: bfloat16 [3072], P('row'), may hold values from -2 to 2
- down_weight: bfloat16 [768, 3072], P('col', 'row'), may hold values from -0.109375 to 0.109375
- down_bias: bfloat16 [768], P('col'), may hold values from -2 to 2
- final_gain: bfloat16 [768], P('col'), may hold values from 0.5 to 1.5
- final_shift: bfloat16 [768], P('col'), may hold values from -2 to 2
- cotangent: bfloat16 [768, 20480], P('col', ('leaf', 'row')), may hold values from -6 to 6
Outputs:
- layer_output: bfloat16 [768, 20480], P('col', ('leaf', 'row'))
- tokens_grad: float32 [768, 20480], P('col', ('leaf', 'row'))
- memory_grad: float32 [128, 768], P('leaf', 'col')
- query_weight_grad: float32 [768, 768], P('col', 'row')
- query_bias_grad: float32 [768], P('row')
- key_weight_grad: float32 [768, 768], P('col', 'row')
- value_weight_grad: float32 [768, 768], P('col', 'row')
- value_bias_grad: float32 [768], P('row')
- out_weight_grad: float32 [768, 768], P('row', 'col')
- out_bias_grad: float32 [768], P('col')
- norm_gain_grad: float32 [768], P('col')
- norm_shift_grad: float32 [768], P('col')
- up_weight_grad: float32 [768, 3072], P('col', 'row')
- up_bias_grad: float32 [3072], P('row')
- down_weight_grad: float32 [768, 3072], P('col', 'row')
- down_bias_grad: float32 [768], P('col')
- final_gain_grad: float32 [768], P('col')
- final_shift_grad: float32 [768], P('col')
The draws below stay inside these ranges and needn't reach their ends.
Inputs may be any that keep to these rules, and one draw needn't show every extreme that they name: `parents`: segment s of a group of 2 trees belongs to tree s mod 2; each tree has 8 trunk segments in a chain from a root, whose parent is -1, 4 branch segments whose parent is the trunk's last, and 2 leaf segments under each branch; a parent is numbered within the group. `memory_slots`: the memory rows of a segment of tree t lie in rows t * 32 to (t + 1) * 32 - 1 of its group's memory rows, numbered within the group; every memory row is named by some segment.
All inputs are finite; a program needn't handle non-finite values.
Results may differ from the reference program's by a relative error of at most 0.019.
Values may be sent and summed in bfloat16 or wider, within the bound.
No kernel may reach another device: no remote copies, remote signals or barrier semaphores. Data moves between devices by JAX's collectives and lax.ppermute only.
A program may use at most 192 MiB of HBM per device.

```python
import jax
import jax.numpy as jnp
import numpy as np
from jax import lax

D = 768
HEADS = 12
HEAD = 64
FF = 3072
SEG = 256
MEM_SEG = 20
MEM_T = 32
TRUNK = 8
BRANCHES = 4
LEAVES = 2
TREES_DEV = 2
SEGS_TREE = 20
SEG_GROUP = 40
TREES = 4
TOKENS = 20480


def parent_roles():
    table = np.zeros((SEGS_TREE,), np.int32)
    for role in range(SEGS_TREE):
        if role < TRUNK:
            table[role] = role - 1
        elif role < TRUNK + BRANCHES:
            table[role] = TRUNK - 1
        else:
            table[role] = TRUNK + (role - TRUNK - BRANCHES) // LEAVES
    return table


def draw_parents(key, part):
    groups = TREES // TREES_DEV
    table = jnp.asarray(parent_roles())

    def one_group(index):
        group_key = jax.random.fold_in(jax.random.fold_in(key, 17), index)
        tree_keys = jax.random.split(group_key, TREES_DEV)
        roles = jax.vmap(lambda tree_key: jax.random.permutation(tree_key, SEGS_TREE))(tree_keys).astype(jnp.int32)
        rank_of_role = jnp.argsort(roles, axis=1, stable=True).astype(jnp.int32)
        parent_role = table[roles]
        parent_rank = jnp.take_along_axis(rank_of_role, jnp.maximum(parent_role, 0), axis=1)
        tree_number = jnp.arange(TREES_DEV, dtype=jnp.int32)[:, None]
        parent_slot = jnp.where(parent_role >= 0, parent_rank * TREES_DEV + tree_number, -1)
        return parent_slot.T.reshape(-1)
    return jax.vmap(one_group)(jnp.arange(groups, dtype=jnp.int32)).reshape(-1).astype(jnp.int32)


def draw_memory_slots(key, part):
    groups = TREES // TREES_DEV

    def one_group(index):
        group_key = jax.random.fold_in(jax.random.fold_in(key, 29), index)
        tree_keys = jax.random.split(group_key, TREES_DEV)
        usage_table = jax.vmap(lambda tree_key: jax.random.permutation(tree_key, SEGS_TREE * MEM_SEG))(tree_keys) % MEM_T
        usage_table = usage_table + (jnp.arange(TREES_DEV, dtype=jnp.int32) * MEM_T)[:, None]
        usage_table = usage_table.reshape(TREES_DEV, SEGS_TREE, MEM_SEG).transpose(1, 0, 2)
        return usage_table.reshape(-1, MEM_SEG)
    return jax.vmap(one_group)(jnp.arange(groups, dtype=jnp.int32)).reshape(-1, MEM_SEG).astype(jnp.int32)


def level_of(stream_key, dims, pieces, smallest, top_value):
    factor_of = 1.0
    for position, shards_of in pieces:
        heights = jax.random.uniform(jax.random.fold_in(jax.random.fold_in(stream_key, 6), position), (shards_of,), jnp.float32, smallest / len(pieces), top_value / len(pieces))
        factor_of = factor_of * jnp.repeat(jnp.exp(heights), dims[position] // shards_of).reshape((-1,) + (1,) * (len(dims) - 1 - position))
    return factor_of


def gaussian(key, dims, scale, limit, shards=(), kind=jnp.bfloat16):
    level = level_of(key, dims, shards, -0.22, 0.18) if shards else 1.0
    values = jax.random.normal(key, dims, jnp.float32) * scale * level
    return jnp.minimum(jnp.maximum(values, -limit), limit).astype(kind)


def setup_inputs(seed: int = 0) -> dict:
    key_list = jax.random.split(jax.random.key(seed), 21)
    tokens = gaussian(key_list[0], (D, TOKENS), 1.0, 6.0, ((0, 4), (1, 8)))
    memory = gaussian(key_list[1], (TREES * MEM_T, D), 1.0, 6.0, ((0, 2), (1, 4)))
    parents = draw_parents(jax.random.fold_in(key_list[20], 71), 0)
    memory_slots = draw_memory_slots(jax.random.fold_in(key_list[20], 71), 0)
    query_weight = gaussian(key_list[4], (D, D), D ** -0.5, 0.21875, ((0, 4), (1, 4)))
    query_bias = gaussian(key_list[5], (D,), 0.5, 3.0, ((0, 4),))
    key_weight = gaussian(key_list[6], (D, D), D ** -0.5, 0.21875, ((0, 4), (1, 4)))
    value_weight = gaussian(key_list[7], (D, D), D ** -0.5, 0.21875, ((0, 4), (1, 4)))
    value_bias = gaussian(key_list[8], (D,), 0.5, 3.0, ((0, 4),))
    out_weight = gaussian(key_list[9], (D, D), (max(D // 64, 1)) ** -0.5, 1.75, ((0, 4), (1, 4)))
    out_bias = gaussian(key_list[10], (D,), 0.3, 2.0, ((0, 4),))
    norm_gain = jnp.clip(1.0 + 0.1 * jax.random.normal(key_list[11], (D,), jnp.float32), 0.5, 1.5).astype(jnp.bfloat16)
    norm_shift = gaussian(key_list[12], (D,), 0.3, 2.0, ((0, 4),))
    up_weight = gaussian(key_list[13], (D, FF), D ** -0.5, 0.21875, ((0, 4), (1, 4)))
    up_bias = gaussian(key_list[14], (FF,), 0.3, 2.0, ((0, 4),))
    down_weight = gaussian(key_list[15], (D, FF), FF ** -0.5, 0.109375, ((0, 4), (1, 4)))
    down_bias = gaussian(key_list[16], (D,), 0.3, 2.0, ((0, 4),))
    final_gain = jnp.clip(1.0 + 0.1 * jax.random.normal(key_list[17], (D,), jnp.float32), 0.5, 1.5).astype(jnp.bfloat16)
    final_shift = gaussian(key_list[18], (D,), 0.3, 2.0, ((0, 4),))
    cotangent = gaussian(key_list[19], (D, TOKENS), 1.0, 6.0, ((0, 4), (1, 8)))
    return dict(tokens=tokens, memory=memory, parents=parents, memory_slots=memory_slots, query_weight=query_weight, query_bias=query_bias, key_weight=key_weight, value_weight=value_weight, value_bias=value_bias, out_weight=out_weight, out_bias=out_bias, norm_gain=norm_gain, norm_shift=norm_shift, up_weight=up_weight, up_bias=up_bias, down_weight=down_weight, down_bias=down_bias, final_gain=final_gain, final_shift=final_shift, cotangent=cotangent)


@jax.custom_vjp
def low(v):
    return lax.optimization_barrier(v.astype(jnp.bfloat16)).astype(jnp.float32)

@jax.custom_vjp
def low_back(v):
    return v

def low_keep(v):
    return (low(v), None)

def low_pass(kept, grad):
    return (grad,)

def back_keep(v):
    return (v, None)

def back_low(kept, grad):
    return (low(grad),)
low.defvjp(low_keep, low_pass)
low_back.defvjp(back_keep, back_low)
NEGATIVE = -1e+30
EPSILON = 1e-05

def matmul(left, right):
    return jnp.dot(left, right, precision=lax.Precision.HIGHEST, preferred_element_type=jnp.float32)

def layer_norm(values, gain, shift):
    center = lax.optimization_barrier(jnp.mean(values, axis=-1, keepdims=True))
    spread = lax.optimization_barrier(jnp.mean(values * values, axis=-1, keepdims=True)) - center * center
    return (values - center) * lax.rsqrt(spread + EPSILON) * gain + shift

def attend(queries, keys, values, memory_keys, memory_values, parent_all, slot_all):
    count = queries.shape[0] // SEG
    query_seg = queries.reshape(count, SEG, HEADS, HEAD)
    key_seg = keys.reshape(count, SEG, HEADS, HEAD)
    value_seg = values.reshape(count, SEG, HEADS, HEAD)
    memory_key_rows = memory_keys.reshape(-1, HEADS, HEAD)
    memory_value_rows = memory_values.reshape(-1, HEADS, HEAD)

    def one_segment(index):
        parent = parent_all[index]
        safe_parent = jnp.maximum(parent, 0)
        chosen = slot_all[index]
        key_rows = jnp.concatenate([memory_key_rows[chosen], key_seg[safe_parent], key_seg[index]], axis=0)
        value_rows = jnp.concatenate([memory_value_rows[chosen], value_seg[safe_parent], value_seg[index]], axis=0)
        raw = jnp.einsum('qhd,khd->hqk', query_seg[index], key_rows, precision=lax.Precision.HIGHEST)
        raw = low_back(raw)
        valid = jnp.concatenate([jnp.ones((MEM_SEG,), bool), jnp.full((SEG,), parent >= 0), jnp.ones((SEG,), bool)])
        scores = jnp.where(valid[None, None, :], raw * HEAD ** (-0.5), NEGATIVE)
        top = lax.optimization_barrier(jnp.max(scores, axis=-1, keepdims=True))
        weights = jnp.exp(scores - top)
        probs = low(weights / lax.optimization_barrier(jnp.sum(weights, axis=-1, keepdims=True)))
        return jnp.einsum('hqk,khd->qhd', probs, value_rows, precision=lax.Precision.HIGHEST)
    mixed = lax.map(jax.checkpoint(one_segment), jnp.arange(count, dtype=jnp.int32))
    return low(low_back(mixed.reshape(queries.shape[0], HEADS * HEAD)))

def forward(tokens, memory, query_weight, query_bias, key_weight, value_weight, value_bias, out_weight, out_bias, norm_gain, norm_shift, up_weight, up_bias, down_weight, down_bias, final_gain, final_shift, parent_all, slot_all):
    queries = low(low_back(matmul(tokens, query_weight) + query_bias))
    keys = low(low_back(matmul(tokens, key_weight)))
    values = low(low_back(matmul(tokens, value_weight) + value_bias))
    memory_keys = low(low_back(matmul(memory, key_weight)))
    memory_values = low(low_back(matmul(memory, value_weight) + value_bias))
    context = attend(queries, keys, values, memory_keys, memory_values, parent_all, slot_all)
    attended = low_back(matmul(context, out_weight) + out_bias) + tokens
    hidden = layer_norm(attended, norm_gain, norm_shift)
    upper = low_back(matmul(low(hidden), up_weight) + up_bias)
    active = low(jax.nn.gelu(upper, approximate=False))
    second = low_back(matmul(active, down_weight) + down_bias) + hidden
    return layer_norm(second, final_gain, final_shift)

def reference(tokens, memory, parents, memory_slots, query_weight, query_bias, key_weight, value_weight, value_bias, out_weight, out_bias, norm_gain, norm_shift, up_weight, up_bias, down_weight, down_bias, final_gain, final_shift, cotangent):
    group = jnp.arange(parents.shape[0], dtype=jnp.int32) // SEG_GROUP
    parent_all = jnp.where(parents >= 0, parents + group * SEG_GROUP, -1).astype(jnp.int32)
    slot_all = (memory_slots + (group * (TREES_DEV * MEM_T))[:, None]).astype(jnp.int32)
    token_major = tokens.astype(jnp.float32).T
    down_major = down_weight.astype(jnp.float32).T
    floats = [token_major] + [array.astype(jnp.float32) for array in (memory, query_weight, query_bias, key_weight, value_weight, value_bias, out_weight, out_bias, norm_gain, norm_shift, up_weight, up_bias)]
    floats = floats + [down_major] + [array.astype(jnp.float32) for array in (down_bias, final_gain, final_shift)]

    def closed(*params):
        return forward(*params, parent_all, slot_all)
    result, pull = jax.vjp(closed, *floats)
    grads = pull(cotangent.astype(jnp.float32).T)
    return (result.T.astype(jnp.bfloat16), grads[0].T, grads[1], grads[2], grads[3], grads[4], grads[5], grads[6], grads[7], grads[8], grads[9], grads[10], grads[11], grads[12], grads[13].T, grads[14], grads[15], grads[16])
```

```python
import functools

import jax
import jax.numpy as jnp
import numpy as np
from jax import lax
from jax.experimental import pallas as pl
from jax.experimental.pallas import tpu as pltpu
from jax.sharding import PartitionSpec as P

HEAD = 64
SEG = 256
NEGATIVE = -1e30
EPSILON = 1e-05
GROUP = ("row", "col")
EVERY = ("leaf", "row", "col")
BF16 = jnp.bfloat16
F32 = jnp.float32


def tn(left, right):
    return lax.dot_general(left, right, (((0,), (0,)), ((), ())), preferred_element_type=F32)


def nt(left, right):
    return lax.dot_general(left, right, (((1,), (1,)), ((), ())), preferred_element_type=F32)


def nn(left, right):
    return lax.dot_general(left, right, (((1,), (0,)), ((), ())), preferred_element_type=F32)


def plan_windows(own, count):
    segments, ranges = [], []
    for index in range(count):
        first, last = index * own, (index + 1) * own
        whole = [s for s in range(first // SEG, -(-last // SEG)) if s * SEG >= first and (s + 1) * SEG <= last]
        cut = [s for s in range(first // SEG, -(-last // SEG)) if s not in whole]
        pieces = [(s * SEG, SEG) for s in whole]
        for s in cut:
            low, high = max(first, s * SEG), min(last, (s + 1) * SEG)
            pieces.append((low, high - low))
            if low > s * SEG:
                pieces.append((s * SEG, low - s * SEG))
            if high < (s + 1) * SEG:
                pieces.append((high, (s + 1) * SEG - high))
        segments.append(whole + cut)
        ranges.append(pieces)
    return segments, ranges


def attention_forward(head_count, lengths, bank, bias_ref, win_ref, par_ref, slot_ref, ctx_ref, lse_ref):
    width = head_count * HEAD
    window = len(lengths) * SEG
    for head in range(head_count):
        low = head * HEAD
        key_mem = win_ref[0, width + low : width + low + HEAD, window : window + bank]
        value_mem = win_ref[0, 2 * width + low : 2 * width + low + HEAD, window : window + bank]
        for j, count in enumerate(lengths):
            cols = slice(j * SEG, (j + 1) * SEG)
            query = win_ref[0, low : low + HEAD, j * SEG : j * SEG + count]
            own = tn(win_ref[0, width + low : width + low + HEAD, cols], query)
            par = tn(par_ref[0, low : low + HEAD, cols], query) + bias_ref[j]
            mem = tn(key_mem, query) + slot_ref[:, j : j + 1]
            top = jnp.maximum(
                jnp.maximum(jnp.max(own, axis=0, keepdims=True), jnp.max(par, axis=0, keepdims=True)),
                jnp.max(mem, axis=0, keepdims=True),
            )
            own, par, mem = jnp.exp(own - top), jnp.exp(par - top), jnp.exp(mem - top)
            total = (
                jnp.sum(own, axis=0, keepdims=True)
                + jnp.sum(par, axis=0, keepdims=True)
                + jnp.sum(mem, axis=0, keepdims=True)
            )
            mixed = (
                nn(win_ref[0, 2 * width + low : 2 * width + low + HEAD, cols], own.astype(BF16))
                + nn(par_ref[0, width + low : width + low + HEAD, cols], par.astype(BF16))
                + nn(value_mem, mem.astype(BF16))
            )
            ctx_ref[0, low : low + HEAD, j * SEG : j * SEG + count] = (mixed / total).astype(BF16)
            lse_ref[0, head : head + 1, j * SEG : j * SEG + count] = top + jnp.log(total)


def attention_backward(
    head_count, lengths, bank, bias_ref, win_ref, par_ref, slot_ref, dctx_ref, lse_ref, dwin_ref, dpar_ref
):
    width = head_count * HEAD
    window = len(lengths) * SEG
    tail = win_ref.shape[2] - window
    for head in range(head_count):
        low = head * HEAD
        qs, ks, vs = (slice(part * width + low, part * width + low + HEAD) for part in range(3))
        key_mem = win_ref[0, ks, window : window + bank]
        value_mem = win_ref[0, vs, window : window + bank]
        dkey_mem = jnp.zeros((HEAD, bank), F32)
        dvalue_mem = jnp.zeros((HEAD, bank), F32)
        for j, count in enumerate(lengths):
            cols = slice(j * SEG, (j + 1) * SEG)
            tok = slice(j * SEG, j * SEG + count)
            query = win_ref[0, qs, tok]
            dctx = dctx_ref[0, low : low + HEAD, tok]
            lse = lse_ref[0, head : head + 1, tok]
            key_own, value_own = win_ref[0, ks, cols], win_ref[0, vs, cols]
            key_par, value_par = par_ref[0, low : low + HEAD, cols], par_ref[0, width + low : width + low + HEAD, cols]
            own = jnp.exp(tn(key_own, query) - lse)
            par = jnp.exp(tn(key_par, query) + bias_ref[j] - lse)
            mem = jnp.exp(tn(key_mem, query) + slot_ref[:, j : j + 1] - lse)
            gown, gpar, gmem = tn(value_own, dctx), tn(value_par, dctx), tn(value_mem, dctx)
            inner = (
                jnp.sum(own * gown, axis=0, keepdims=True)
                + jnp.sum(par * gpar, axis=0, keepdims=True)
                + jnp.sum(mem * gmem, axis=0, keepdims=True)
            )
            gown = (own * (gown - inner)).astype(BF16)
            gpar = (par * (gpar - inner)).astype(BF16)
            gmem = (mem * (gmem - inner)).astype(BF16)
            dquery = nn(key_own, gown) + nn(key_par, gpar) + nn(key_mem, gmem)
            dwin_ref[0, qs, tok] = (dquery * HEAD ** (-0.5)).astype(BF16)
            if count < SEG:
                dwin_ref[0, qs, j * SEG + count : (j + 1) * SEG] = jnp.zeros((HEAD, SEG - count), BF16)
            dwin_ref[0, ks, cols] = nt(query, gown).astype(BF16)
            dwin_ref[0, vs, cols] = nt(dctx, own.astype(BF16)).astype(BF16)
            dpar_ref[0, low : low + HEAD, cols] = nt(query, gpar).astype(BF16)
            dpar_ref[0, width + low : width + low + HEAD, cols] = nt(dctx, par.astype(BF16)).astype(BF16)
            dkey_mem += nt(query, gmem)
            dvalue_mem += nt(dctx, mem.astype(BF16))
        pad = jnp.zeros((HEAD, tail - bank), F32)
        dwin_ref[0, qs, window:] = jnp.zeros((HEAD, tail), BF16)
        dwin_ref[0, ks, window:] = jnp.concatenate([dkey_mem, pad], axis=1).astype(BF16)
        dwin_ref[0, vs, window:] = jnp.concatenate([dvalue_mem, pad], axis=1).astype(BF16)


def step_block(array):
    return pl.BlockSpec((1,) + array.shape[1:], lambda step, *_: (step, 0, 0))


def whole_block(array):
    return pl.BlockSpec(array.shape, lambda step, *_: (0,) * len(array.shape))


def attend(lengths, bank, parent_bias, window, parent, slots):
    groups, rows, columns = window.shape
    width = rows // 3
    own = sum(lengths)
    heads = width // HEAD
    outs = (
        jax.ShapeDtypeStruct((groups, width, own), BF16),
        jax.ShapeDtypeStruct((groups, heads, own), F32),
    )
    return pl.pallas_call(
        functools.partial(attention_forward, heads, lengths, bank),
        grid=(groups,),
        in_specs=[
            pl.BlockSpec(memory_space=pltpu.SMEM),
            step_block(window),
            step_block(parent),
            whole_block(slots),
        ],
        out_specs=[step_block(out) for out in outs],
        out_shape=outs,
        compiler_params=pltpu.CompilerParams(vmem_limit_bytes=40 << 20),
        name="attention_forward",
    )(parent_bias, window, parent, slots)


def attend_back(lengths, bank, parent_bias, window, parent, slots, dctx, lse):
    groups, rows, columns = window.shape
    heads = rows // 3 // HEAD
    outs = (jax.ShapeDtypeStruct(window.shape, BF16), jax.ShapeDtypeStruct(parent.shape, BF16))
    return pl.pallas_call(
        functools.partial(attention_backward, heads, lengths, bank),
        grid=(groups,),
        in_specs=[
            pl.BlockSpec(memory_space=pltpu.SMEM),
            step_block(window),
            step_block(parent),
            whole_block(slots),
            step_block(dctx),
            step_block(lse),
        ],
        out_specs=[step_block(out) for out in outs],
        out_shape=outs,
        compiler_params=pltpu.CompilerParams(vmem_limit_bytes=40 << 20),
        name="attention_backward",
    )(parent_bias, window, parent, slots, dctx, lse)


def copy_block(index_ref, source_ref, out_ref):
    out_ref[...] = source_ref[...]


def pick_parents(parents, gathered, seg_row, per_device):
    count = parents.shape[0]
    feat = gathered.shape[1]
    return pl.pallas_call(
        copy_block,
        grid_spec=pltpu.PrefetchScalarGridSpec(
            num_scalar_prefetch=1,
            grid=(count,),
            in_specs=[
                pl.BlockSpec((1, feat, SEG), lambda n, index: (index[n] // seg_row, 0, index[n] % seg_row)),
            ],
            out_specs=pl.BlockSpec((1, feat, SEG), lambda n, index: (n // per_device, 0, n % per_device)),
        ),
        out_shape=jax.ShapeDtypeStruct((count // per_device, feat, per_device * SEG), gathered.dtype),
        name="pick_parents",
    )(parents, gathered)


def add_parents_kernel(count, seg_row, per_device, bank, index_ref, mem_ref, par_ref, out_ref, sum_ref):
    feat = par_ref.shape[1]
    sum_ref[...] = jnp.zeros(sum_ref.shape, F32)
    for n in range(count):
        seg = index_ref[n]

        @pl.when(seg >= 0)
        def add(n=n, seg=seg):
            block = par_ref[n // per_device, :, (n % per_device) * SEG : (n % per_device + 1) * SEG]
            sum_ref[seg] += block.astype(F32)

    rows = out_ref.shape[0]
    for r in range(rows):
        for s in range(seg_row):
            out_ref[r, :, s * SEG : (s + 1) * SEG] = sum_ref[r * seg_row + s].astype(BF16)
        out_ref[r, :, seg_row * SEG :] = mem_ref[...].astype(BF16)


def add_parents(parents, mem, contributions, rows, seg_row, per_device):
    count = parents.shape[0]
    feat, bank = mem.shape
    out = jax.ShapeDtypeStruct((rows, feat, seg_row * SEG + bank), BF16)
    return pl.pallas_call(
        functools.partial(add_parents_kernel, count, seg_row, per_device, bank),
        in_specs=[
            pl.BlockSpec(memory_space=pltpu.SMEM),
            pl.BlockSpec(memory_space=pltpu.VMEM),
            pl.BlockSpec(memory_space=pltpu.VMEM),
        ],
        out_specs=pl.BlockSpec(memory_space=pltpu.VMEM),
        out_shape=out,
        scratch_shapes=[pltpu.VMEM((rows * seg_row, feat, SEG), F32)],
        compiler_params=pltpu.CompilerParams(vmem_limit_bytes=40 << 20),
        name="add_parents",
    )(parents, mem, contributions)


def exchange(blocks):
    return lax.all_to_all(blocks, "col", 0, 0, tiled=True)


def norm_stats(values):
    center = jnp.mean(values, axis=0, keepdims=True)
    spread = jnp.mean(values * values, axis=0, keepdims=True) - center * center
    return center, lax.rsqrt(spread + EPSILON)


def norm_back(grad, normed, scale, gain):
    scaled = grad * gain
    return scale * (
        scaled
        - jnp.mean(scaled, axis=0, keepdims=True)
        - normed * jnp.mean(scaled * normed, axis=0, keepdims=True)
    )


def lane_sum(array):
    return jnp.sum(array, axis=-1, dtype=F32)


def on_device(
    tokens,
    memory,
    parents,
    memory_slots,
    query_weight,
    query_bias,
    key_weight,
    value_weight,
    value_bias,
    out_weight,
    out_bias,
    norm_gain,
    norm_shift,
    up_weight,
    up_bias,
    down_weight,
    down_bias,
    final_gain,
    final_shift,
    cotangent,
):
    rows, cols = lax.axis_size("row"), lax.axis_size("col")
    row, col = lax.axis_index("row"), lax.axis_index("col")
    feat, row_tokens = tokens.shape
    own = row_tokens // cols
    seg_row = row_tokens // SEG
    model = feat * cols
    width = query_weight.shape[1]
    hidden_width = up_weight.shape[1]
    bank = memory.shape[0]
    segments, ranges = plan_windows(own, cols)
    per_device = len(segments[0])
    window = per_device * SEG
    lengths = tuple(min(SEG, own - j * SEG) for j in range(per_device))

    first_shard = jnp.concatenate([query_weight, key_weight, value_weight, out_weight.T], axis=1)
    first = lax.all_gather(first_shard, GROUP, axis=0, tiled=True).reshape(rows, model, -1)
    up = lax.all_gather(up_weight, GROUP, axis=0, tiled=True).reshape(rows, model, -1)
    down = lax.all_gather(down_weight, GROUP, axis=0, tiled=True).reshape(rows, model, -1)

    def window_of(array, index):
        return jnp.concatenate([array[:, a : a + n] for a, n in ranges[index]], axis=1)

    vectors = jnp.stack([out_bias, norm_gain, norm_shift, down_bias, final_gain, final_shift], axis=1)
    tail = -(-(bank + vectors.shape[1]) // 128) * 128
    side = jnp.concatenate(
        [memory.T, vectors, jnp.zeros((feat, tail - bank - vectors.shape[1]), BF16)], axis=1
    )
    sent = jnp.stack([jnp.concatenate([window_of(tokens, i), side], axis=1) for i in range(cols)])
    tok_window = exchange(sent).reshape(model, window + tail)
    grad_out = exchange(jnp.stack([window_of(cotangent, i)[:, :own] for i in range(cols)]))
    grad_out = grad_out.reshape(model, own).astype(F32)
    column = lambda i: tok_window[:, window + bank + i : window + bank + i + 1].astype(F32)
    out_b, gain_1, shift_1, down_b, gain_2, shift_2 = (column(i) for i in range(6))

    row_vectors = jnp.concatenate(
        [query_bias[:, None], value_bias[:, None], up_bias.reshape(-1, feat).T], axis=1
    )
    row_side = jnp.concatenate([row_vectors, jnp.zeros((feat, 128 - row_vectors.shape[1]), BF16)], axis=1)
    everything = lax.all_gather(jnp.concatenate([tokens, row_side], axis=1), "row", axis=0)
    row_cols = everything[:, :, row_tokens : row_tokens + row_vectors.shape[1]].astype(F32)
    query_b, value_b = row_cols[:, :, 0:1], row_cols[:, :, 1:2]
    up_b = row_cols[:, :, 2:].transpose(0, 2, 1).reshape(rows, hidden_width, 1)

    row_parents = lax.dynamic_slice_in_dim(parents, row * seg_row, seg_row, 0)
    row_slots = lax.dynamic_slice_in_dim(memory_slots, row * seg_row, seg_row, 0)
    chosen = np.array(segments, np.int32)
    pick = (chosen.reshape(-1)[:, None] == np.arange(seg_row)[None, :]).astype(np.int32)
    all_parents = jnp.sum(pick * row_parents[None, :], axis=1)
    own_pick = lax.dynamic_index_in_dim(
        jnp.asarray(pick.reshape(cols, per_device, seg_row)), col, 0, keepdims=False
    )
    own_parents = jnp.sum(own_pick * row_parents[None, :], axis=1)
    parent_bias = jnp.where(own_parents >= 0, 0.0, NEGATIVE).astype(F32)
    counts = jnp.sum((row_slots[:, :, None] == jnp.arange(bank)[None, None, :]).astype(F32), axis=1)
    own_counts = jnp.sum(own_pick[:, :, None].astype(F32) * counts[None], axis=1)
    slots = jnp.where(own_counts > 0, jnp.log(jnp.maximum(own_counts, 1.0)), NEGATIVE).T

    par_sent = pick_parents(jnp.maximum(all_parents, 0), everything, seg_row, per_device)
    tok_parent = exchange(par_sent).reshape(model, window)

    def project(block, toks):
        return jnp.einsum("rdf,dt->rft", block, toks, preferred_element_type=F32)

    scale = HEAD ** (-0.5)
    joint = project(first[:, :, : 3 * width], tok_window)
    win = jnp.concatenate(
        [
            (joint[:, :width] + query_b).astype(BF16) * jnp.asarray(scale, BF16),
            joint[:, width : 2 * width].astype(BF16),
            (joint[:, 2 * width :] + value_b).astype(BF16),
        ],
        axis=1,
    )
    joint_par = project(first[:, :, width : 3 * width], tok_parent)
    par = jnp.concatenate(
        [joint_par[:, :width].astype(BF16), (joint_par[:, width:] + value_b).astype(BF16)], axis=1
    )
    ctx, lse = attend(lengths, bank, parent_bias, win, par, slots)
    out_t = first[:, :, 3 * width :].transpose(1, 0, 2).reshape(model, rows * width)
    ctx = ctx.reshape(rows * width, own)
    tok_own = tok_window[:, :own].astype(F32)
    attended = nn(out_t, ctx) + out_b + tok_own
    center_1, scale_1 = norm_stats(attended)
    normed_1 = (attended - center_1) * scale_1
    hidden = normed_1 * gain_1 + shift_1
    hidden_low = hidden.astype(BF16)
    upper = project(up, hidden_low) + up_b
    phi = 0.5 * (1.0 + lax.erf(upper * np.float32(0.5**0.5)))
    active = (upper * phi).astype(BF16)
    slope = phi + upper * jnp.exp(-0.5 * upper * upper) * np.float32(1.0 / np.sqrt(2.0 * np.pi))
    second = jnp.einsum("rdj,rjt->dt", down, active, preferred_element_type=F32) + down_b + hidden
    center_2, scale_2 = norm_stats(second)
    normed_2 = (second - center_2) * scale_2
    result = (normed_2 * gain_2 + shift_2).astype(BF16)

    second_grad = norm_back(grad_out, normed_2, scale_2, gain_2)
    final_gain_grad = lane_sum(grad_out * normed_2)
    final_shift_grad = lane_sum(grad_out)
    down_low = second_grad.astype(BF16)
    down_grad = jnp.einsum("dt,rjt->rdj", down_low, active, preferred_element_type=F32)
    down_bias_grad = lane_sum(down_low)
    upper_low = (project(down, down_low) * slope).astype(BF16)
    up_grad = jnp.einsum("dt,rjt->rdj", hidden_low, upper_low, preferred_element_type=F32)
    up_bias_grad = lane_sum(upper_low).reshape(-1)
    hidden_grad = jnp.einsum("rdj,rjt->dt", up, upper_low, preferred_element_type=F32) + second_grad
    first_grad = norm_back(hidden_grad, normed_1, scale_1, gain_1)
    norm_gain_grad = lane_sum(hidden_grad * normed_1)
    norm_shift_grad = lane_sum(hidden_grad)
    first_low = first_grad.astype(BF16)
    out_bias_grad = lane_sum(first_low)
    out_grad = nt(first_low, ctx).reshape(model, rows, width).transpose(1, 0, 2)
    dctx = tn(out_t, first_low).astype(BF16).reshape(rows, width, own)
    dwin, dpar = attend_back(lengths, bank, parent_bias, win, par, slots, dctx, lse)

    joint_grad = jnp.einsum("dt,rft->rdf", tok_window, dwin, preferred_element_type=F32)
    par_grad = jnp.einsum("dt,rft->rdf", tok_parent, dpar, preferred_element_type=F32)
    first_grads = jnp.concatenate(
        [joint_grad[:, :, :width], joint_grad[:, :, width:] + par_grad, out_grad], axis=2
    ).astype(BF16)
    query_bias_grad = lane_sum(dwin[:, :width]).reshape(-1)
    value_bias_grad = (lane_sum(dwin[:, 2 * width :]) + lane_sum(dpar[:, width:])).reshape(-1)

    dtok = jnp.einsum("rdf,rft->dt", first[:, :, : 3 * width], dwin, preferred_element_type=F32)
    dtok = dtok.at[:, :own].add(first_grad).astype(BF16)
    dtok_par = jnp.einsum("rdf,rft->dt", first[:, :, width : 3 * width], dpar, preferred_element_type=F32)
    back = exchange(jnp.concatenate([dtok, dtok_par.astype(BF16)], axis=1).reshape(cols, feat, -1))
    mem_part = jnp.sum(back[:, :, window : window + 128].astype(F32), axis=0)
    placed = add_parents(all_parents, mem_part, back[:, :, window + tail :], rows, seg_row, per_device)
    placed = lax.psum_scatter(placed, "row", scatter_dimension=0, tiled=False).astype(F32)
    memory_grad = placed[:, row_tokens : row_tokens + bank].T
    pieces = []
    step = np.gcd(own, SEG)
    for start in range(0, row_tokens, step):
        total = placed[:, start : start + step]
        for i in range(cols):
            at = 0
            for a, n in ranges[i]:
                if a <= start < a + n:
                    total = total + back[i, :, at + start - a : at + start - a + step].astype(F32)
                at += n
        pieces.append(total)
    tokens_grad = jnp.concatenate(pieces, axis=1)

    returned = exchange(result.reshape(cols, feat, own))
    order = {}
    for i in range(cols):
        at = 0
        for a, n in ranges[i]:
            if at < own:
                order[a] = (i, at, n)
            at += n
    layer_output = jnp.concatenate(
        [returned[i, :, at : at + n] for a, (i, at, n) in sorted(order.items())], axis=1
    )

    def reduce_weights(grads):
        mine = lax.psum_scatter(grads.reshape(-1, grads.shape[-1]), GROUP, scatter_dimension=0, tiled=True)
        return lax.psum(mine, "leaf").astype(F32)

    down_total = reduce_weights(down_grad.astype(BF16))
    up_total = reduce_weights(up_grad.astype(BF16))
    first_total = reduce_weights(first_grads)
    sums = lax.psum(
        jnp.concatenate(
            [
                query_bias_grad,
                value_bias_grad,
                out_bias_grad,
                norm_gain_grad,
                norm_shift_grad,
                up_bias_grad,
                down_bias_grad,
                final_gain_grad,
                final_shift_grad,
            ]
        ),
        EVERY,
    )

    def part(offset, length, index):
        return lax.dynamic_slice_in_dim(sums, offset + index * length, length, 0)

    return (
        layer_output,
        tokens_grad,
        memory_grad,
        first_total[:, :width],
        part(0, width, row),
        first_total[:, width : 2 * width],
        first_total[:, 2 * width : 3 * width],
        part(model, width, row),
        first_total[:, 3 * width :].T,
        part(2 * model, feat, col),
        part(3 * model, feat, col),
        part(4 * model, feat, col),
        up_total,
        part(5 * model, hidden_width, row),
        down_total,
        part(5 * model + rows * hidden_width, feat, col),
        part(6 * model + rows * hidden_width, feat, col),
        part(7 * model + rows * hidden_width, feat, col),
    )


def solution(mesh):
    return jax.shard_map(
        on_device,
        mesh=mesh,
        in_specs=(
            P("col", ("leaf", "row")),
            P("leaf", "col"),
            P("leaf"),
            P("leaf", None),
            P("col", "row"),
            P("row"),
            P("col", "row"),
            P("col", "row"),
            P("row"),
            P("row", "col"),
            P("col"),
            P("col"),
            P("col"),
            P("col", "row"),
            P("row"),
            P("col", "row"),
            P("col"),
            P("col"),
            P("col"),
            P("col", ("leaf", "row")),
        ),
        out_specs=(
            P("col", ("leaf", "row")),
            P("col", ("leaf", "row")),
            P("leaf", "col"),
            P("col", "row"),
            P("row"),
            P("col", "row"),
            P("col", "row"),
            P("row"),
            P("row", "col"),
            P("col"),
            P("col"),
            P("col"),
            P("col", "row"),
            P("row"),
            P("col", "row"),
            P("col"),
            P("col"),
            P("col"),
        ),
        check_vma=False,
    )
```

```python
import functools

import jax
import jax.numpy as jnp
import numpy as np
from jax import lax
from jax.experimental import pallas as pl
from jax.experimental.pallas import tpu as pltpu
from jax.sharding import PartitionSpec as P

HEAD = 64
SEG = 256
NEGATIVE = -1e30
EPSILON = 1e-05
EVERY = ("leaf", "row", "col")
BF16 = jnp.bfloat16
F32 = jnp.float32


def after(value, *others):
    return lax.optimization_barrier((value, others))[0]


def tn(left, right):
    return lax.dot_general(left, right, (((0,), (0,)), ((), ())), preferred_element_type=F32)


def nt(left, right):
    return lax.dot_general(left, right, (((1,), (1,)), ((), ())), preferred_element_type=F32)


def nn(left, right):
    return lax.dot_general(left, right, (((1,), (0,)), ((), ())), preferred_element_type=F32)


def plan_windows(own, count):
    segments, ranges = [], []
    for index in range(count):
        first, last = index * own, (index + 1) * own
        whole = [s for s in range(first // SEG, -(-last // SEG)) if s * SEG >= first and (s + 1) * SEG <= last]
        cut = [s for s in range(first // SEG, -(-last // SEG)) if s not in whole]
        pieces = [(s * SEG, SEG) for s in whole]
        for s in cut:
            low, high = max(first, s * SEG), min(last, (s + 1) * SEG)
            pieces.append((low, high - low))
            if low > s * SEG:
                pieces.append((s * SEG, low - s * SEG))
            if high < (s + 1) * SEG:
                pieces.append((high, (s + 1) * SEG - high))
        segments.append(whole + cut)
        ranges.append(pieces)
    return segments, ranges


def static_of(index, values):
    out = jnp.int32(values[0])
    for i, value in enumerate(values[1:], 1):
        out = jnp.where(index == i, jnp.int32(value), out)
    return out


def own_segments(segments, here_ref):
    return [
        here_ref[0] * here_ref[3] + static_of(here_ref[1], [lists[j] for lists in segments])
        for j in range(len(segments[0]))
    ]


def window_biases(segments, bank, here_ref, parents_ref, slots_ref):
    rows = lax.broadcasted_iota(jnp.int32, (bank, 1), 0)
    out = []
    for seg in own_segments(segments, here_ref):
        count = jnp.zeros((bank, 1), F32)
        for m in range(slots_ref.shape[1]):
            count = count + jnp.where(rows == slots_ref[seg, m], 1.0, 0.0)
        slot = jnp.where(count > 0, jnp.log(jnp.maximum(count, 1.0)), NEGATIVE)
        out.append((jnp.where(parents_ref[seg] >= 0, 0.0, NEGATIVE).astype(F32), slot))
    return out


def attention_forward(
    head_count, lengths, segments, bank, here_ref, parents_ref, slots_ref, win_ref, par_ref, ctx_ref, lse_ref
):
    width = head_count * HEAD
    biases = window_biases(segments, bank, here_ref, parents_ref, slots_ref)
    window = len(lengths) * SEG
    for head in range(head_count):
        low = head * HEAD
        key_mem = win_ref[0, width + low : width + low + HEAD, window : window + bank]
        value_mem = win_ref[0, 2 * width + low : 2 * width + low + HEAD, window : window + bank]
        for j, count in enumerate(lengths):
            cols = slice(j * SEG, (j + 1) * SEG)
            query = win_ref[0, low : low + HEAD, j * SEG : j * SEG + count]
            own = tn(win_ref[0, width + low : width + low + HEAD, cols], query)
            par = tn(par_ref[0, low : low + HEAD, cols], query) + biases[j][0]
            mem = tn(key_mem, query) + biases[j][1]
            top = jnp.maximum(
                jnp.maximum(jnp.max(own, axis=0, keepdims=True), jnp.max(par, axis=0, keepdims=True)),
                jnp.max(mem, axis=0, keepdims=True),
            )
            own, par, mem = jnp.exp(own - top), jnp.exp(par - top), jnp.exp(mem - top)
            total = (
                jnp.sum(own, axis=0, keepdims=True)
                + jnp.sum(par, axis=0, keepdims=True)
                + jnp.sum(mem, axis=0, keepdims=True)
            )
            mixed = (
                nn(win_ref[0, 2 * width + low : 2 * width + low + HEAD, cols], own.astype(BF16))
                + nn(par_ref[0, width + low : width + low + HEAD, cols], par.astype(BF16))
                + nn(value_mem, mem.astype(BF16))
            )
            ctx_ref[0, low : low + HEAD, j * SEG : j * SEG + count] = (mixed / total).astype(BF16)
            lse_ref[0, head : head + 1, j * SEG : j * SEG + count] = top + jnp.log(total)


def attention_backward(
    head_count,
    lengths,
    segments,
    bank,
    here_ref,
    parents_ref,
    slots_ref,
    win_ref,
    par_ref,
    dctx_ref,
    lse_ref,
    dwin_ref,
    dpar_ref,
):
    width = head_count * HEAD
    biases = window_biases(segments, bank, here_ref, parents_ref, slots_ref)
    window = len(lengths) * SEG
    tail = win_ref.shape[2] - window
    for head in range(head_count):
        low = head * HEAD
        qs, ks, vs = (slice(part * width + low, part * width + low + HEAD) for part in range(3))
        key_mem = win_ref[0, ks, window : window + bank]
        value_mem = win_ref[0, vs, window : window + bank]
        dkey_mem = jnp.zeros((HEAD, bank), F32)
        dvalue_mem = jnp.zeros((HEAD, bank), F32)
        for j, count in enumerate(lengths):
            cols = slice(j * SEG, (j + 1) * SEG)
            tok = slice(j * SEG, j * SEG + count)
            query = win_ref[0, qs, tok]
            dctx = dctx_ref[0, low : low + HEAD, tok]
            lse = lse_ref[0, head : head + 1, tok]
            key_own, value_own = win_ref[0, ks, cols], win_ref[0, vs, cols]
            key_par, value_par = par_ref[0, low : low + HEAD, cols], par_ref[0, width + low : width + low + HEAD, cols]
            own = jnp.exp(tn(key_own, query) - lse)
            par = jnp.exp(tn(key_par, query) + biases[j][0] - lse)
            mem = jnp.exp(tn(key_mem, query) + biases[j][1] - lse)
            gown, gpar, gmem = tn(value_own, dctx), tn(value_par, dctx), tn(value_mem, dctx)
            inner = (
                jnp.sum(own * gown, axis=0, keepdims=True)
                + jnp.sum(par * gpar, axis=0, keepdims=True)
                + jnp.sum(mem * gmem, axis=0, keepdims=True)
            )
            gown = (own * (gown - inner)).astype(BF16)
            gpar = (par * (gpar - inner)).astype(BF16)
            gmem = (mem * (gmem - inner)).astype(BF16)
            dquery = nn(key_own, gown) + nn(key_par, gpar) + nn(key_mem, gmem)
            dwin_ref[0, qs, tok] = (dquery * HEAD ** (-0.5)).astype(BF16)
            if count < SEG:
                dwin_ref[0, qs, j * SEG + count : (j + 1) * SEG] = jnp.zeros((HEAD, SEG - count), BF16)
            dwin_ref[0, ks, cols] = nt(query, gown).astype(BF16)
            dwin_ref[0, vs, cols] = nt(dctx, own.astype(BF16)).astype(BF16)
            dpar_ref[0, low : low + HEAD, cols] = nt(query, gpar).astype(BF16)
            dpar_ref[0, width + low : width + low + HEAD, cols] = nt(dctx, par.astype(BF16)).astype(BF16)
            dkey_mem += nt(query, gmem)
            dvalue_mem += nt(dctx, mem.astype(BF16))
        pad = jnp.zeros((HEAD, tail - bank), F32)
        dwin_ref[0, qs, window:] = jnp.zeros((HEAD, tail), BF16)
        dwin_ref[0, ks, window:] = jnp.concatenate([dkey_mem, pad], axis=1).astype(BF16)
        dwin_ref[0, vs, window:] = jnp.concatenate([dvalue_mem, pad], axis=1).astype(BF16)


def step_block(array):
    return pl.BlockSpec((1,) + array.shape[1:], lambda step, *_: (step, 0, 0))


def whole_block(array):
    return pl.BlockSpec(array.shape, lambda step, *_: (0,) * len(array.shape))


def cost(microseconds):
    return pl.CostEstimate(flops=int(microseconds * 1.0e9), bytes_accessed=0, transcendentals=0)


def params(mib):
    return pltpu.CompilerParams(vmem_limit_bytes=mib << 20)


def across_lanes(rows, index, low, high, columns):
    chosen = (lax.broadcasted_iota(jnp.int32, (rows.shape[0], 128), 0) == index).astype(BF16)
    column = tn(rows[:, low:high] if high - low < rows.shape[1] else rows, chosen)
    return jnp.concatenate([column] * (columns // 128), axis=1)


def project_kernel(low, high, scaled, near_ref, far_ref, toks_ref, bias_ref, out_ref):
    depth = near_ref.shape[1]
    out = tn(near_ref[0, :, low:high], toks_ref[:depth]) + tn(far_ref[0, :, low:high], toks_ref[depth:])
    out = (out + across_lanes(bias_ref[0], 1, low, high, out.shape[1])).astype(BF16)
    if scaled:
        out_ref[0, :scaled] = out[:scaled] * jnp.asarray(HEAD ** (-0.5), BF16)
        out_ref[0, scaled:] = out[scaled:]
    else:
        out_ref[0] = out


def project(near, far, toks, bias, low, high, scaled):
    groups = near.shape[0]
    out = jax.ShapeDtypeStruct((groups, high - low, toks.shape[1]), BF16)
    return pl.pallas_call(
        functools.partial(project_kernel, low, high, scaled),
        grid=(groups,),
        in_specs=[step_block(near), step_block(far), whole_block(toks), step_block(bias)],
        out_specs=step_block(out),
        out_shape=out,
        compiler_params=params(40),
        cost_estimate=cost(0.1),
        name="project",
    )(near, far, toks, bias)


def chunks(columns):
    return columns // 128


def mlp_forward_kernel(
    at,
    ctx_ref,
    win_ref,
    cot_keep,
    cot_got,
    cot_last,
    out_ref,
    near_up,
    far_up,
    near_down,
    far_down,
    bias_ref,
    keep_ref,
    along_ref,
    close_ref,
    active_ref,
    slope_ref,
    grad_ref,
    low_ref,
    hidden_ref,
    normed_ref,
    scale_ref,
    sums_ref,
    total_ref,
    wide_ref,
    parts_ref,
):
    step, last = pl.program_id(0), pl.num_programs(0) - 1
    depth = near_up.shape[2]
    model, own = total_ref.shape
    feat = keep_ref.shape[1]

    def column(i):
        return win_ref[:, at + i : at + i + 1].astype(F32)

    @pl.when(step == 0)
    def start():
        total_ref[...] = nn(out_ref[...], ctx_ref[...])
        bias, gain, shift = column(0), column(1), column(2)

        def body(i, carry):
            cols = pl.ds(pl.multiple_of(i * 128, 128), 128)
            values = total_ref[:, cols] + bias + win_ref[:, cols].astype(F32)
            center, scale = norm_stats(values)
            normed = (values - center) * scale
            hidden = normed * gain + shift
            normed_ref[:, cols] = normed
            scale_ref[:, cols] = scale
            wide_ref[:, cols] = hidden
            hidden_ref[:, cols] = hidden.astype(BF16)
            return carry

        lax.fori_loop(0, chunks(own), body, 0)
        total_ref[...] = jnp.zeros(total_ref.shape, F32)

    width = near_up.shape[3]
    piece = width // 3
    for low in range(0, width, piece):
        rows = slice(low, low + piece)
        upper = tn(near_up[0, 0, :, rows], hidden_ref[:depth]) + tn(far_up[0, 0, :, rows], hidden_ref[depth:])
        upper = upper + across_lanes(bias_ref[0], 0, low, low + piece, own)
        phi = 0.5 * (1.0 + lax.erf(upper * np.float32(0.5**0.5)))
        active_ref[0, rows] = (upper * phi).astype(BF16)
        slope_ref[0, rows] = (
            phi + upper * jnp.exp(-0.5 * upper * upper) * np.float32(1.0 / np.sqrt(2.0 * np.pi))
        ).astype(BF16)
    total_ref[:depth] += nn(near_down[0, 0], active_ref[0])
    total_ref[depth:] += nn(far_down[0, 0], active_ref[0])

    @pl.when(step == last)
    def finish():
        bias, gain, shift = column(3), column(4), column(5)
        parts_ref[...] = jnp.zeros(parts_ref.shape, F32)

        def body(i, carry):
            cols = pl.ds(pl.multiple_of(i * 128, 128), 128)
            values = total_ref[:, cols] + bias + wide_ref[:, cols]
            center, scale = norm_stats(values)
            normed = (values - center) * scale
            result = (normed * gain + shift).astype(BF16)
            keep_ref[0, :, cols] = result[:feat]
            along_ref[0, :, cols] = result[feat : 2 * feat]
            close_ref[0, :, cols] = result[2 * feat : 3 * feat]
            along_ref[1, :, cols] = result[3 * feat :]
            pieces = (cot_keep, cot_got, cot_last)
            cot = jnp.concatenate([pieces[i][j, :, cols] for i, j in PIECES], axis=0).astype(F32)
            grad = norm_back(cot, normed, scale, gain)
            grad_ref[:, cols] = grad
            grad_low = grad.astype(BF16)
            low_ref[:, cols] = grad_low
            parts_ref[0] += grad_low.astype(F32)
            parts_ref[1] += cot * normed
            parts_ref[2] += cot
            return carry

        lax.fori_loop(0, chunks(own), body, 0)
        for i in range(3):
            sums_ref[:, i : i + 1] = jnp.sum(parts_ref[i], axis=1, keepdims=True)


def weight_block(array, which):
    return pl.BlockSpec((1, 1) + array.shape[2:], lambda step, *_: (which, step, 0, 0))


def mlp_forward(at, ctx, win, cot, out_t, near, far, bias):
    groups, depth, width = near.shape[1:]
    feat, own = cot[0].shape[1:]
    model = feat * 4
    outs = [
        jax.ShapeDtypeStruct((1, feat, own), BF16),
        jax.ShapeDtypeStruct((2, feat, own), BF16),
        jax.ShapeDtypeStruct((1, feat, own), BF16),
        jax.ShapeDtypeStruct((groups, width, own), BF16),
        jax.ShapeDtypeStruct((groups, width, own), BF16),
        jax.ShapeDtypeStruct((model, own), F32),
        jax.ShapeDtypeStruct((model, own), BF16),
        jax.ShapeDtypeStruct((model, own), BF16),
        jax.ShapeDtypeStruct((model, own), F32),
        jax.ShapeDtypeStruct((1, own), F32),
        jax.ShapeDtypeStruct((model, 3), F32),
    ]
    specs = [step_block(o) if i in (3, 4) else whole_block(o) for i, o in enumerate(outs)]
    return pl.pallas_call(
        functools.partial(mlp_forward_kernel, at),
        grid=(groups,),
        in_specs=[
            whole_block(ctx),
            whole_block(win),
            *[whole_block(piece) for piece in cot],
            whole_block(out_t),
            weight_block(near, 0),
            weight_block(far, 0),
            weight_block(near, 1),
            weight_block(far, 1),
            step_block(bias),
        ],
        out_specs=specs,
        out_shape=outs,
        scratch_shapes=[
            pltpu.VMEM((model, own), F32),
            pltpu.VMEM((model, own), F32),
            pltpu.VMEM((3, model, 128), F32),
        ],
        compiler_params=params(56),
        cost_estimate=cost(240),
        name="mlp_forward",
    )(ctx, win, *cot, out_t, near, far, near, far, bias)


def down_grad_kernel(low_ref, active_ref, keep_ref, send_ref):
    grads = nt(low_ref[...], active_ref[0]).astype(BF16)
    depth = keep_ref.shape[1]
    keep_ref[0] = grads[:depth]
    send_ref[0] = grads[depth:]


def down_grads(low, active):
    groups, width, own = active.shape
    out = jax.ShapeDtypeStruct((groups, low.shape[0] // 2, width), BF16)
    return pl.pallas_call(
        down_grad_kernel,
        grid=(groups,),
        in_specs=[whole_block(low), step_block(active)],
        out_specs=[step_block(out)] * 2,
        out_shape=[out] * 2,
        compiler_params=params(32),
        cost_estimate=cost(50),
        name="down_grads",
    )(low, active)


def mlp_backward_kernel(
    at,
    low_ref,
    slope_ref,
    hidden_ref,
    near_up,
    far_up,
    near_down,
    far_down,
    grad_ref,
    normed_ref,
    scale_ref,
    win_ref,
    out_ref,
    keep_ref,
    send_ref,
    first_ref,
    first_low_ref,
    dctx_ref,
    bias_ref,
    sums_ref,
    total_ref,
    parts_ref,
):
    step, last = pl.program_id(0), pl.num_programs(0) - 1
    depth = near_up.shape[2]
    model, own = low_ref.shape

    @pl.when(step == 0)
    def start():
        total_ref[...] = grad_ref[...]

    upper = tn(near_down[0, 0], low_ref[:depth]) + tn(far_down[0, 0], low_ref[depth:])
    upper = (upper * slope_ref[0].astype(F32)).astype(BF16)
    bias_ref[0] = jnp.sum(upper.astype(F32), axis=1, keepdims=True)
    total_ref[:depth] += nn(near_up[0, 0], upper)
    total_ref[depth:] += nn(far_up[0, 0], upper)
    keep_ref[0] = nt(hidden_ref[:depth], upper).astype(BF16)
    send_ref[0] = nt(hidden_ref[depth:], upper).astype(BF16)

    @pl.when(step == last)
    def finish():
        gain = win_ref[:, at + 1 : at + 2].astype(F32)
        parts_ref[...] = jnp.zeros(parts_ref.shape, F32)

        def body(i, carry):
            cols = pl.ds(pl.multiple_of(i * 128, 128), 128)
            hidden_grad = total_ref[:, cols]
            normed = normed_ref[:, cols]
            first = norm_back(hidden_grad, normed, scale_ref[:, cols], gain)
            first_ref[:, cols] = first
            first_low = first.astype(BF16)
            first_low_ref[:, cols] = first_low
            parts_ref[0] += first_low.astype(F32)
            parts_ref[1] += hidden_grad * normed
            parts_ref[2] += hidden_grad
            return carry

        lax.fori_loop(0, chunks(own), body, 0)
        for i in range(3):
            sums_ref[:, i : i + 1] = jnp.sum(parts_ref[i], axis=1, keepdims=True)
        dctx_ref[...] = tn(out_ref[...], first_low_ref[...]).astype(BF16)


def mlp_backward(at, low, slope, hidden, near, far, grad, normed, scale, win, out_t):
    groups, depth, width = near.shape[1:]
    model, own = low.shape
    outs = [
        jax.ShapeDtypeStruct((groups, depth, width), BF16),
        jax.ShapeDtypeStruct((groups, depth, width), BF16),
        jax.ShapeDtypeStruct((model, own), F32),
        jax.ShapeDtypeStruct((model, own), BF16),
        jax.ShapeDtypeStruct((out_t.shape[1], own), BF16),
        jax.ShapeDtypeStruct((groups, width, 1), F32),
        jax.ShapeDtypeStruct((model, 3), F32),
    ]
    specs = [step_block(o) if i in (0, 1, 5) else whole_block(o) for i, o in enumerate(outs)]
    return pl.pallas_call(
        functools.partial(mlp_backward_kernel, at),
        grid=(groups,),
        in_specs=[
            whole_block(low),
            step_block(slope),
            whole_block(hidden),
            weight_block(near, 0),
            weight_block(far, 0),
            weight_block(near, 1),
            weight_block(far, 1),
            whole_block(grad),
            whole_block(normed),
            whole_block(scale),
            whole_block(win),
            whole_block(out_t),
        ],
        out_specs=specs,
        out_shape=outs,
        scratch_shapes=[pltpu.VMEM((model, own), F32), pltpu.VMEM((3, model, 128), F32)],
        compiler_params=params(56),
        cost_estimate=cost(240),
        name="mlp_backward",
    )(low, slope, hidden, near, far, near, far, grad, normed, scale, win, out_t)


def first_grad_kernel(
    width, win_ref, par_ref, dwin_ref, dpar_ref, low_ref, ctx_ref, up_ref, first_ref, last_ref, keep_ref, send_ref
):
    depth = keep_ref.shape[1]
    half = depth // 4
    query = jnp.sum(dwin_ref[0, :width].astype(F32), axis=1, keepdims=True)
    value = jnp.sum(dwin_ref[0, 2 * width :].astype(F32), axis=1, keepdims=True)
    value = value + jnp.sum(dpar_ref[0, width:].astype(F32), axis=1, keepdims=True)
    by_row = [array[i : i + half] for array in (query, value, up_ref[0]) for i in range(0, array.shape[0], half)]
    by_row = jnp.concatenate(by_row, axis=1)
    by_row = jnp.concatenate([by_row] * 4, axis=0)
    used = by_row.shape[1] + 6
    pad = jnp.zeros((depth, keep_ref.shape[2] - 4 * width - used), F32)
    for part, out_ref in enumerate((keep_ref, send_ref)):
        rows = slice(part * depth, (part + 1) * depth)
        win, par = win_ref[rows], par_ref[rows]
        out_ref[0, :, :width] = nt(win, dwin_ref[0, :width]).astype(BF16)
        for i in range(1, 3):
            grads = nt(win, dwin_ref[0, i * width : (i + 1) * width])
            grads = grads + nt(par, dpar_ref[0, (i - 1) * width : i * width])
            out_ref[0, :, i * width : (i + 1) * width] = grads.astype(BF16)
        out_ref[0, :, 3 * width : 4 * width] = nt(low_ref[rows], ctx_ref[0]).astype(BF16)
        extra = jnp.concatenate([by_row, first_ref[rows], last_ref[rows], pad], axis=1)
        out_ref[0, :, 4 * width :] = extra.astype(BF16)


def first_grads(win, par, dwin, dpar, low, ctx, up_bias, first_sums, last_sums):
    groups, width, own = ctx.shape
    out = jax.ShapeDtypeStruct((groups, low.shape[0] // 2, 4 * width + 128), BF16)
    return pl.pallas_call(
        functools.partial(first_grad_kernel, width),
        grid=(groups,),
        in_specs=[
            whole_block(win),
            whole_block(par),
            step_block(dwin),
            step_block(dpar),
            whole_block(low),
            step_block(ctx),
            step_block(up_bias),
            whole_block(first_sums),
            whole_block(last_sums),
        ],
        out_specs=[step_block(out)] * 2,
        out_shape=[out] * 2,
        compiler_params=params(40),
        cost_estimate=cost(120),
        name="first_grads",
    )(win, par, dwin, dpar, low, ctx, up_bias, first_sums, last_sums)


def token_grad_kernel(low, high, parent, near_ref, far_ref, dwin_ref, more_ref, keep_ref, along_ref, close_ref, total_ref):
    step, last = pl.program_id(0), pl.num_programs(0) - 1
    depth = near_ref.shape[1]
    columns = total_ref.shape[1]
    own = more_ref.shape[1]

    @pl.when(step == 0)
    def start():
        total_ref[...] = jnp.zeros(total_ref.shape, F32)
        if not parent:
            total_ref[:, :own] = more_ref[...]

    if parent:
        grads = jnp.concatenate([more_ref[0], dwin_ref[0, low:high, more_ref.shape[2] :]], axis=1)
    else:
        grads = dwin_ref[0, low:high, :columns]
    total_ref[:depth] += nn(near_ref[0, :, low:high], grads)
    total_ref[depth:] += nn(far_ref[0, :, low:high], grads)

    @pl.when(step == last)
    def finish():
        feat = keep_ref.shape[1]
        for i, out in enumerate((keep_ref.at[0], along_ref.at[0], close_ref.at[0], along_ref.at[1])):
            out[...] = total_ref[i * feat : (i + 1) * feat].astype(BF16)


def token_grads(near, far, dwin, more, low, high, parent, columns):
    groups, depth = near.shape[:2]
    feat = depth // 2
    outs = [jax.ShapeDtypeStruct((n, feat, columns), BF16) for n in (1, 2, 1)]
    return pl.pallas_call(
        functools.partial(token_grad_kernel, low, high, parent),
        grid=(groups,),
        in_specs=[
            step_block(near),
            step_block(far),
            step_block(dwin),
            step_block(more) if parent else whole_block(more),
        ],
        out_specs=[whole_block(out) for out in outs],
        out_shape=outs,
        scratch_shapes=[pltpu.VMEM((2 * depth, columns), F32)],
        compiler_params=params(40),
        cost_estimate=cost(50),
        name="token_grads",
    )(near, far, dwin, more)


def attend(lengths, segments, bank, scalars, window, parent):
    groups, rows, columns = window.shape
    width = rows // 3
    heads = width // HEAD
    outs = (
        jax.ShapeDtypeStruct((groups, width, sum(lengths)), BF16),
        jax.ShapeDtypeStruct((groups, heads, sum(lengths)), F32),
    )
    return pl.pallas_call(
        functools.partial(attention_forward, heads, lengths, segments, bank),
        grid=(groups,),
        in_specs=[SMEM] * 3 + [step_block(window), step_block(parent)],
        out_specs=[step_block(out) for out in outs],
        out_shape=outs,
        compiler_params=params(40),
        cost_estimate=cost(130),
        name="attention_forward",
    )(*scalars, window, parent)


def attend_back(lengths, segments, bank, scalars, window, parent, dctx, lse):
    groups, rows, columns = window.shape
    outs = (jax.ShapeDtypeStruct(window.shape, BF16), jax.ShapeDtypeStruct(parent.shape, BF16))
    return pl.pallas_call(
        functools.partial(attention_backward, rows // 3 // HEAD, lengths, segments, bank),
        grid=(groups,),
        in_specs=[SMEM] * 3 + [step_block(window), step_block(parent), step_block(dctx), step_block(lse)],
        out_specs=[step_block(out) for out in outs],
        out_shape=outs,
        compiler_params=params(40),
        cost_estimate=cost(200),
        name="attention_backward",
    )(*scalars, window, parent, dctx, lse)


def swap(array, axis, mask):
    count = lax.axis_size(axis)
    return lax.ppermute(array, axis, [(i, i ^ mask) for i in range(count)])


SMEM = pl.BlockSpec(memory_space=pltpu.SMEM)
VMEM = pl.BlockSpec(memory_space=pltpu.VMEM)
ORDER = (0, 2, 1, 3)
SENDS = ((0, 0), (1, 0), (2, 0), (1, 1))


def at_distance(here_ref, lists, slot, j):
    distance = ORDER[slot]
    return static_of(here_ref[1], [lists[i ^ distance][j] for i in range(len(lists))])


def flipped(here_ref, part, half):
    return pl.multiple_of((part ^ here_ref[2]) * half, 32)


def spots(rows, columns, shift):
    return (
        lax.broadcasted_iota(jnp.int32, (rows, columns), 0) + shift
        == lax.broadcasted_iota(jnp.int32, (rows, columns), 1)
    ).astype(BF16)


def pack_weights_kernel(
    here_ref,
    query_ref,
    key_ref,
    value_ref,
    out_ref,
    up_ref,
    down_ref,
    up_b_ref,
    query_b_ref,
    value_b_ref,
    half_ref,
    turned_ref,
):
    feat, width = query_ref.shape
    half = feat // 2
    rows = pl.ds(flipped(here_ref, 0, half), half)
    turned_ref[...] = tn(out_ref[...], spots(width, width, 0)).astype(BF16)
    for i, ref in enumerate((query_ref, key_ref, value_ref, turned_ref)):
        half_ref[:half, i * width : (i + 1) * width] = ref[rows, :]
    half_ref[half : 2 * half] = up_ref[rows, :]
    half_ref[2 * half : 3 * half] = down_ref[rows, :]
    zero = jnp.zeros((1, width), F32)
    joint = [query_b_ref[...].astype(F32), zero, value_b_ref[...].astype(F32), zero]
    wide = (half_ref.shape[0] - 3 * half, half_ref.shape[1])
    index = lax.broadcasted_iota(jnp.int32, wide, 0)
    up_row = jnp.broadcast_to(up_b_ref[...].astype(F32), wide)
    joint_row = jnp.broadcast_to(jnp.concatenate(joint, axis=1), wide)
    half_ref[3 * half :] = jnp.where(index == 0, up_row, jnp.where(index == 1, joint_row, 0.0)).astype(BF16)


def pack_weights(here, query, key, value, out, up, down, *biases):
    feat, width = query.shape
    hidden = up.shape[1]
    return pl.pallas_call(
        pack_weights_kernel,
        in_specs=[SMEM] + [VMEM] * 9,
        out_specs=VMEM,
        out_shape=jax.ShapeDtypeStruct((3 * feat // 2 + 16, hidden), BF16),
        scratch_shapes=[pltpu.VMEM((feat, width), BF16)],
        compiler_params=params(24),
        cost_estimate=cost(0.1),
        name="pack_weights",
    )(here, query, key, value, out, up, down, *[bias.reshape(1, -1) for bias in biases])


def pack_kernel(blocks, sided, here_ref, source_ref, *refs):
    half = source_ref.shape[0] // 2
    count = len(blocks[0])
    outs = refs[2:5] if sided else refs
    if sided:
        mem_ref, vec_ref, side_ref = refs[0], refs[1], refs[5]
        bank = mem_ref.shape[0]
        side = tn(mem_ref[...], spots(bank, 128, 0)) + tn(vec_ref[...], spots(vec_ref.shape[0], 128, bank))
        side_ref[...] = side.astype(BF16)
    for slot, (out, place) in enumerate(SENDS):
        for part in range(2):
            low = flipped(here_ref, part, half)
            rows = slice(part * half, (part + 1) * half)
            for j in range(count):
                at = pl.multiple_of(at_distance(here_ref, blocks, slot, j) * 128, 128)
                outs[out][place, rows, j * 128 : (j + 1) * 128] = source_ref[pl.ds(low, half), pl.ds(at, 128)]
            if sided:
                outs[out][place, rows, count * 128 :] = side_ref[pl.ds(low, half), :]


def pack(blocks, here, source, *side):
    feat = source.shape[0]
    columns = len(blocks[0]) * 128 + (128 if side else 0)
    return pl.pallas_call(
        functools.partial(pack_kernel, blocks, bool(side)),
        in_specs=[SMEM] + [VMEM] * (1 + len(side)),
        out_specs=[VMEM] * 3,
        out_shape=[jax.ShapeDtypeStruct((n, feat, columns), source.dtype) for n in (1, 2, 1)],
        scratch_shapes=[pltpu.VMEM((feat, 128), BF16)] if side else [],
        compiler_params=params(24),
        cost_estimate=cost(0.1),
        name="pack",
    )(here, source, *side)


def exchange(keep, along, near):
    got = swap(along, "col", 2)
    return keep, got, swap(jnp.concatenate([near, got[1:]], axis=0), "col", 1)


def joined(pieces):
    keep, got, last = pieces
    return jnp.concatenate([keep, got[:1], last], axis=0)


PIECES = ((0, 0), (1, 0), (2, 0), (2, 1))


def parent_of(here_ref, parents_ref, segments, slot, j):
    return parents_ref[here_ref[0] * here_ref[3] + at_distance(here_ref, segments, slot, j)]


def pick_kernel(segments, here_ref, parents_ref, source_ref, *outs):
    half = source_ref.shape[1] // 2
    seg_row = here_ref[3]
    for slot, (out, place) in enumerate(SENDS):
        for j in range(len(segments[0])):
            seg = jnp.maximum(parent_of(here_ref, parents_ref, segments, slot, j), 0)
            row = lax.div(seg, seg_row)
            at = pl.multiple_of((seg - row * seg_row) * SEG, SEG)
            for part in range(2):
                rows = slice(part * half, (part + 1) * half)
                outs[out][place, rows, j * SEG : (j + 1) * SEG] = source_ref[
                    row, pl.ds(flipped(here_ref, part, half), half), pl.ds(at, SEG)
                ]


def pick_parents(segments, here, parents, gathered):
    feat = gathered.shape[1]
    columns = len(segments[0]) * SEG
    return pl.pallas_call(
        functools.partial(pick_kernel, segments),
        in_specs=[SMEM, SMEM, VMEM],
        out_specs=[VMEM] * 3,
        out_shape=[jax.ShapeDtypeStruct((n, feat, columns), gathered.dtype) for n in (1, 2, 1)],
        compiler_params=params(24),
        cost_estimate=cost(1),
        name="pick_parents",
    )(here, parents, gathered)


def add_parents_kernel(segments, seg_row, here_ref, parents_ref, *refs):
    pieces, out_ref, sum_ref = refs[:3], refs[3], refs[4]
    window = len(segments[0]) * SEG
    sum_ref[...] = jnp.zeros(sum_ref.shape, F32)
    for slot, (piece, place) in enumerate(PIECES):
        for j in range(len(segments[0])):
            seg = parent_of(here_ref, parents_ref, segments, slot, j)

            @pl.when(seg >= 0)
            def add(seg=seg, piece=piece, place=place, cols=slice(j * SEG, (j + 1) * SEG)):
                sum_ref[seg] += pieces[piece][place, :, cols].astype(F32)

    mem = sum(pieces[piece][place, :, window:].astype(F32) for piece, place in PIECES)
    for r in range(out_ref.shape[0]):
        for s in range(seg_row):
            out_ref[r, :, s * SEG : (s + 1) * SEG] = sum_ref[r * seg_row + s].astype(BF16)
        out_ref[r, :, seg_row * SEG :] = mem.astype(BF16)


def add_parents(segments, here, parents, pieces, rows, seg_row):
    feat, columns = pieces[0].shape[1:]
    bank = columns - len(segments[0]) * SEG
    return pl.pallas_call(
        functools.partial(add_parents_kernel, segments, seg_row),
        in_specs=[SMEM, SMEM, VMEM, VMEM, VMEM],
        out_specs=VMEM,
        out_shape=jax.ShapeDtypeStruct((rows, feat, seg_row * SEG + bank), BF16),
        scratch_shapes=[pltpu.VMEM((rows * seg_row, feat, SEG), F32)],
        compiler_params=params(40),
        cost_estimate=cost(20),
        name="add_parents",
    )(here, parents, *pieces)


def finish_kernel(blocks, here_ref, placed_ref, *refs):
    pieces, out_ref = refs[:3], refs[3]
    half = out_ref.shape[0] // 2
    for part in range(2):
        low = flipped(here_ref, part, half)
        rows = slice(part * half, (part + 1) * half)
        out_ref[pl.ds(low, half), :] = placed_ref[rows, : out_ref.shape[1]].astype(F32)
        for slot, (piece, place) in enumerate(PIECES):
            for j in range(len(blocks[0])):
                at = pl.multiple_of(at_distance(here_ref, blocks, slot, j) * 128, 128)
                out_ref[pl.ds(low, half), pl.ds(at, 128)] += pieces[piece][
                    place, rows, j * 128 : (j + 1) * 128
                ].astype(F32)


def finish_tokens(blocks, here, placed, pieces, columns):
    return pl.pallas_call(
        functools.partial(finish_kernel, blocks),
        in_specs=[SMEM, VMEM, VMEM, VMEM, VMEM],
        out_specs=VMEM,
        out_shape=jax.ShapeDtypeStruct((placed.shape[0], columns), F32),
        compiler_params=params(24),
        cost_estimate=cost(2.5),
        name="finish_tokens",
    )(here, placed, *pieces)


def place_kernel(blocks, here_ref, *refs):
    pieces, out_ref = refs[:3], refs[3]
    half = out_ref.shape[0] // 2
    for part in range(2):
        low = flipped(here_ref, part, half)
        rows = slice(part * half, (part + 1) * half)
        for slot, (piece, place) in enumerate(PIECES):
            for j in range(pieces[0].shape[2] // 128):
                at = pl.multiple_of(at_distance(here_ref, blocks, slot, j) * 128, 128)
                out_ref[pl.ds(low, half), pl.ds(at, 128)] = pieces[piece][place, rows, j * 128 : (j + 1) * 128]


def place(blocks, here, pieces, columns):
    return pl.pallas_call(
        functools.partial(place_kernel, blocks),
        in_specs=[SMEM, VMEM, VMEM, VMEM],
        out_specs=VMEM,
        out_shape=jax.ShapeDtypeStruct((pieces[0].shape[1], columns), pieces[0].dtype),
        compiler_params=params(24),
        cost_estimate=cost(1.7),
        name="place",
    )(here, *pieces)


def gather_weights(half):
    return [half] + [swap(half, "row", n) for n in range(1, lax.axis_size("row"))]


def spread_weights(along):
    along = jnp.stack(along, axis=1)
    opposite = swap(along, "leaf", 1)
    across = swap(along, "col", 2)
    return along, opposite, across, swap(across, "leaf", 1)


def whole_weights(parts):
    near = jnp.stack(parts, axis=2)
    arrays, rows, blocks, depth, columns = near.shape
    near = near.reshape(arrays, rows, blocks * depth, columns)
    return near, swap(near, "col", 1)


def add_up(*terms):
    total = terms[0].astype(F32)
    for term in terms[1:]:
        total = total + term.astype(F32)
    return total


def reduce_blocks(keep):
    rows, features, columns = keep.shape
    return rows, 2, 2, features // 4, columns


def reduce_across(keep, near):
    shape = reduce_blocks(keep)
    return add_up(keep.reshape(shape)[:, :, 1], near.reshape(shape)[:, :, 1]).astype(BF16)


def reduce_up(keep, near, across):
    shape = reduce_blocks(keep)
    return add_up(keep.reshape(shape)[:, 1, 0], near.reshape(shape)[:, 1, 0], across[:, 1]).astype(BF16)


def reduce_along(keep, near, across, up):
    shape = reduce_blocks(keep)
    mine = add_up(keep.reshape(shape)[:, 0, 0], near.reshape(shape)[:, 0, 0], across[:, 0], up)
    return [mine[n].astype(BF16) for n in range(shape[0])]


def reduce_rows(along, got):
    total = add_up(along[0], *got)
    mask = 2
    while mask < lax.axis_size("leaf"):
        total = add_up(total, swap(total.astype(BF16), "leaf", mask))
        mask *= 2
    return total.astype(BF16)


def reduce_corner(keep, near):
    shape = reduce_blocks(keep)
    middle = shape[0] // 2
    corner = add_up(keep.reshape(shape)[:, 1, 1], near.reshape(shape)[:, 1, 1]).astype(BF16)
    return corner[:middle], corner[middle:]


def reduce_edges(keep, near, by_leaf, by_col):
    shape = reduce_blocks(keep)
    middle = shape[0] // 2
    keep, near = keep.reshape(shape), near.reshape(shape)
    leaf = add_up(keep[:, 0, 1], near[:, 0, 1])
    leaf = jnp.concatenate([leaf[:middle], add_up(leaf[middle:], by_col)], axis=0).astype(BF16)
    along = add_up(keep[:, 1, 0], near[:, 1, 0])
    along = jnp.concatenate([add_up(along[:middle], by_leaf), along[middle:]], axis=0).astype(BF16)
    return leaf, along


def reduce_mine(keep, near, leaf, along):
    shape = reduce_blocks(keep)
    mine = add_up(keep.reshape(shape)[:, 0, 0], near.reshape(shape)[:, 0, 0], leaf, along)
    return [mine[n].astype(BF16) for n in range(shape[0])]


def send_rows(along):
    return [swap(block, "row", n) for n, block in enumerate(along) if n]


def norm_stats(values):
    center = jnp.mean(values, axis=0, keepdims=True)
    spread = jnp.mean(values * values, axis=0, keepdims=True) - center * center
    return center, lax.rsqrt(spread + EPSILON)


def norm_back(grad, normed, scale, gain):
    scaled = grad * gain
    return scale * (
        scaled
        - jnp.mean(scaled, axis=0, keepdims=True)
        - normed * jnp.mean(scaled * normed, axis=0, keepdims=True)
    )


def lane_sum(array):
    return jnp.sum(array, axis=-1, dtype=F32)


def on_device(
    tokens,
    memory,
    parents,
    memory_slots,
    query_weight,
    query_bias,
    key_weight,
    value_weight,
    value_bias,
    out_weight,
    out_bias,
    norm_gain,
    norm_shift,
    up_weight,
    up_bias,
    down_weight,
    down_bias,
    final_gain,
    final_shift,
    cotangent,
):
    rows, cols = lax.axis_size("row"), lax.axis_size("col")
    row, col = lax.axis_index("row"), lax.axis_index("col")
    feat, row_tokens = tokens.shape
    own = row_tokens // cols
    seg_row = row_tokens // SEG
    model = feat * cols
    width = query_weight.shape[1]
    hidden_width = up_weight.shape[1]
    bank = memory.shape[0]
    segments, ranges = plan_windows(own, cols)
    window = len(segments[0]) * SEG
    tail = 128
    lengths = tuple(min(SEG, own - j * SEG) for j in range(len(segments[0])))
    half = feat // 2
    parity = lax.axis_index("leaf") % 2
    here = jnp.stack([row, col, parity, jnp.int32(seg_row)]).astype(jnp.int32)
    blocks = [[b for a, n in ranges[i] for b in range(a // 128, (a + n) // 128)] for i in range(cols)]
    own_blocks = [each[: own // 128] for each in blocks]
    scalars = (here, parents, memory_slots)

    weight_half = pack_weights(
        here, query_weight, key_weight, value_weight, out_weight, up_weight, down_weight, up_bias, query_bias, value_bias
    )
    along = gather_weights(weight_half)

    zero = jnp.zeros((feat,), BF16)
    vectors = jnp.stack([out_bias, norm_gain, norm_shift, down_bias, final_gain, final_shift, zero, zero])
    token_sends = pack(blocks, here, after(tokens, weight_half), memory, vectors)
    cot_sends = pack(own_blocks, here, after(cotangent, token_sends))
    token_got = swap(token_sends[1], "col", 2)
    along = after(along, cot_sends, token_got)
    everything = lax.all_gather(after(tokens, along), "row", axis=0)
    row_vectors = jnp.stack([piece[3 * half :] for piece in along])
    near_first, far_first = (array[0] for array in whole_weights(spread_weights([piece[:half][None] for piece in along])))
    token_last = swap(jnp.concatenate([token_sends[2], token_got[1:]], axis=0), "col", 1)
    tok_window = joined((token_sends[0], token_got, token_last)).reshape(model, window + tail)
    second_parts = spread_weights([piece[half : 3 * half].reshape(2, half, -1) for piece in along])
    win = project(near_first, far_first, tok_window, row_vectors, 0, 3 * width, width)
    out_t = jnp.concatenate([near_first[:, :, 3 * width :], far_first[:, :, 3 * width :]], axis=1)
    out_t = out_t.transpose(1, 0, 2).reshape(model, rows * width)
    everything = after(everything, win, out_t, second_parts[2])
    par_keep, par_along, par_near = pick_parents(segments, here, parents, everything)
    par_got = swap(par_along, "col", 2)
    near, far = whole_weights(after(second_parts, par_along))
    par_got = after(par_got, near)
    par_near = jnp.concatenate([par_near, par_got[1:]], axis=0)
    tok_parent = joined((par_keep, par_got, swap(par_near, "col", 1))).reshape(model, window)
    par = project(near_first, far_first, tok_parent, row_vectors, width, 3 * width, 0)
    cot_keep, cot_along, cot_near = after(cot_sends, par_near)
    cot_got = swap(cot_along, "col", 2)
    ctx, lse = attend(lengths, segments, bank, scalars, win, par)
    cot_got = after(cot_got, ctx)
    cot_pieces = cot_keep, cot_got, swap(jnp.concatenate([cot_near, cot_got[1:]], axis=0), "col", 1)
    at = window + bank
    *result, active, slope, second_grad, down_low, hidden_low, normed, scale, last_sums = mlp_forward(
        at, ctx.reshape(rows * width, own), tok_window, cot_pieces, out_t, near, far, row_vectors
    )
    down_keep, down_send = down_grads(down_low, active)
    up_keep, up_send, first_grad, first_low, dctx, up_bias_grad, first_sums = mlp_backward(
        at, after(down_low, down_send), slope, hidden_low, near, far, second_grad, normed, scale, tok_window, out_t
    )
    down_near, up_near = swap(down_send, "col", 1), swap(up_send, "col", 1)
    down_across = reduce_across(after(down_keep, dctx), down_near)
    up_across = reduce_across(after(up_keep, down_across), up_near)
    dctx = after(dctx, down_across, up_across).reshape(rows, width, own)
    dwin, dpar = attend_back(lengths, segments, bank, scalars, win, par, dctx, lse)

    dtok_par = token_grads(near_first, far_first, dwin, dpar, width, 3 * width, True, window + tail)
    par_keep, par_along, par_near = dtok_par
    par_got = swap(par_along, "col", 2)
    first_low = after(first_low, par_along)
    first_keep, first_send = first_grads(
        tok_window, tok_parent, dwin, dpar, first_low, ctx, up_bias_grad, first_sums, last_sums
    )
    par_got = after(par_got, first_send)
    par_near = jnp.concatenate([par_near, par_got[1:]], axis=0)
    first_near = swap(first_send, "col", 1)
    down_across = swap(down_across, "leaf", 1)
    down_up = reduce_up(after(down_keep, par_near), down_near, down_across)
    par_last = after(swap(par_near, "col", 1), down_up)
    placed = add_parents(segments, here, parents, (par_keep, par_got, par_last), rows, seg_row)
    corner = reduce_corner(after(first_keep, placed), first_near)
    by_leaf, by_col = swap(corner[0], "leaf", 1), swap(corner[1], "col", 2)
    dtok = token_grads(near_first, far_first, dwin, after(first_grad, corner), 0, 3 * width, False, window)
    placed = lax.psum_scatter(placed, "row", scatter_dimension=0, tiled=False)
    edges = reduce_edges(after(first_keep, dtok), first_near, by_leaf, by_col)
    by_leaf, by_col = swap(edges[0], "leaf", 1), swap(edges[1], "col", 2)
    up_across = swap(up_across, "leaf", 1)
    up_up = reduce_up(after(up_keep, edges), up_near, up_across)
    down_up = swap(down_up, "col", 2)
    down_rows = reduce_along(after(down_keep, up_up), down_near, down_across, down_up)
    up_up = swap(up_up, "col", 2)
    up_rows = reduce_along(after(up_keep, down_rows), up_near, up_across, up_up)
    first_rows = reduce_mine(after(first_keep, up_rows), first_near, by_leaf, by_col)
    result_pieces = exchange(*after(result, first_rows))
    down_got, up_got, first_got = send_rows(down_rows), send_rows(up_rows), send_rows(first_rows)
    second_mine = jnp.concatenate([reduce_rows(down_rows, down_got), reduce_rows(up_rows, up_got)], axis=1)
    second_other = swap(second_mine, "leaf", 1)
    first_mine = reduce_rows(after(first_rows, second_mine), first_got)
    first_other = swap(first_mine, "leaf", 1)
    layer_output = place(own_blocks, here, result_pieces, row_tokens)

    def in_order(mine, other):
        return jnp.where(
            parity == 0, jnp.concatenate([mine, other], axis=0), jnp.concatenate([other, mine], axis=0)
        ).astype(F32)

    second_total, first_total = in_order(second_mine, second_other), in_order(first_mine, first_other)
    down_total, up_total = second_total[:, :hidden_width], second_total[:, hidden_width:]
    count = (2 * width + hidden_width) // half
    by_row = first_mine[:, 4 * width : 4 * width + count].astype(F32).T.reshape(-1)
    by_col = first_total[:, 4 * width + count : 4 * width + count + 6].T

    mem_sum = placed[:, row_tokens : row_tokens + bank].astype(F32)
    memory_grad = jnp.where(parity == 0, mem_sum, jnp.roll(mem_sum, half, axis=0)).T
    tokens_grad = finish_tokens(blocks, here, placed, exchange(*dtok), row_tokens)

    return (
        layer_output,
        tokens_grad,
        memory_grad,
        first_total[:, :width],
        by_row[:width],
        first_total[:, width : 2 * width],
        first_total[:, 2 * width : 3 * width],
        by_row[width : 2 * width],
        first_total[:, 3 * width : 4 * width].T,
        by_col[0],
        by_col[1],
        by_col[2],
        up_total,
        by_row[2 * width :],
        down_total,
        by_col[3],
        by_col[4],
        by_col[5],
    )


def solution(mesh):
    return jax.shard_map(
        on_device,
        mesh=mesh,
        in_specs=(
            P("col", ("leaf", "row")),
            P("leaf", "col"),
            P("leaf"),
            P("leaf", None),
            P("col", "row"),
            P("row"),
            P("col", "row"),
            P("col", "row"),
            P("row"),
            P("row", "col"),
            P("col"),
            P("col"),
            P("col"),
            P("col", "row"),
            P("row"),
            P("col", "row"),
            P("col"),
            P("col"),
            P("col"),
            P("col", ("leaf", "row")),
        ),
        out_specs=(
            P("col", ("leaf", "row")),
            P("col", ("leaf", "row")),
            P("leaf", "col"),
            P("col", "row"),
            P("row"),
            P("col", "row"),
            P("col", "row"),
            P("row"),
            P("row", "col"),
            P("col"),
            P("col"),
            P("col"),
            P("col", "row"),
            P("row"),
            P("col", "row"),
            P("col"),
            P("col"),
            P("col"),
        ),
        check_vma=False,
    )
```

```python
import functools

import jax
import jax.numpy as jnp
import numpy as np
from jax import lax
from jax.experimental import pallas as pl
from jax.experimental.pallas import tpu as pltpu
from jax.sharding import PartitionSpec as P

HEAD = 64
SEG = 256
NEGATIVE = -1e30
EPSILON = 1e-05
EVERY = ("leaf", "row", "col")
BF16 = jnp.bfloat16
F32 = jnp.float32


def after(value, *others):
    return lax.optimization_barrier((value, others))[0]


def tn(left, right):
    return lax.dot_general(left, right, (((0,), (0,)), ((), ())), preferred_element_type=F32)


def nt(left, right):
    return lax.dot_general(left, right, (((1,), (1,)), ((), ())), preferred_element_type=F32)


def nn(left, right):
    return lax.dot_general(left, right, (((1,), (0,)), ((), ())), preferred_element_type=F32)


def plan_windows(own, count):
    segments, ranges = [], []
    for index in range(count):
        first, last = index * own, (index + 1) * own
        whole = [s for s in range(first // SEG, -(-last // SEG)) if s * SEG >= first and (s + 1) * SEG <= last]
        cut = [s for s in range(first // SEG, -(-last // SEG)) if s not in whole]
        pieces = [(s * SEG, SEG) for s in whole]
        for s in cut:
            low, high = max(first, s * SEG), min(last, (s + 1) * SEG)
            pieces.append((low, high - low))
            if low > s * SEG:
                pieces.append((s * SEG, low - s * SEG))
            if high < (s + 1) * SEG:
                pieces.append((high, (s + 1) * SEG - high))
        segments.append(whole + cut)
        ranges.append(pieces)
    return segments, ranges


def static_of(index, values):
    out = jnp.int32(values[0])
    for i, value in enumerate(values[1:], 1):
        out = jnp.where(index == i, jnp.int32(value), out)
    return out


def own_segments(segments, here_ref):
    return [
        here_ref[0] * here_ref[3] + static_of(here_ref[1], [lists[j] for lists in segments])
        for j in range(len(segments[0]))
    ]


def window_biases(segments, bank, here_ref, parents_ref, slots_ref):
    rows = lax.broadcasted_iota(jnp.int32, (bank, 1), 0)
    out = []
    for seg in own_segments(segments, here_ref):
        count = jnp.zeros((bank, 1), F32)
        for m in range(slots_ref.shape[1]):
            count = count + jnp.where(rows == slots_ref[seg, m], 1.0, 0.0)
        slot = jnp.where(count > 0, jnp.log(jnp.maximum(count, 1.0)), NEGATIVE)
        out.append((jnp.where(parents_ref[seg] >= 0, 0.0, NEGATIVE).astype(F32), slot))
    return out


def attention_forward(
    head_count, lengths, segments, bank, here_ref, parents_ref, slots_ref, win_ref, par_ref, ctx_ref, lse_ref
):
    width = head_count * HEAD
    biases = window_biases(segments, bank, here_ref, parents_ref, slots_ref)
    window = len(lengths) * SEG
    for head in range(head_count):
        low = head * HEAD
        key_mem = win_ref[0, width + low : width + low + HEAD, window : window + bank]
        value_mem = win_ref[0, 2 * width + low : 2 * width + low + HEAD, window : window + bank]
        for j, count in enumerate(lengths):
            cols = slice(j * SEG, (j + 1) * SEG)
            query = win_ref[0, low : low + HEAD, j * SEG : j * SEG + count]
            own = tn(win_ref[0, width + low : width + low + HEAD, cols], query)
            par = tn(par_ref[0, low : low + HEAD, cols], query) + biases[j][0]
            mem = tn(key_mem, query) + biases[j][1]
            top = jnp.maximum(
                jnp.maximum(jnp.max(own, axis=0, keepdims=True), jnp.max(par, axis=0, keepdims=True)),
                jnp.max(mem, axis=0, keepdims=True),
            )
            own, par, mem = jnp.exp(own - top), jnp.exp(par - top), jnp.exp(mem - top)
            total = (
                jnp.sum(own, axis=0, keepdims=True)
                + jnp.sum(par, axis=0, keepdims=True)
                + jnp.sum(mem, axis=0, keepdims=True)
            )
            mixed = (
                nn(win_ref[0, 2 * width + low : 2 * width + low + HEAD, cols], own.astype(BF16))
                + nn(par_ref[0, width + low : width + low + HEAD, cols], par.astype(BF16))
                + nn(value_mem, mem.astype(BF16))
            )
            ctx_ref[0, low : low + HEAD, j * SEG : j * SEG + count] = (mixed / total).astype(BF16)
            lse_ref[0, head : head + 1, j * SEG : j * SEG + count] = top + jnp.log(total)


def attention_backward(
    head_count,
    lengths,
    segments,
    bank,
    here_ref,
    parents_ref,
    slots_ref,
    win_ref,
    par_ref,
    dctx_ref,
    lse_ref,
    dwin_ref,
    dpar_ref,
):
    width = head_count * HEAD
    biases = window_biases(segments, bank, here_ref, parents_ref, slots_ref)
    window = len(lengths) * SEG
    tail = win_ref.shape[2] - window
    for head in range(head_count):
        low = head * HEAD
        qs, ks, vs = (slice(part * width + low, part * width + low + HEAD) for part in range(3))
        key_mem = win_ref[0, ks, window : window + bank]
        value_mem = win_ref[0, vs, window : window + bank]
        dkey_mem = jnp.zeros((HEAD, bank), F32)
        dvalue_mem = jnp.zeros((HEAD, bank), F32)
        for j, count in enumerate(lengths):
            cols = slice(j * SEG, (j + 1) * SEG)
            tok = slice(j * SEG, j * SEG + count)
            query = win_ref[0, qs, tok]
            dctx = dctx_ref[0, low : low + HEAD, tok]
            lse = lse_ref[0, head : head + 1, tok]
            key_own, value_own = win_ref[0, ks, cols], win_ref[0, vs, cols]
            key_par, value_par = par_ref[0, low : low + HEAD, cols], par_ref[0, width + low : width + low + HEAD, cols]
            own = jnp.exp(tn(key_own, query) - lse)
            par = jnp.exp(tn(key_par, query) + biases[j][0] - lse)
            mem = jnp.exp(tn(key_mem, query) + biases[j][1] - lse)
            gown, gpar, gmem = tn(value_own, dctx), tn(value_par, dctx), tn(value_mem, dctx)
            inner = (
                jnp.sum(own * gown, axis=0, keepdims=True)
                + jnp.sum(par * gpar, axis=0, keepdims=True)
                + jnp.sum(mem * gmem, axis=0, keepdims=True)
            )
            gown = (own * (gown - inner)).astype(BF16)
            gpar = (par * (gpar - inner)).astype(BF16)
            gmem = (mem * (gmem - inner)).astype(BF16)
            dquery = nn(key_own, gown) + nn(key_par, gpar) + nn(key_mem, gmem)
            dwin_ref[0, qs, tok] = (dquery * HEAD ** (-0.5)).astype(BF16)
            if count < SEG:
                dwin_ref[0, qs, j * SEG + count : (j + 1) * SEG] = jnp.zeros((HEAD, SEG - count), BF16)
            dwin_ref[0, ks, cols] = nt(query, gown).astype(BF16)
            dwin_ref[0, vs, cols] = nt(dctx, own.astype(BF16)).astype(BF16)
            dpar_ref[0, low : low + HEAD, cols] = nt(query, gpar).astype(BF16)
            dpar_ref[0, width + low : width + low + HEAD, cols] = nt(dctx, par.astype(BF16)).astype(BF16)
            dkey_mem += nt(query, gmem)
            dvalue_mem += nt(dctx, mem.astype(BF16))
        pad = jnp.zeros((HEAD, tail - bank), F32)
        dwin_ref[0, qs, window:] = jnp.zeros((HEAD, tail), BF16)
        dwin_ref[0, ks, window:] = jnp.concatenate([dkey_mem, pad], axis=1).astype(BF16)
        dwin_ref[0, vs, window:] = jnp.concatenate([dvalue_mem, pad], axis=1).astype(BF16)


def step_block(array):
    return pl.BlockSpec((1,) + array.shape[1:], lambda step, *_: (step, 0, 0))


def whole_block(array):
    return pl.BlockSpec(array.shape, lambda step, *_: (0,) * len(array.shape))


def cost(microseconds):
    return pl.CostEstimate(flops=int(microseconds * 1.0e9), bytes_accessed=0, transcendentals=0)


def held(*arrays):
    return tuple(pltpu.with_memory_space_constraint(array, pltpu.HBM) for array in arrays)


def params(mib):
    return pltpu.CompilerParams(vmem_limit_bytes=mib << 20)


def across_lanes(rows, index, low, high, columns):
    chosen = (lax.broadcasted_iota(jnp.int32, (rows.shape[0], 128), 0) == index).astype(BF16)
    column = tn(rows[:, low:high] if high - low < rows.shape[1] else rows, chosen)
    return jnp.concatenate([column] * (columns // 128), axis=1)


def join_pieces(refs, toks_ref):
    @pl.when(pl.program_id(0) == 0)
    def join():
        feat = refs[0].shape[1]
        for i, (piece, place) in enumerate(PIECES):
            toks_ref[i * feat : (i + 1) * feat] = refs[piece][place]


def project_kernel(low, high, scaled, near_ref, far_ref, *refs):
    depth = near_ref.shape[1]
    if len(refs) > 3:
        toks_ref, bias_ref, out_ref = refs[5], refs[3], refs[4]
        join_pieces(refs[:3], toks_ref)
    else:
        toks_ref, bias_ref, out_ref = refs
    out = tn(near_ref[0, :, low:high], toks_ref[:depth]) + tn(far_ref[0, :, low:high], toks_ref[depth:])
    out = (out + across_lanes(bias_ref[0], 1, low, high, out.shape[1])).astype(BF16)
    if scaled:
        out_ref[0, :scaled] = out[:scaled] * jnp.asarray(HEAD ** (-0.5), BF16)
        out_ref[0, scaled:] = out[scaled:]
    else:
        out_ref[0] = out


def project(near, far, toks, bias, low, high, scaled):
    groups, depth = near.shape[:2]
    pieces = toks if isinstance(toks, tuple) else (toks,)
    out = jax.ShapeDtypeStruct((groups, high - low, pieces[0].shape[-1]), BF16)
    return pl.pallas_call(
        functools.partial(project_kernel, low, high, scaled),
        grid=(groups,),
        in_specs=[step_block(near), step_block(far), *[whole_block(piece) for piece in pieces], step_block(bias)],
        scratch_shapes=[pltpu.VMEM((2 * depth, pieces[0].shape[-1]), BF16)] if len(pieces) > 1 else [],
        out_specs=step_block(out),
        out_shape=out,
        compiler_params=params(40),
        cost_estimate=cost(0.1),
        name="project",
    )(near, far, *pieces, bias)


def chunks(columns):
    return columns // 128


def mlp_kernel(
    at,
    ctx_ref,
    win_ref,
    cot_keep,
    cot_got,
    cot_last,
    near_first,
    far_first,
    near_ref,
    far_ref,
    bias_ref,
    keep_ref,
    along_ref,
    close_ref,
    active_ref,
    upper_ref,
    hidden_ref,
    low_ref,
    first_low_ref,
    dctx_ref,
    up_sum_ref,
    sums_ref,
    total_ref,
    wide_ref,
    parts_ref,
    normed_ref,
    scale_ref,
    slope_ref,
    columns_ref,
    out_ref,
    weights_ref,
    sem,
):
    step, groups = pl.program_id(0), slope_ref.shape[0]
    depth, width = near_ref.shape[2:]
    model, own = total_ref.shape
    feat = keep_ref.shape[1]
    heads = ctx_ref.shape[1]
    skip = out_ref.shape[3] - heads

    def weight_copies(block):
        return [
            pltpu.make_async_copy(
                source.at[which, block], weights_ref.at[which, side, block], sem.at[2 + 4 * block + 2 * which + side]
            )
            for which in range(2)
            for side, source in enumerate((near_ref, far_ref))
        ]

    first_copies = [
        pltpu.make_async_copy(
            source.at[:, :, pl.ds(width - out_ref.shape[3], out_ref.shape[3])], out_ref.at[side], sem.at[side]
        )
        for side, source in enumerate((near_first, far_first))
    ]

    def over_columns(body):
        def run(i, carry):
            body(pl.ds(pl.multiple_of(i * 128, 128), 128))
            return carry

        lax.fori_loop(0, own // 128, run, 0)

    def sum_parts(first):
        for i in range(3):
            sums_ref[:, first + i : first + i + 1] = jnp.sum(parts_ref[i], axis=1, keepdims=True)
        parts_ref[...] = jnp.zeros(parts_ref.shape, F32)

    @pl.when(step == 0)
    def start():
        for copy in first_copies:
            copy.start()
        for block in range(groups):
            for copy in weight_copies(block):
                copy.start()
        for i in range(6):
            columns_ref[i] = jnp.broadcast_to(win_ref[:, at + i : at + i + 1].astype(F32), (model, 128))
        parts_ref[...] = jnp.zeros(parts_ref.shape, F32)
        for copy in first_copies:
            copy.wait()
        for n in range(groups):
            near, far = nn(out_ref[0, n, :, skip:], ctx_ref[n]), nn(out_ref[1, n, :, skip:], ctx_ref[n])
            if n == 0:
                total_ref[:depth], total_ref[depth:] = near, far
            else:
                total_ref[:depth] += near
                total_ref[depth:] += far

        def body(cols):
            values = total_ref[:, cols] + columns_ref[0] + win_ref[:, cols].astype(F32)
            center, scale = norm_stats(values)
            normed = (values - center) * scale
            hidden = normed * columns_ref[1] + columns_ref[2]
            normed_ref[:, cols] = normed
            scale_ref[:, cols] = scale
            wide_ref[:, cols] = hidden
            hidden_ref[:, cols] = hidden.astype(BF16)

        over_columns(body)
        total_ref[...] = jnp.zeros(total_ref.shape, F32)

    @pl.when(step < groups)
    def forward():
        for block in range(groups):

            @pl.when(step == block)
            def arrive(block=block):
                for copy in weight_copies(block):
                    copy.wait()

        piece = width // 3
        for low in range(0, width, piece):
            rows = slice(low, low + piece)
            upper = tn(weights_ref[0, 0, step, :, rows], hidden_ref[:depth])
            upper = upper + tn(weights_ref[0, 1, step, :, rows], hidden_ref[depth:])
            upper = upper + across_lanes(bias_ref[0], 0, low, low + piece, own)
            phi = 0.5 * (1.0 + lax.erf(upper * np.float32(0.5**0.5)))
            active_ref[0, rows] = (upper * phi).astype(BF16)
            slope_ref[step, rows] = (
                phi + upper * jnp.exp(-0.5 * upper * upper) * np.float32(1.0 / np.sqrt(2.0 * np.pi))
            ).astype(BF16)
        active = active_ref[0]
        total_ref[:depth] += nn(weights_ref[1, 0, step], active)
        total_ref[depth:] += nn(weights_ref[1, 1, step], active)

    @pl.when(step == groups - 1)
    def turn():
        pieces = (cot_keep, cot_got, cot_last)

        def body(cols):
            values = total_ref[:, cols] + columns_ref[3] + wide_ref[:, cols]
            center, scale = norm_stats(values)
            normed = (values - center) * scale
            result = (normed * columns_ref[4] + columns_ref[5]).astype(BF16)
            keep_ref[0, :, cols] = result[:feat]
            along_ref[0, :, cols] = result[feat : 2 * feat]
            close_ref[0, :, cols] = result[2 * feat : 3 * feat]
            along_ref[1, :, cols] = result[3 * feat :]
            cot = jnp.concatenate([pieces[i][j, :, cols] for i, j in PIECES], axis=0).astype(F32)
            grad = norm_back(cot, normed, scale, columns_ref[4])
            total_ref[:, cols] = grad
            grad_low = grad.astype(BF16)
            low_ref[:, cols] = grad_low
            parts_ref[0] += grad_low.astype(F32)
            parts_ref[1] += cot * normed
            parts_ref[2] += cot

        over_columns(body)
        sum_parts(3)

    @pl.when(step >= groups)
    def backward():
        block = step - groups
        upper = tn(weights_ref[1, 0, block], low_ref[:depth]) + tn(weights_ref[1, 1, block], low_ref[depth:])
        upper = (upper * slope_ref[block].astype(F32)).astype(BF16)
        upper_ref[0] = upper
        up_sum_ref[0] = jnp.sum(upper.astype(F32), axis=1, keepdims=True)
        total_ref[:depth] += nn(weights_ref[0, 0, block], upper)
        total_ref[depth:] += nn(weights_ref[0, 1, block], upper)

    @pl.when(step == 2 * groups - 1)
    def finish():
        def body(cols):
            hidden_grad = total_ref[:, cols]
            normed = normed_ref[:, cols]
            first_low = norm_back(hidden_grad, normed, scale_ref[:, cols], columns_ref[1]).astype(BF16)
            first_low_ref[:, cols] = first_low
            parts_ref[0] += first_low.astype(F32)
            parts_ref[1] += hidden_grad * normed
            parts_ref[2] += hidden_grad

        over_columns(body)
        sum_parts(0)
        for n in range(groups):
            grads = tn(out_ref[0, n, :, skip:], first_low_ref[:depth]) + tn(out_ref[1, n, :, skip:], first_low_ref[depth:])
            dctx_ref[n] = grads.astype(BF16)


def once(array):
    return pl.BlockSpec(
        array.shape, lambda step, *_: (0,) * len(array.shape), pipeline_mode=pl.Buffered(1)
    )


def mlp(at, ctx, win, cot, near_first, far_first, near, far, bias):
    groups, depth, width = near.shape[1:]
    feat, own = cot[0].shape[1:]
    model = feat * 4
    out_columns = -(-ctx.shape[1] // 128) * 128

    def early(array):
        return pl.BlockSpec((1,) + array.shape[1:], lambda step, *_: (jnp.minimum(step, groups - 1), 0, 0))

    def late(array):
        return pl.BlockSpec((1,) + array.shape[1:], lambda step, *_: (jnp.maximum(step - groups, 0), 0, 0))

    outs = [
        jax.ShapeDtypeStruct((1, feat, own), BF16),
        jax.ShapeDtypeStruct((2, feat, own), BF16),
        jax.ShapeDtypeStruct((1, feat, own), BF16),
        jax.ShapeDtypeStruct((groups, width, own), BF16),
        jax.ShapeDtypeStruct((groups, width, own), BF16),
        jax.ShapeDtypeStruct((model, own), BF16),
        jax.ShapeDtypeStruct((model, own), BF16),
        jax.ShapeDtypeStruct((model, own), BF16),
        jax.ShapeDtypeStruct(ctx.shape, BF16),
        jax.ShapeDtypeStruct((groups, width, 1), F32),
        jax.ShapeDtypeStruct((model, 6), F32),
    ]
    return pl.pallas_call(
        functools.partial(mlp_kernel, at),
        grid=(2 * groups,),
        in_specs=[
            once(ctx),
            once(win),
            *[once(piece) for piece in cot],
            HBM,
            HBM,
            HBM,
            HBM,
            pl.BlockSpec((1,) + bias.shape[1:], lambda step, *_: (jnp.minimum(step, groups - 1), 0, 0)),
        ],
        out_specs=[early(o) if i == 3 else late(o) if i in (4, 9) else once(o) for i, o in enumerate(outs)],
        out_shape=outs,
        scratch_shapes=[
            pltpu.VMEM((model, own), F32),
            pltpu.VMEM((model, own), F32),
            pltpu.VMEM((3, model, 128), F32),
            pltpu.VMEM((model, own), F32),
            pltpu.VMEM((1, own), F32),
            pltpu.VMEM((groups, width, own), BF16),
            pltpu.VMEM((6, model, 128), F32),
            pltpu.VMEM((2, groups, depth, out_columns), BF16),
            pltpu.VMEM((2, 2, groups, depth, width), BF16),
            pltpu.SemaphoreType.DMA((2 + 4 * groups,)),
        ],
        compiler_params=params(44),
        cost_estimate=cost(400),
        name="mlp",
    )(ctx, win, *cot, *held(near_first, far_first, near, far), bias)


def hidden_grad_kernel(low_ref, hidden_ref, active_ref, upper_ref, down_keep, down_send, up_keep, up_send):
    depth = down_keep.shape[1]
    for keep, send, left, right in (
        (down_keep, down_send, low_ref, active_ref),
        (up_keep, up_send, hidden_ref, upper_ref),
    ):
        keep[0] = nt(left[:depth], right[0]).astype(BF16)
        send[0] = nt(left[depth:], right[0]).astype(BF16)


def hidden_grads(low, hidden, active, upper):
    groups, width, own = active.shape
    out = jax.ShapeDtypeStruct((groups, low.shape[0] // 2, width), BF16)
    return pl.pallas_call(
        hidden_grad_kernel,
        grid=(groups,),
        in_specs=[whole_block(low), whole_block(hidden), step_block(active), step_block(upper)],
        out_specs=[step_block(out)] * 4,
        out_shape=[out] * 4,
        compiler_params=params(32),
        cost_estimate=cost(100),
        name="hidden_grads",
    )(low, hidden, active, upper)


def first_grad_kernel(
    width,
    win_ref,
    par_keep,
    par_got,
    par_last,
    dwin_ref,
    dpar_ref,
    low_ref,
    ctx_ref,
    up_ref,
    sums_ref,
    keep_ref,
    send_ref,
    par_ref,
):
    join_pieces((par_keep, par_got, par_last), par_ref)
    depth = keep_ref.shape[1]
    half = depth // 4
    query = jnp.sum(dwin_ref[0, :width].astype(F32), axis=1, keepdims=True)
    value = jnp.sum(dwin_ref[0, 2 * width :].astype(F32), axis=1, keepdims=True)
    value = value + jnp.sum(dpar_ref[0, width:].astype(F32), axis=1, keepdims=True)
    by_row = [array[i : i + half] for array in (query, value, up_ref[0]) for i in range(0, array.shape[0], half)]
    by_row = jnp.concatenate(by_row, axis=1)
    by_row = jnp.concatenate([by_row] * 4, axis=0)
    used = by_row.shape[1] + 6
    pad = jnp.zeros((depth, keep_ref.shape[2] - 4 * width - used), F32)
    for part, out_ref in enumerate((keep_ref, send_ref)):
        rows = slice(part * depth, (part + 1) * depth)
        win, par = win_ref[rows], par_ref[rows]
        out_ref[0, :, :width] = nt(win, dwin_ref[0, :width]).astype(BF16)
        for i in range(1, 3):
            grads = nt(win, dwin_ref[0, i * width : (i + 1) * width])
            grads = grads + nt(par, dpar_ref[0, (i - 1) * width : i * width])
            out_ref[0, :, i * width : (i + 1) * width] = grads.astype(BF16)
        out_ref[0, :, 3 * width : 4 * width] = nt(low_ref[rows], ctx_ref[0]).astype(BF16)
        extra = jnp.concatenate([by_row, sums_ref[rows], pad], axis=1)
        out_ref[0, :, 4 * width :] = extra.astype(BF16)


def first_grads(win, par, dwin, dpar, low, ctx, up_bias, sums):
    groups, width, own = ctx.shape
    out = jax.ShapeDtypeStruct((groups, low.shape[0] // 2, 4 * width + 128), BF16)
    return pl.pallas_call(
        functools.partial(first_grad_kernel, width),
        grid=(groups,),
        in_specs=[
            whole_block(win),
            *[whole_block(piece) for piece in par],
            step_block(dwin),
            step_block(dpar),
            whole_block(low),
            step_block(ctx),
            step_block(up_bias),
            whole_block(sums),
        ],
        out_specs=[step_block(out)] * 2,
        out_shape=[out] * 2,
        scratch_shapes=[pltpu.VMEM((low.shape[0], par[0].shape[2]), BF16)],
        compiler_params=params(40),
        cost_estimate=cost(15),
        name="first_grads",
    )(win, *par, dwin, dpar, low, ctx, up_bias, sums)


def token_grad_kernel(low, high, parent, near_ref, far_ref, dwin_ref, more_ref, keep_ref, along_ref, close_ref, total_ref):
    step, last = pl.program_id(0), pl.num_programs(0) - 1
    depth = near_ref.shape[1]
    columns = total_ref.shape[1]
    own = more_ref.shape[1]

    @pl.when(step == 0)
    def start():
        total_ref[...] = jnp.zeros(total_ref.shape, F32)
        if not parent:
            total_ref[:, :own] = more_ref[...].astype(F32)

    if parent:
        grads = jnp.concatenate([more_ref[0], dwin_ref[0, low:high, more_ref.shape[2] :]], axis=1)
    else:
        grads = dwin_ref[0, low:high, :columns]
    total_ref[:depth] += nn(near_ref[0, :, low:high], grads)
    total_ref[depth:] += nn(far_ref[0, :, low:high], grads)

    @pl.when(step == last)
    def finish():
        feat = keep_ref.shape[1]
        for i, out in enumerate((keep_ref.at[0], along_ref.at[0], close_ref.at[0], along_ref.at[1])):
            out[...] = total_ref[i * feat : (i + 1) * feat].astype(BF16)


def token_grads(near, far, dwin, more, low, high, parent, columns):
    groups, depth = near.shape[:2]
    feat = depth // 2
    outs = [jax.ShapeDtypeStruct((n, feat, columns), BF16) for n in (1, 2, 1)]
    return pl.pallas_call(
        functools.partial(token_grad_kernel, low, high, parent),
        grid=(groups,),
        in_specs=[
            step_block(near),
            step_block(far),
            step_block(dwin),
            step_block(more) if parent else whole_block(more),
        ],
        out_specs=[whole_block(out) for out in outs],
        out_shape=outs,
        scratch_shapes=[pltpu.VMEM((2 * depth, columns), F32)],
        compiler_params=params(40),
        cost_estimate=cost(50 if parent else 30),
        name="token_grads",
    )(near, far, dwin, more)


def attend(lengths, segments, bank, scalars, window, parent):
    groups, rows, columns = window.shape
    width = rows // 3
    heads = width // HEAD
    outs = (
        jax.ShapeDtypeStruct((groups, width, sum(lengths)), BF16),
        jax.ShapeDtypeStruct((groups, heads, sum(lengths)), F32),
    )
    return pl.pallas_call(
        functools.partial(attention_forward, heads, lengths, segments, bank),
        grid=(groups,),
        in_specs=[SMEM] * 3 + [step_block(window), step_block(parent)],
        out_specs=[step_block(out) for out in outs],
        out_shape=outs,
        compiler_params=params(40),
        cost_estimate=cost(130),
        name="attention_forward",
    )(*scalars, window, parent)


def attend_back(lengths, segments, bank, scalars, window, parent, dctx, lse):
    groups, rows, columns = window.shape
    outs = (jax.ShapeDtypeStruct(window.shape, BF16), jax.ShapeDtypeStruct(parent.shape, BF16))
    return pl.pallas_call(
        functools.partial(attention_backward, rows // 3 // HEAD, lengths, segments, bank),
        grid=(groups,),
        in_specs=[SMEM] * 3 + [step_block(array) for array in (window, parent, dctx, lse)],
        out_specs=[step_block(out) for out in outs],
        out_shape=outs,
        compiler_params=params(40),
        cost_estimate=cost(200),
        name="attention_backward",
    )(*scalars, window, parent, dctx, lse)


def swap(array, axis, mask):
    count = lax.axis_size(axis)
    return lax.ppermute(array, axis, [(i, i ^ mask) for i in range(count)])


SMEM = pl.BlockSpec(memory_space=pltpu.SMEM)
VMEM = pl.BlockSpec(memory_space=pltpu.VMEM)
HBM = pl.BlockSpec(memory_space=pltpu.HBM)
ORDER = (0, 2, 1, 3)
SENDS = ((0, 0), (1, 0), (2, 0), (1, 1))


def at_distance(here_ref, lists, slot, j):
    distance = ORDER[slot]
    return static_of(here_ref[1], [lists[i ^ distance][j] for i in range(len(lists))])


def flipped(here_ref, part, half):
    return pl.multiple_of((part ^ here_ref[2]) * half, 32)


def spots(rows, columns, shift):
    return (
        lax.broadcasted_iota(jnp.int32, (rows, columns), 0) + shift
        == lax.broadcasted_iota(jnp.int32, (rows, columns), 1)
    ).astype(BF16)


def as_row(ref):
    return ref[...].astype(F32).reshape(1, ref.shape[0])


def fetch(pairs, sem):
    copies = [pltpu.make_async_copy(source, target, sem.at[i]) for i, (source, target) in enumerate(pairs)]
    for copy in copies:
        copy.start()
    for copy in copies:
        copy.wait()


def pack_weights_kernel(here_ref, *refs):
    count = 9
    inputs, half_ref = refs[:count], refs[count]
    held, turned_ref, sem = refs[count + 1 : -2], refs[-2], refs[-1]
    feat, width = inputs[0].shape
    half = feat // 2
    rows = pl.ds(flipped(here_ref, 0, half), half)
    small = [inputs[i] for i in (0, 1, 2, 3, 6, 7, 8)]
    fetch(
        [*zip(small, held)]
        + [(inputs[4 + i].at[rows, :], half_ref.at[pl.ds((1 + i) * half, half), :]) for i in range(2)],
        sem,
    )
    query_ref, key_ref, value_ref, out_ref, up_b_ref, query_b_ref, value_b_ref = held
    turned_ref[...] = tn(out_ref[...], spots(width, width, 0)).astype(BF16)
    for i, ref in enumerate((query_ref, key_ref, value_ref, turned_ref)):
        half_ref[:half, i * width : (i + 1) * width] = ref[rows, :]
    zero = jnp.zeros((1, width), F32)
    joint = [as_row(query_b_ref), zero, as_row(value_b_ref), zero]
    wide = (half_ref.shape[0] - 3 * half, half_ref.shape[1])
    index = lax.broadcasted_iota(jnp.int32, wide, 0)
    up_row = jnp.broadcast_to(as_row(up_b_ref), wide)
    joint_row = jnp.broadcast_to(jnp.concatenate(joint, axis=1), wide)
    half_ref[3 * half :] = jnp.where(index == 0, up_row, jnp.where(index == 1, joint_row, 0.0)).astype(BF16)


def pack_weights(here, query, key, value, out, up, down, *biases):
    feat, width = query.shape
    hidden = up.shape[1]
    inputs = (query, key, value, out, up, down, *biases)
    small = [query, key, value, out, *biases]
    return pl.pallas_call(
        pack_weights_kernel,
        in_specs=[SMEM] + [HBM] * len(inputs),
        out_specs=VMEM,
        out_shape=jax.ShapeDtypeStruct((3 * feat // 2 + 16, hidden), BF16),
        scratch_shapes=[pltpu.VMEM(array.shape, array.dtype) for array in small]
        + [pltpu.VMEM((feat, width), BF16), pltpu.SemaphoreType.DMA((len(inputs),))],
        compiler_params=params(24),
        cost_estimate=cost(0.1),
        name="pack_weights",
    )(here, *held(*inputs))


def pack_kernel(blocks, sided, here_ref, *refs):
    given = 1 + sided
    outs, held, sem = refs[given : given + 3], refs[given + 3 : given + 3 + given], refs[-1]
    fetch([*zip(refs[:given], held)], sem)
    source_ref = held[0]
    half = source_ref.shape[0] // 2
    count = len(blocks[0])
    if sided:
        mem_ref, vector_refs, side_ref = held[1], held[2:], refs[-2]
        bank = mem_ref.shape[0]
        vectors = jnp.concatenate([as_row(ref) for ref in vector_refs], axis=0)
        vectors = jnp.concatenate([vectors, jnp.zeros((8 - len(vector_refs), vectors.shape[1]), F32)], axis=0)
        side = tn(mem_ref[...], spots(bank, 128, 0)) + tn(vectors.astype(BF16), spots(8, 128, bank))
        side_ref[...] = side.astype(BF16)
    for slot, (out, place) in enumerate(SENDS):
        for part in range(2):
            low = flipped(here_ref, part, half)
            rows = slice(part * half, (part + 1) * half)
            for j in range(count):
                at = pl.multiple_of(at_distance(here_ref, blocks, slot, j) * 128, 128)
                outs[out][place, rows, j * 128 : (j + 1) * 128] = source_ref[pl.ds(low, half), pl.ds(at, 128)]
            if sided:
                outs[out][place, rows, count * 128 :] = side_ref[pl.ds(low, half), :]


def pack(blocks, here, source, *side):
    feat = source.shape[0]
    columns = len(blocks[0]) * 128 + (128 if side else 0)
    inputs = (source, *side)
    return pl.pallas_call(
        functools.partial(pack_kernel, blocks, len(side)),
        in_specs=[SMEM] + [HBM] * len(inputs),
        out_specs=[VMEM] * 3,
        out_shape=[jax.ShapeDtypeStruct((n, feat, columns), source.dtype) for n in (1, 2, 1)],
        scratch_shapes=[pltpu.VMEM(array.shape, array.dtype) for array in inputs]
        + ([pltpu.VMEM((feat, 128), BF16)] if side else [])
        + [pltpu.SemaphoreType.DMA((len(inputs),))],
        compiler_params=params(24),
        cost_estimate=cost(0.1),
        name="pack",
    )(here, *held(*inputs))


def exchange(keep, along, near):
    got = swap(along, "col", 2)
    return keep, got, swap(jnp.concatenate([near, got[1:]], axis=0), "col", 1)


def joined(pieces):
    keep, got, last = pieces
    return jnp.concatenate([keep, got[:1], last], axis=0)


PIECES = ((0, 0), (1, 0), (2, 0), (2, 1))


def parent_of(here_ref, parents_ref, segments, slot, j):
    return parents_ref[here_ref[0] * here_ref[3] + at_distance(here_ref, segments, slot, j)]


def pick_kernel(segments, here_ref, parents_ref, source_ref, *refs):
    outs, sem = refs[:3], refs[3]
    half = source_ref.shape[1] // 2
    seg_row = here_ref[3]
    pairs = []
    for slot, (out, place) in enumerate(SENDS):
        for j in range(len(segments[0])):
            seg = jnp.maximum(parent_of(here_ref, parents_ref, segments, slot, j), 0)
            row = lax.div(seg, seg_row)
            at = pl.multiple_of((seg - row * seg_row) * SEG, SEG)
            for part in range(2):
                rows = slice(part * half, (part + 1) * half)
                source = source_ref.at[row, pl.ds(flipped(here_ref, part, half), half), pl.ds(at, SEG)]
                pairs.append((source, outs[out].at[place, rows, pl.ds(j * SEG, SEG)]))
    fetch(pairs, sem)


def pick_parents(segments, here, parents, gathered):
    feat = gathered.shape[1]
    columns = len(segments[0]) * SEG
    return pl.pallas_call(
        functools.partial(pick_kernel, segments),
        in_specs=[SMEM, SMEM, HBM],
        out_specs=[VMEM] * 3,
        out_shape=[jax.ShapeDtypeStruct((n, feat, columns), gathered.dtype) for n in (1, 2, 1)],
        scratch_shapes=[pltpu.SemaphoreType.DMA((8 * len(segments[0]),))],
        compiler_params=params(24),
        cost_estimate=cost(1),
        name="pick_parents",
    )(here, parents, *held(gathered))


def add_parents_kernel(segments, seg_row, here_ref, parents_ref, *refs):
    pieces, given_ref, sum_ref, out_ref, sem = refs[:3], refs[3], refs[4], refs[5], refs[6]
    window = len(segments[0]) * SEG
    copies = []
    sum_ref[...] = jnp.zeros(sum_ref.shape, F32)
    for slot, (piece, place) in enumerate(PIECES):
        for j in range(len(segments[0])):
            seg = parent_of(here_ref, parents_ref, segments, slot, j)

            @pl.when(seg >= 0)
            def add(seg=seg, piece=piece, place=place, cols=slice(j * SEG, (j + 1) * SEG)):
                sum_ref[seg] += pieces[piece][place, :, cols].astype(F32)

    mem = sum(pieces[piece][place, :, window:].astype(F32) for piece, place in PIECES)
    for r in range(out_ref.shape[0]):
        for s in range(seg_row):
            out_ref[r, :, s * SEG : (s + 1) * SEG] = sum_ref[r * seg_row + s].astype(BF16)
        out_ref[r, :, seg_row * SEG :] = mem.astype(BF16)
        copies.append(pltpu.make_async_copy(out_ref.at[r], given_ref.at[r], sem.at[r]))
        copies[-1].start()
    for copy in copies:
        copy.wait()


def add_parents(segments, here, parents, pieces, rows, seg_row):
    feat, columns = pieces[0].shape[1:]
    bank = columns - len(segments[0]) * SEG
    return pl.pallas_call(
        functools.partial(add_parents_kernel, segments, seg_row),
        in_specs=[SMEM, SMEM, VMEM, VMEM, VMEM],
        out_specs=HBM,
        out_shape=pltpu.HBM((rows, feat, seg_row * SEG + bank), BF16),
        scratch_shapes=[
            pltpu.VMEM((rows * seg_row, feat, SEG), F32),
            pltpu.VMEM((rows, feat, seg_row * SEG + bank), BF16),
            pltpu.SemaphoreType.DMA((rows,)),
        ],
        compiler_params=params(40),
        cost_estimate=cost(60),
        name="add_parents",
    )(here, parents, *pieces)


def finish_kernel(blocks, here_ref, placed_ref, *refs):
    pieces, out_ref = refs[:3], refs[3]
    half = out_ref.shape[0] // 2
    for part in range(2):
        low = flipped(here_ref, part, half)
        rows = slice(part * half, (part + 1) * half)
        out_ref[pl.ds(low, half), :] = placed_ref[rows, : out_ref.shape[1]].astype(F32)
        for slot, (piece, place) in enumerate(PIECES):
            for j in range(len(blocks[0])):
                at = pl.multiple_of(at_distance(here_ref, blocks, slot, j) * 128, 128)
                out_ref[pl.ds(low, half), pl.ds(at, 128)] += pieces[piece][
                    place, rows, j * 128 : (j + 1) * 128
                ].astype(F32)


def finish_tokens(blocks, here, placed, pieces, columns):
    return pl.pallas_call(
        functools.partial(finish_kernel, blocks),
        in_specs=[SMEM, VMEM, VMEM, VMEM, VMEM],
        out_specs=VMEM,
        out_shape=jax.ShapeDtypeStruct((placed.shape[0], columns), F32),
        compiler_params=params(24),
        cost_estimate=cost(2.5),
        name="finish_tokens",
    )(here, placed, *pieces)


def place_kernel(blocks, here_ref, *refs):
    pieces, out_ref = refs[:3], refs[3]
    half = out_ref.shape[0] // 2
    for part in range(2):
        low = flipped(here_ref, part, half)
        rows = slice(part * half, (part + 1) * half)
        for slot, (piece, place) in enumerate(PIECES):
            for j in range(pieces[0].shape[2] // 128):
                at = pl.multiple_of(at_distance(here_ref, blocks, slot, j) * 128, 128)
                out_ref[pl.ds(low, half), pl.ds(at, 128)] = pieces[piece][place, rows, j * 128 : (j + 1) * 128]


def place(blocks, here, pieces, columns):
    return pl.pallas_call(
        functools.partial(place_kernel, blocks),
        in_specs=[SMEM, VMEM, VMEM, VMEM],
        out_specs=VMEM,
        out_shape=jax.ShapeDtypeStruct((pieces[0].shape[1], columns), pieces[0].dtype),
        compiler_params=params(24),
        cost_estimate=cost(1.7),
        name="place",
    )(here, *pieces)


def unpack_kernel(width, count, here_ref, mine_ref, other_ref, query_ref, key_ref, value_ref, out_ref, more_ref, all_ref):
    half = mine_ref.shape[0]
    all_ref[pl.ds(flipped(here_ref, 0, half), half), :] = mine_ref[...].astype(F32)
    all_ref[pl.ds(flipped(here_ref, 1, half), half), :] = other_ref[...].astype(F32)
    for i, ref in enumerate((query_ref, key_ref, value_ref)):
        ref[...] = all_ref[:, i * width : (i + 1) * width]
    out_ref[...] = all_ref[:, 3 * width : 4 * width].T
    rows = all_ref[:, 4 * width :].T
    more_ref[...] = rows[: more_ref.shape[0]]


def unpack(here, mine, other, width, count):
    feat = 2 * mine.shape[0]
    square = jax.ShapeDtypeStruct((feat, width), F32)
    return pl.pallas_call(
        functools.partial(unpack_kernel, width, count),
        in_specs=[SMEM, VMEM, VMEM],
        out_specs=[VMEM] * 5,
        out_shape=[square] * 3 + [jax.ShapeDtypeStruct((width, feat), F32), jax.ShapeDtypeStruct((24, feat), F32)],
        scratch_shapes=[pltpu.VMEM((feat, mine.shape[1]), F32)],
        compiler_params=params(24),
        cost_estimate=cost(2),
        name="unpack",
    )(here, mine, other)


def gather_weights(half):
    return [half] + [swap(half, "row", n) for n in range(1, lax.axis_size("row"))]


def spread_weights(along, *gate):
    along = jnp.stack(along, axis=1)
    opposite = swap(along, "leaf", 1)
    across = after(swap(along, "col", 2), *gate)
    return along, opposite, across, swap(across, "leaf", 1)


def whole_weights(parts):
    near = jnp.stack(parts, axis=2)
    arrays, rows, blocks, depth, columns = near.shape
    near = near.reshape(arrays, rows, blocks * depth, columns)
    return near, swap(near, "col", 1)


def add_up(*terms):
    total = terms[0].astype(F32)
    for term in terms[1:]:
        total = total + term.astype(F32)
    return total


def reduce_blocks(keep):
    rows, features, columns = keep.shape
    return rows, 2, 2, features // 4, columns


def reduce_across(keep, near):
    shape = reduce_blocks(keep)
    return add_up(keep.reshape(shape)[:, :, 1], near.reshape(shape)[:, :, 1]).astype(BF16)


def reduce_y(keep, near):
    shape = reduce_blocks(keep)
    return add_up(keep.reshape(shape)[:, 1], near.reshape(shape)[:, 1]).astype(BF16)


def reduce_x(keep, near, got):
    shape = reduce_blocks(keep)
    return add_up(keep.reshape(shape)[:, 0, 1], near.reshape(shape)[:, 0, 1], got[:, 1]).astype(BF16)


def reduce_up(keep, near, across):
    shape = reduce_blocks(keep)
    return add_up(keep.reshape(shape)[:, 1, 0], near.reshape(shape)[:, 1, 0], across[:, 1]).astype(BF16)


def reduce_along(keep, near, across, up):
    shape = reduce_blocks(keep)
    mine = add_up(keep.reshape(shape)[:, 0, 0], near.reshape(shape)[:, 0, 0], across[:, 0], up)
    return [mine[n].astype(BF16) for n in range(shape[0])]


def reduce_rows(along, got):
    total = add_up(along[0], *got)
    mask = 2
    while mask < lax.axis_size("leaf"):
        total = add_up(total, swap(total.astype(BF16), "leaf", mask))
        mask *= 2
    return total.astype(BF16)


def reduce_corner(keep, near):
    shape = reduce_blocks(keep)
    middle = shape[0] // 2
    corner = add_up(keep.reshape(shape)[:, 1, 1], near.reshape(shape)[:, 1, 1]).astype(BF16)
    return corner[:middle], corner[middle:]


def reduce_edges(keep, near, by_leaf, by_col):
    shape = reduce_blocks(keep)
    middle = shape[0] // 2
    keep, near = keep.reshape(shape), near.reshape(shape)
    leaf = add_up(keep[:, 0, 1], near[:, 0, 1])
    leaf = jnp.concatenate([leaf[:middle], add_up(leaf[middle:], by_col)], axis=0).astype(BF16)
    along = add_up(keep[:, 1, 0], near[:, 1, 0])
    along = jnp.concatenate([add_up(along[:middle], by_leaf), along[middle:]], axis=0).astype(BF16)
    return leaf, along


def reduce_mine(keep, near, leaf, along):
    shape = reduce_blocks(keep)
    mine = add_up(keep.reshape(shape)[:, 0, 0], near.reshape(shape)[:, 0, 0], leaf, along)
    return [mine[n].astype(BF16) for n in range(shape[0])]


def send_rows(along):
    return [swap(block, "row", n) for n, block in enumerate(along) if n]


def norm_stats(values):
    center = jnp.mean(values, axis=0, keepdims=True)
    spread = jnp.mean(values * values, axis=0, keepdims=True) - center * center
    return center, lax.rsqrt(spread + EPSILON)


def norm_back(grad, normed, scale, gain):
    scaled = grad * gain
    return scale * (
        scaled
        - jnp.mean(scaled, axis=0, keepdims=True)
        - normed * jnp.mean(scaled * normed, axis=0, keepdims=True)
    )


def lane_sum(array):
    return jnp.sum(array, axis=-1, dtype=F32)


def on_device(
    tokens,
    memory,
    parents,
    memory_slots,
    query_weight,
    query_bias,
    key_weight,
    value_weight,
    value_bias,
    out_weight,
    out_bias,
    norm_gain,
    norm_shift,
    up_weight,
    up_bias,
    down_weight,
    down_bias,
    final_gain,
    final_shift,
    cotangent,
):
    rows, cols = lax.axis_size("row"), lax.axis_size("col")
    row, col = lax.axis_index("row"), lax.axis_index("col")
    feat, row_tokens = tokens.shape
    own = row_tokens // cols
    seg_row = row_tokens // SEG
    model = feat * cols
    width = query_weight.shape[1]
    hidden_width = up_weight.shape[1]
    bank = memory.shape[0]
    segments, ranges = plan_windows(own, cols)
    window = len(segments[0]) * SEG
    tail = 128
    lengths = tuple(min(SEG, own - j * SEG) for j in range(len(segments[0])))
    half = feat // 2
    parity = lax.axis_index("leaf") % 2
    here = jnp.stack([row, col, parity, jnp.int32(seg_row)]).astype(jnp.int32)
    blocks = [[b for a, n in ranges[i] for b in range(a // 128, (a + n) // 128)] for i in range(cols)]
    own_blocks = [each[: own // 128] for each in blocks]
    scalars = (here, parents, memory_slots)

    weight_half = pack_weights(
        here, query_weight, key_weight, value_weight, out_weight, up_weight, down_weight, up_bias, query_bias, value_bias
    )
    along = gather_weights(weight_half)

    vectors = (out_bias, norm_gain, norm_shift, down_bias, final_gain, final_shift)
    token_sends = pack(blocks, here, after(tokens, weight_half), memory, *vectors)
    cot_sends = pack(own_blocks, here, after(cotangent, token_sends))
    token_got = swap(token_sends[1], "col", 2)
    along = after(along, cot_sends, token_got)
    everything = lax.all_gather(after(tokens, along), "row", axis=0)
    row_vectors = jnp.stack([piece[3 * half :] for piece in along])
    near_first, far_first = (array[0] for array in whole_weights(spread_weights([piece[:half][None] for piece in along])))
    token_last = swap(jnp.concatenate([token_sends[2], token_got[1:]], axis=0), "col", 1)
    tok_window = joined((token_sends[0], token_got, token_last)).reshape(model, window + tail)
    win = project(near_first, far_first, tok_window, row_vectors, 0, 3 * width, width)
    second_parts = spread_weights([piece[half : 3 * half].reshape(2, half, -1) for piece in along], win)
    cot_keep, cot_along, cot_near = after(cot_sends, second_parts[2])
    cot_got = swap(cot_along, "col", 2)
    cot_near = jnp.concatenate([cot_near, cot_got[1:]], axis=0)
    cot_pieces = cot_keep, cot_got, swap(cot_near, "col", 1)
    everything = after(everything, second_parts[2], cot_near)
    par_keep, par_along, par_near = pick_parents(segments, here, parents, everything)
    par_got = swap(par_along, "col", 2)
    near, far = whole_weights(after(second_parts, par_along))
    par_got = after(par_got, near)
    par_near = jnp.concatenate([par_near, par_got[1:]], axis=0)
    tok_parent = (par_keep, par_got, swap(par_near, "col", 1))
    par = project(near_first, far_first, tok_parent, row_vectors, width, 3 * width, 0)
    ctx, lse = attend(lengths, segments, bank, scalars, win, par)
    at = window + bank
    *result, active, upper_low, hidden_low, down_low, first_low, dctx, up_bias_grad, sums = mlp(
        at, ctx, tok_window, cot_pieces, near_first, far_first, near, far, row_vectors
    )
    result_keep, result_along, result_near = result
    dwin, dpar = attend_back(lengths, segments, bank, scalars, win, par, dctx, lse)

    par_keep, par_along, par_near = token_grads(
        near_first, far_first, dwin, dpar, width, 3 * width, True, window + tail
    )
    par_got = swap(par_along, "col", 2)
    down_keep, down_send, up_keep, up_send = hidden_grads(after(down_low, par_along), hidden_low, active, upper_low)
    down_near, up_near = swap(down_send, "col", 1), swap(up_send, "col", 1)
    par_got = after(par_got, up_send)
    par_near = jnp.concatenate([par_near, par_got[1:]], axis=0)
    placed = add_parents(segments, here, parents, (par_keep, par_got, swap(par_near, "col", 1)), rows, seg_row)
    down_across = reduce_across(after(down_keep, placed), down_near)
    up_along = reduce_y(after(up_keep, down_across), up_near)
    first_keep, first_send = first_grads(
        tok_window, tok_parent, dwin, dpar, after(first_low, up_along), ctx, up_bias_grad, sums
    )
    placed = lax.psum_scatter(placed, "row", scatter_dimension=0, tiled=False)
    first_near = swap(first_send, "col", 1)
    dtok = token_grads(near_first, far_first, dwin, after(first_low, first_send), 0, 3 * width, False, window)
    corner = reduce_corner(after(first_keep, dtok), first_near)
    by_leaf, by_col = swap(corner[0], "leaf", 1), swap(corner[1], "col", 2)
    up_got = swap(up_along, "col", 2)
    up_across = reduce_x(after(up_keep, corner), up_near, up_got)
    down_across = swap(down_across, "leaf", 1)
    down_up = reduce_up(after(down_keep, up_across), down_near, down_across)
    edges = reduce_edges(after(first_keep, down_up), first_near, by_leaf, by_col)
    by_leaf, by_col = swap(edges[0], "leaf", 1), swap(edges[1], "col", 2)
    up_across = swap(up_across, "leaf", 1)
    up_rows = reduce_mine(after(up_keep, edges), up_near, up_got[:, 0], up_across)
    down_up = swap(down_up, "col", 2)
    down_rows = reduce_along(after(down_keep, up_rows), down_near, down_across, down_up)
    result_got = after(swap(result_along, "col", 2), down_rows)
    result_near = jnp.concatenate([result_near, result_got[1:]], axis=0)
    result_pieces = result_keep, result_got, swap(result_near, "col", 1)
    first_rows = reduce_mine(after(first_keep, down_rows), first_near, by_leaf, by_col)
    dtok_keep, dtok_along, dtok_near = dtok
    dtok_got = after(swap(dtok_along, "col", 2), first_rows, result_near)
    dtok_near = jnp.concatenate([dtok_near, dtok_got[1:]], axis=0)
    layer_output = place(own_blocks, here, result_pieces, row_tokens)
    mem_sum = placed[:, row_tokens : row_tokens + bank].astype(F32)
    memory_grad = jnp.where(parity == 0, mem_sum, jnp.roll(mem_sum, half, axis=0)).T
    tokens_grad = finish_tokens(
        blocks, here, placed, (dtok_keep, dtok_got, swap(dtok_near, "col", 1)), row_tokens
    )
    down_got, up_got, first_got = send_rows(down_rows), send_rows(up_rows), send_rows(first_rows)
    down_rows, up_rows = after((down_rows, up_rows), first_rows)
    second_mine = jnp.concatenate([reduce_rows(down_rows, down_got), reduce_rows(up_rows, up_got)], axis=1)
    second_other = swap(second_mine, "leaf", 1)
    first_mine = reduce_rows(after(first_rows, second_mine, tokens_grad, memory_grad, layer_output), first_got)
    first_other = swap(first_mine, "leaf", 1)

    def in_order(mine, other):
        return jnp.where(
            parity == 0, jnp.concatenate([mine, other], axis=0), jnp.concatenate([other, mine], axis=0)
        ).astype(F32)

    second_total = in_order(second_mine, second_other)
    down_total, up_total = second_total[:, :hidden_width], second_total[:, hidden_width:]
    count = (2 * width + hidden_width) // half
    first_query, first_key, first_value, first_out, vectors = unpack(here, first_mine, first_other, width, count + 6)
    by_row = vectors[:count, :half].reshape(-1)
    by_col = vectors[count : count + 6]

    return (
        layer_output,
        tokens_grad,
        memory_grad,
        first_query,
        by_row[:width],
        first_key,
        first_value,
        by_row[width : 2 * width],
        first_out,
        by_col[0],
        by_col[1],
        by_col[2],
        up_total,
        by_row[2 * width :],
        down_total,
        by_col[3],
        by_col[4],
        by_col[5],
    )


def solution(mesh):
    return jax.shard_map(
        on_device,
        mesh=mesh,
        in_specs=(
            P("col", ("leaf", "row")),
            P("leaf", "col"),
            P("leaf"),
            P("leaf", None),
            P("col", "row"),
            P("row"),
            P("col", "row"),
            P("col", "row"),
            P("row"),
            P("row", "col"),
            P("col"),
            P("col"),
            P("col"),
            P("col", "row"),
            P("row"),
            P("col", "row"),
            P("col"),
            P("col"),
            P("col"),
            P("col", ("leaf", "row")),
        ),
        out_specs=(
            P("col", ("leaf", "row")),
            P("col", ("leaf", "row")),
            P("leaf", "col"),
            P("col", "row"),
            P("row"),
            P("col", "row"),
            P("col", "row"),
            P("row"),
            P("row", "col"),
            P("col"),
            P("col"),
            P("col"),
            P("col", "row"),
            P("row"),
            P("col", "row"),
            P("col"),
            P("col"),
            P("col"),
        ),
        check_vma=False,
    )
```

```python
import functools

import jax
import jax.numpy as jnp
import numpy as np
from jax import lax
from jax.experimental import pallas as pl
from jax.experimental.pallas import tpu as pltpu
from jax.sharding import PartitionSpec as P

HEAD = 64
SEG = 256
NEGATIVE = -1e30
EPSILON = 1e-05
EVERY = ("leaf", "row", "col")
BF16 = jnp.bfloat16
F32 = jnp.float32


def after(value, *others):
    return lax.optimization_barrier((value, others))[0]


def tn(left, right):
    return lax.dot_general(left, right, (((0,), (0,)), ((), ())), preferred_element_type=F32)


def nt(left, right):
    return lax.dot_general(left, right, (((1,), (1,)), ((), ())), preferred_element_type=F32)


def nn(left, right):
    return lax.dot_general(left, right, (((1,), (0,)), ((), ())), preferred_element_type=F32)


def plan_windows(own, count):
    segments, ranges = [], []
    for index in range(count):
        first, last = index * own, (index + 1) * own
        whole = [s for s in range(first // SEG, -(-last // SEG)) if s * SEG >= first and (s + 1) * SEG <= last]
        cut = [s for s in range(first // SEG, -(-last // SEG)) if s not in whole]
        pieces = [(s * SEG, SEG) for s in whole]
        for s in cut:
            low, high = max(first, s * SEG), min(last, (s + 1) * SEG)
            pieces.append((low, high - low))
            if low > s * SEG:
                pieces.append((s * SEG, low - s * SEG))
            if high < (s + 1) * SEG:
                pieces.append((high, (s + 1) * SEG - high))
        segments.append(whole + cut)
        ranges.append(pieces)
    return segments, ranges


def static_of(index, values):
    out = jnp.int32(values[0])
    for i, value in enumerate(values[1:], 1):
        out = jnp.where(index == i, jnp.int32(value), out)
    return out


def own_segments(segments, here_ref):
    return [
        here_ref[0] * here_ref[3] + static_of(here_ref[1], [lists[j] for lists in segments])
        for j in range(len(segments[0]))
    ]


def window_biases(segments, bank, here_ref, parents_ref, slots_ref):
    rows = lax.broadcasted_iota(jnp.int32, (bank, 1), 0)
    out = []
    for seg in own_segments(segments, here_ref):
        count = jnp.zeros((bank, 1), F32)
        for m in range(slots_ref.shape[1]):
            count = count + jnp.where(rows == slots_ref[seg, m], 1.0, 0.0)
        slot = jnp.where(count > 0, jnp.log(jnp.maximum(count, 1.0)), NEGATIVE)
        out.append((jnp.where(parents_ref[seg] >= 0, 0.0, NEGATIVE).astype(F32), slot))
    return out


def attention_own(
    head_count, lengths, segments, bank, here_ref, parents_ref, slots_ref, win_ref, mixed_ref, top_ref, total_ref
):
    width = head_count * HEAD
    window = len(lengths) * SEG
    biases = window_biases(segments, bank, here_ref, parents_ref, slots_ref)
    for head in range(head_count):
        low = head * HEAD
        key_mem = win_ref[0, width + low : width + low + HEAD, window : window + bank]
        value_mem = win_ref[0, 2 * width + low : 2 * width + low + HEAD, window : window + bank]
        for j, count in enumerate(lengths):
            cols = slice(j * SEG, (j + 1) * SEG)
            toks = slice(j * SEG, j * SEG + count)
            query = win_ref[0, low : low + HEAD, toks]
            own = tn(win_ref[0, width + low : width + low + HEAD, cols], query)
            mem = tn(key_mem, query) + biases[j][1]
            top = jnp.maximum(jnp.max(own, axis=0, keepdims=True), jnp.max(mem, axis=0, keepdims=True))
            own, mem = jnp.exp(own - top), jnp.exp(mem - top)
            mixed_ref[0, low : low + HEAD, toks] = nn(
                win_ref[0, 2 * width + low : 2 * width + low + HEAD, cols], own.astype(BF16)
            ) + nn(value_mem, mem.astype(BF16))
            top_ref[0, head : head + 1, toks] = top
            total_ref[0, head : head + 1, toks] = jnp.sum(own, axis=0, keepdims=True) + jnp.sum(
                mem, axis=0, keepdims=True
            )


def attention_parent(
    head_count,
    lengths,
    segments,
    here_ref,
    parents_ref,
    win_ref,
    mixed_ref,
    top_ref,
    total_ref,
    near_ref,
    far_ref,
    par_keep,
    par_got,
    par_last,
    bias_ref,
    par_ref,
    ctx_ref,
    lse_ref,
    toks_ref,
):
    width = head_count * HEAD
    depth = near_ref.shape[1]
    join_pieces((par_keep, par_got, par_last), toks_ref)
    both = tn(near_ref[0, :, width : 3 * width], toks_ref[:depth]) + tn(far_ref[0, :, width : 3 * width], toks_ref[depth:])
    par_ref[0] = (both + across_lanes(bias_ref[0], 1, width, 3 * width, both.shape[1])).astype(BF16)
    biases = [jnp.where(parents_ref[seg] >= 0, 0.0, NEGATIVE).astype(F32) for seg in own_segments(segments, here_ref)]
    for head in range(head_count):
        low = head * HEAD
        for j, count in enumerate(lengths):
            cols = slice(j * SEG, (j + 1) * SEG)
            toks = slice(j * SEG, j * SEG + count)
            par = tn(par_ref[0, low : low + HEAD, cols], win_ref[0, low : low + HEAD, toks]) + biases[j]
            first = top_ref[0, head : head + 1, toks]
            top = jnp.maximum(first, jnp.max(par, axis=0, keepdims=True))
            par = jnp.exp(par - top)
            scale = jnp.exp(first - top)
            total = total_ref[0, head : head + 1, toks] * scale + jnp.sum(par, axis=0, keepdims=True)
            mixed = mixed_ref[0, low : low + HEAD, toks] * scale
            mixed = mixed + nn(par_ref[0, width + low : width + low + HEAD, cols], par.astype(BF16))
            ctx_ref[0, low : low + HEAD, toks] = (mixed / total).astype(BF16)
            lse_ref[0, head : head + 1, toks] = top + jnp.log(total)


def attention_backward(
    head_count,
    lengths,
    segments,
    bank,
    here_ref,
    parents_ref,
    slots_ref,
    win_ref,
    par_ref,
    ctx_ref,
    dctx_ref,
    lse_ref,
    near_ref,
    far_ref,
    dwin_ref,
    dpar_ref,
    keep_ref,
    along_ref,
    close_ref,
    total_ref,
):
    width = head_count * HEAD
    biases = window_biases(segments, bank, here_ref, parents_ref, slots_ref)
    window = len(lengths) * SEG
    tail = win_ref.shape[2] - window
    for head in range(head_count):
        low = head * HEAD
        qs, ks, vs = (slice(part * width + low, part * width + low + HEAD) for part in range(3))
        key_mem = win_ref[0, ks, window : window + bank]
        value_mem = win_ref[0, vs, window : window + bank]
        dkey_mem = jnp.zeros((HEAD, bank), F32)
        dvalue_mem = jnp.zeros((HEAD, bank), F32)
        for j, count in enumerate(lengths):
            cols = slice(j * SEG, (j + 1) * SEG)
            tok = slice(j * SEG, j * SEG + count)
            query = win_ref[0, qs, tok]
            dctx = dctx_ref[0, low : low + HEAD, tok]
            lse = lse_ref[0, head : head + 1, tok]
            key_own, value_own = win_ref[0, ks, cols], win_ref[0, vs, cols]
            key_par, value_par = par_ref[0, low : low + HEAD, cols], par_ref[0, width + low : width + low + HEAD, cols]
            own = jnp.exp(tn(key_own, query) - lse)
            par = jnp.exp(tn(key_par, query) + biases[j][0] - lse)
            mem = jnp.exp(tn(key_mem, query) + biases[j][1] - lse)
            gown, gpar, gmem = tn(value_own, dctx), tn(value_par, dctx), tn(value_mem, dctx)
            ctx = ctx_ref[0, low : low + HEAD, tok].astype(F32)
            inner = jnp.sum(ctx * dctx.astype(F32), axis=0, keepdims=True)
            gown = (own * (gown - inner)).astype(BF16)
            gpar = (par * (gpar - inner)).astype(BF16)
            gmem = (mem * (gmem - inner)).astype(BF16)
            dquery = nn(key_own, gown) + nn(key_par, gpar) + nn(key_mem, gmem)
            dwin_ref[0, qs, tok] = (dquery * HEAD ** (-0.5)).astype(BF16)
            if count < SEG:
                dwin_ref[0, qs, j * SEG + count : (j + 1) * SEG] = jnp.zeros((HEAD, SEG - count), BF16)
            dwin_ref[0, ks, cols] = nt(query, gown).astype(BF16)
            dwin_ref[0, vs, cols] = nt(dctx, own.astype(BF16)).astype(BF16)
            dpar_ref[0, low : low + HEAD, cols] = nt(query, gpar).astype(BF16)
            dpar_ref[0, width + low : width + low + HEAD, cols] = nt(dctx, par.astype(BF16)).astype(BF16)
            dkey_mem += nt(query, gmem)
            dvalue_mem += nt(dctx, mem.astype(BF16))
        pad = jnp.zeros((HEAD, tail - bank), F32)
        dwin_ref[0, qs, window:] = jnp.zeros((HEAD, tail), BF16)
        dwin_ref[0, ks, window:] = jnp.concatenate([dkey_mem, pad], axis=1).astype(BF16)
        dwin_ref[0, vs, window:] = jnp.concatenate([dvalue_mem, pad], axis=1).astype(BF16)

    step, last = pl.program_id(0), pl.num_programs(0) - 1
    depth = near_ref.shape[1]
    grads = jnp.concatenate([dpar_ref[0], dwin_ref[0, width:, window:]], axis=1)
    near, far = nn(near_ref[0, :, width : 3 * width], grads), nn(far_ref[0, :, width : 3 * width], grads)

    @pl.when(step == 0)
    def begin():
        total_ref[:depth], total_ref[depth:] = near, far

    @pl.when(step > 0)
    def add():
        total_ref[:depth] += near
        total_ref[depth:] += far

    @pl.when(step == last)
    def finish():
        feat = keep_ref.shape[1]
        for i, out in enumerate((keep_ref.at[0], along_ref.at[0], close_ref.at[0], along_ref.at[1])):
            out[...] = total_ref[i * feat : (i + 1) * feat].astype(BF16)


def step_block(array):
    return pl.BlockSpec((1,) + array.shape[1:], lambda step, *_: (step, 0, 0))


def whole_block(array):
    return pl.BlockSpec(array.shape, lambda step, *_: (0,) * len(array.shape))


def cost(microseconds):
    return pl.CostEstimate(flops=int(microseconds * 1.0e9), bytes_accessed=0, transcendentals=0)


def held(*arrays):
    return tuple(pltpu.with_memory_space_constraint(array, pltpu.HBM) for array in arrays)


def in_hbm(shape):
    return pltpu.HBM(shape.shape, shape.dtype)


def params(mib):
    return pltpu.CompilerParams(vmem_limit_bytes=mib << 20)


def across_lanes(rows, index, low, high, columns):
    chosen = (lax.broadcasted_iota(jnp.int32, (rows.shape[0], 128), 0) == index).astype(BF16)
    column = tn(rows[:, low:high] if high - low < rows.shape[1] else rows, chosen)
    return jnp.concatenate([column] * (columns // 128), axis=1)


def join_pieces(refs, toks_ref):
    @pl.when(pl.program_id(0) == 0)
    def join():
        feat = refs[0].shape[1]
        for i, (piece, place) in enumerate(PIECES):
            toks_ref[i * feat : (i + 1) * feat] = refs[piece][place]


def project_kernel(low, high, scaled, near_ref, far_ref, *refs):
    depth = near_ref.shape[1]
    if len(refs) > 3:
        toks_ref, bias_ref, out_ref = refs[5], refs[3], refs[4]
        join_pieces(refs[:3], toks_ref)
    else:
        toks_ref, bias_ref, out_ref = refs
    out = tn(near_ref[0, :, low:high], toks_ref[:depth]) + tn(far_ref[0, :, low:high], toks_ref[depth:])
    out = (out + across_lanes(bias_ref[0], 1, low, high, out.shape[1])).astype(BF16)
    if scaled:
        out_ref[0, :scaled] = out[:scaled] * jnp.asarray(HEAD ** (-0.5), BF16)
        out_ref[0, scaled:] = out[scaled:]
    else:
        out_ref[0] = out


def project(near, far, toks, bias, low, high, scaled):
    groups, depth = near.shape[:2]
    pieces = toks if isinstance(toks, tuple) else (toks,)
    out = jax.ShapeDtypeStruct((groups, high - low, pieces[0].shape[-1]), BF16)
    return pl.pallas_call(
        functools.partial(project_kernel, low, high, scaled),
        grid=(groups,),
        in_specs=[step_block(near), step_block(far), *[whole_block(piece) for piece in pieces], step_block(bias)],
        scratch_shapes=[pltpu.VMEM((2 * depth, pieces[0].shape[-1]), BF16)] if len(pieces) > 1 else [],
        out_specs=step_block(out),
        out_shape=out,
        compiler_params=params(12),
        cost_estimate=cost(0.1),
        name="project",
    )(near, far, *pieces, bias)


def chunks(columns):
    return columns // 128


def mlp_kernel(
    at,
    ctx_ref,
    win_ref,
    cot_keep,
    cot_got,
    cot_last,
    near_first,
    far_first,
    near_ref,
    far_ref,
    bias_ref,
    keep_ref,
    along_ref,
    close_ref,
    active_ref,
    upper_ref,
    hidden_ref,
    low_ref,
    first_low_ref,
    dctx_ref,
    up_sum_ref,
    sums_ref,
    total_ref,
    wide_ref,
    parts_ref,
    normed_ref,
    scale_ref,
    slope_ref,
    columns_ref,
    out_ref,
    weights_ref,
    sem,
):
    step, groups = pl.program_id(0), slope_ref.shape[0]
    depth, width = near_ref.shape[2:]
    model, own = total_ref.shape
    feat = keep_ref.shape[1]
    heads = ctx_ref.shape[1]
    skip = out_ref.shape[3] - heads

    def weight_copies(block):
        return [
            pltpu.make_async_copy(
                source.at[which, block], weights_ref.at[which, side, block], sem.at[2 + 4 * block + 2 * which + side]
            )
            for which in range(2)
            for side, source in enumerate((near_ref, far_ref))
        ]

    first_copies = [
        pltpu.make_async_copy(
            source.at[:, :, pl.ds(width - out_ref.shape[3], out_ref.shape[3])], out_ref.at[side], sem.at[side]
        )
        for side, source in enumerate((near_first, far_first))
    ]

    def over_columns(body):
        def run(i, carry):
            body(pl.ds(pl.multiple_of(i * 128, 128), 128))
            return carry

        lax.fori_loop(0, own // 128, run, 0)

    def sum_parts(first):
        for i in range(3):
            sums_ref[:, first + i : first + i + 1] = jnp.sum(parts_ref[i], axis=1, keepdims=True)
        parts_ref[...] = jnp.zeros(parts_ref.shape, F32)

    @pl.when(step == 0)
    def start():
        for copy in first_copies:
            copy.start()
        for block in range(groups):
            for copy in weight_copies(block):
                copy.start()
        for i in range(6):
            columns_ref[i] = jnp.broadcast_to(win_ref[:, at + i : at + i + 1].astype(F32), (model, 128))
        parts_ref[...] = jnp.zeros(parts_ref.shape, F32)
        for copy in first_copies:
            copy.wait()
        for n in range(groups):
            near, far = nn(out_ref[0, n, :, skip:], ctx_ref[n]), nn(out_ref[1, n, :, skip:], ctx_ref[n])
            if n == 0:
                total_ref[:depth], total_ref[depth:] = near, far
            else:
                total_ref[:depth] += near
                total_ref[depth:] += far

        def body(cols):
            values = total_ref[:, cols] + columns_ref[0] + win_ref[:, cols].astype(F32)
            center, scale = norm_stats(values)
            normed = (values - center) * scale
            hidden = normed * columns_ref[1] + columns_ref[2]
            normed_ref[:, cols] = normed
            scale_ref[:, cols] = scale
            wide_ref[:, cols] = hidden
            hidden_ref[:, cols] = hidden.astype(BF16)

        over_columns(body)
        total_ref[...] = jnp.zeros(total_ref.shape, F32)

    @pl.when(step < groups)
    def forward():
        for block in range(groups):

            @pl.when(step == block)
            def arrive(block=block):
                for copy in weight_copies(block):
                    copy.wait()

        piece = width // 3
        for low in range(0, width, piece):
            rows = slice(low, low + piece)
            upper = tn(weights_ref[0, 0, step, :, rows], hidden_ref[:depth])
            upper = upper + tn(weights_ref[0, 1, step, :, rows], hidden_ref[depth:])
            upper = upper + across_lanes(bias_ref[0], 0, low, low + piece, own)
            phi = 0.5 * (1.0 + lax.erf(upper * np.float32(0.5**0.5)))
            active_ref[0, rows] = (upper * phi).astype(BF16)
            slope_ref[step, rows] = (
                phi + upper * jnp.exp(-0.5 * upper * upper) * np.float32(1.0 / np.sqrt(2.0 * np.pi))
            ).astype(BF16)
        active = active_ref[0]
        total_ref[:depth] += nn(weights_ref[1, 0, step], active)
        total_ref[depth:] += nn(weights_ref[1, 1, step], active)

    @pl.when(step == groups - 1)
    def turn():
        pieces = (cot_keep, cot_got, cot_last)

        def body(cols):
            values = total_ref[:, cols] + columns_ref[3] + wide_ref[:, cols]
            center, scale = norm_stats(values)
            normed = (values - center) * scale
            result = (normed * columns_ref[4] + columns_ref[5]).astype(BF16)
            keep_ref[0, :, cols] = result[:feat]
            along_ref[0, :, cols] = result[feat : 2 * feat]
            close_ref[0, :, cols] = result[2 * feat : 3 * feat]
            along_ref[1, :, cols] = result[3 * feat :]
            cot = jnp.concatenate([pieces[i][j, :, cols] for i, j in PIECES], axis=0).astype(F32)
            grad = norm_back(cot, normed, scale, columns_ref[4])
            total_ref[:, cols] = grad
            grad_low = grad.astype(BF16)
            low_ref[:, cols] = grad_low
            parts_ref[0] += grad_low.astype(F32)
            parts_ref[1] += cot * normed
            parts_ref[2] += cot

        over_columns(body)
        sum_parts(3)

    @pl.when(step >= groups)
    def backward():
        block = step - groups
        upper = tn(weights_ref[1, 0, block], low_ref[:depth]) + tn(weights_ref[1, 1, block], low_ref[depth:])
        upper = (upper * slope_ref[block].astype(F32)).astype(BF16)
        upper_ref[0] = upper
        up_sum_ref[0] = jnp.sum(upper.astype(F32), axis=1, keepdims=True)
        total_ref[:depth] += nn(weights_ref[0, 0, block], upper)
        total_ref[depth:] += nn(weights_ref[0, 1, block], upper)

    @pl.when(step == 2 * groups - 1)
    def finish():
        def body(cols):
            hidden_grad = total_ref[:, cols]
            normed = normed_ref[:, cols]
            first_low = norm_back(hidden_grad, normed, scale_ref[:, cols], columns_ref[1]).astype(BF16)
            first_low_ref[:, cols] = first_low
            parts_ref[0] += first_low.astype(F32)
            parts_ref[1] += hidden_grad * normed
            parts_ref[2] += hidden_grad

        over_columns(body)
        sum_parts(0)
        for n in range(groups):
            grads = tn(out_ref[0, n, :, skip:], first_low_ref[:depth]) + tn(out_ref[1, n, :, skip:], first_low_ref[depth:])
            dctx_ref[n] = grads.astype(BF16)


def once(array):
    return pl.BlockSpec(
        array.shape, lambda step, *_: (0,) * len(array.shape), pipeline_mode=pl.Buffered(1)
    )


def mlp(at, ctx, win, cot, near_first, far_first, near, far, bias):
    groups, depth, width = near.shape[1:]
    feat, own = cot[0].shape[1:]
    model = feat * 4
    out_columns = -(-ctx.shape[1] // 128) * 128

    def early(array):
        return pl.BlockSpec((1,) + array.shape[1:], lambda step, *_: (jnp.minimum(step, groups - 1), 0, 0))

    def late(array):
        return pl.BlockSpec((1,) + array.shape[1:], lambda step, *_: (jnp.maximum(step - groups, 0), 0, 0))

    outs = [
        jax.ShapeDtypeStruct((1, feat, own), BF16),
        jax.ShapeDtypeStruct((2, feat, own), BF16),
        jax.ShapeDtypeStruct((1, feat, own), BF16),
        jax.ShapeDtypeStruct((groups, width, own), BF16),
        jax.ShapeDtypeStruct((groups, width, own), BF16),
        jax.ShapeDtypeStruct((model, own), BF16),
        jax.ShapeDtypeStruct((model, own), BF16),
        jax.ShapeDtypeStruct((model, own), BF16),
        jax.ShapeDtypeStruct(ctx.shape, BF16),
        jax.ShapeDtypeStruct((groups, width, 1), F32),
        jax.ShapeDtypeStruct((model, 6), F32),
    ]
    return pl.pallas_call(
        functools.partial(mlp_kernel, at),
        grid=(2 * groups,),
        in_specs=[
            once(ctx),
            once(win),
            *[once(piece) for piece in cot],
            HBM,
            HBM,
            HBM,
            HBM,
            pl.BlockSpec((1,) + bias.shape[1:], lambda step, *_: (jnp.minimum(step, groups - 1), 0, 0)),
        ],
        out_specs=[early(o) if i == 3 else late(o) if i in (4, 9) else once(o) for i, o in enumerate(outs)],
        out_shape=[in_hbm(o) if i in (3, 4, 5, 6, 7) else o for i, o in enumerate(outs)],
        scratch_shapes=[
            pltpu.VMEM((model, own), F32),
            pltpu.VMEM((model, own), F32),
            pltpu.VMEM((3, model, 128), F32),
            pltpu.VMEM((model, own), F32),
            pltpu.VMEM((1, own), F32),
            pltpu.VMEM((groups, width, own), BF16),
            pltpu.VMEM((6, model, 128), F32),
            pltpu.VMEM((2, groups, depth, out_columns), BF16),
            pltpu.VMEM((2, 2, groups, depth, width), BF16),
            pltpu.SemaphoreType.DMA((2 + 4 * groups,)),
        ],
        compiler_params=params(44),
        cost_estimate=cost(400),
        name="mlp",
    )(ctx, win, *cot, near_first, far_first, near, far, bias)


def hidden_grad_kernel(low_ref, hidden_ref, active_ref, upper_ref, down_keep, down_send, up_keep, up_send):
    depth = down_keep.shape[1]
    for keep, send, left, right in (
        (down_keep, down_send, low_ref, active_ref),
        (up_keep, up_send, hidden_ref, upper_ref),
    ):
        keep[0] = nt(left[:depth], right[0]).astype(BF16)
        send[0] = nt(left[depth:], right[0]).astype(BF16)


def hidden_grads(low, hidden, active, upper):
    groups, width, own = active.shape
    out = jax.ShapeDtypeStruct((groups, low.shape[0] // 2, width), BF16)
    return pl.pallas_call(
        hidden_grad_kernel,
        grid=(groups,),
        in_specs=[whole_block(low), whole_block(hidden), step_block(active), step_block(upper)],
        out_specs=[step_block(out)] * 4,
        out_shape=[in_hbm(out)] * 4,
        compiler_params=params(14),
        cost_estimate=cost(100),
        name="hidden_grads",
    )(*held(low, hidden, active, upper))


def first_grad_kernel(
    width,
    win_ref,
    par_keep,
    par_got,
    par_last,
    dwin_ref,
    dpar_ref,
    low_ref,
    ctx_ref,
    up_ref,
    sums_ref,
    keep_ref,
    send_ref,
    par_ref,
):
    join_pieces((par_keep, par_got, par_last), par_ref)
    depth = keep_ref.shape[1]
    half = depth // 4
    query = jnp.sum(dwin_ref[0, :width].astype(F32), axis=1, keepdims=True)
    value = jnp.sum(dwin_ref[0, 2 * width :].astype(F32), axis=1, keepdims=True)
    value = value + jnp.sum(dpar_ref[0, width:].astype(F32), axis=1, keepdims=True)
    by_row = [array[i : i + half] for array in (query, value, up_ref[0]) for i in range(0, array.shape[0], half)]
    by_row = jnp.concatenate(by_row, axis=1)
    by_row = jnp.concatenate([by_row] * 4, axis=0)
    used = by_row.shape[1] + 6
    pad = jnp.zeros((depth, keep_ref.shape[2] - 4 * width - used), F32)
    for part, out_ref in enumerate((keep_ref, send_ref)):
        rows = slice(part * depth, (part + 1) * depth)
        win, par = win_ref[rows], par_ref[rows]
        out_ref[0, :, :width] = nt(win, dwin_ref[0, :width]).astype(BF16)
        for i in range(1, 3):
            grads = nt(win, dwin_ref[0, i * width : (i + 1) * width])
            grads = grads + nt(par, dpar_ref[0, (i - 1) * width : i * width])
            out_ref[0, :, i * width : (i + 1) * width] = grads.astype(BF16)
        out_ref[0, :, 3 * width : 4 * width] = nt(low_ref[rows], ctx_ref[0]).astype(BF16)
        extra = jnp.concatenate([by_row, sums_ref[rows], pad], axis=1)
        out_ref[0, :, 4 * width :] = extra.astype(BF16)


def first_grads(win, par, dwin, dpar, low, ctx, up_bias, sums):
    groups, width, own = ctx.shape
    out = jax.ShapeDtypeStruct((groups, low.shape[0] // 2, 4 * width + 128), BF16)
    return pl.pallas_call(
        functools.partial(first_grad_kernel, width),
        grid=(groups,),
        in_specs=[
            whole_block(win),
            *[whole_block(piece) for piece in par],
            step_block(dwin),
            step_block(dpar),
            whole_block(low),
            step_block(ctx),
            step_block(up_bias),
            whole_block(sums),
        ],
        out_specs=[step_block(out)] * 2,
        out_shape=[out] * 2,
        scratch_shapes=[pltpu.VMEM((low.shape[0], par[0].shape[2]), BF16)],
        compiler_params=params(16),
        cost_estimate=cost(15),
        name="first_grads",
    )(*held(win, *par, dwin, dpar, low, ctx), up_bias, sums)


def token_grad_kernel(high, near_ref, far_ref, dwin_ref, more_ref, keep_ref, along_ref, close_ref, total_ref):
    step, last = pl.program_id(0), pl.num_programs(0) - 1
    depth = near_ref.shape[1]
    own = more_ref.shape[1]

    @pl.when(step == 0)
    def start():
        total_ref[...] = jnp.zeros(total_ref.shape, F32)
        total_ref[:, :own] = more_ref[...].astype(F32)

    grads = dwin_ref[0]
    total_ref[:depth] += nn(near_ref[0, :, :high], grads)
    total_ref[depth:] += nn(far_ref[0, :, :high], grads)

    @pl.when(step == last)
    def finish():
        feat = keep_ref.shape[1]
        for i, out in enumerate((keep_ref.at[0], along_ref.at[0], close_ref.at[0], along_ref.at[1])):
            out[...] = total_ref[i * feat : (i + 1) * feat].astype(BF16)


def token_grads(near, far, dwin, more, columns):
    groups, depth = near.shape[:2]
    feat = depth // 2
    outs = [jax.ShapeDtypeStruct((n, feat, columns), BF16) for n in (1, 2, 1)]
    return pl.pallas_call(
        functools.partial(token_grad_kernel, dwin.shape[1]),
        grid=(groups,),
        in_specs=[
            step_block(near),
            step_block(far),
            pl.BlockSpec((1, dwin.shape[1], columns), lambda step: (step, 0, 0)),
            whole_block(more),
        ],
        out_specs=[whole_block(out) for out in outs],
        out_shape=outs,
        scratch_shapes=[pltpu.VMEM((2 * depth, columns), F32)],
        compiler_params=params(14),
        cost_estimate=cost(30),
        name="token_grads",
    )(near, far, dwin, more)


def attend_own(lengths, segments, bank, scalars, window):
    groups, rows, columns = window.shape
    width = rows // 3
    own = sum(lengths)
    outs = (
        jax.ShapeDtypeStruct((groups, width, own), F32),
        jax.ShapeDtypeStruct((groups, width // HEAD, own), F32),
        jax.ShapeDtypeStruct((groups, width // HEAD, own), F32),
    )
    return pl.pallas_call(
        functools.partial(attention_own, width // HEAD, lengths, segments, bank),
        grid=(groups,),
        in_specs=[SMEM] * 3 + [step_block(window)],
        out_specs=[step_block(out) for out in outs],
        out_shape=outs,
        compiler_params=params(14),
        cost_estimate=cost(0.1),
        name="attention_own",
    )(*scalars, window)


def attend_parent(lengths, segments, scalars, window, partial, near, far, toks, bias):
    groups, rows, columns = window.shape
    width = rows // 3
    depth = near.shape[1]
    outs = (
        jax.ShapeDtypeStruct((groups, 2 * width, toks[0].shape[2]), BF16),
        jax.ShapeDtypeStruct((groups, width, sum(lengths)), BF16),
        jax.ShapeDtypeStruct((groups, width // HEAD, sum(lengths)), F32),
    )
    return pl.pallas_call(
        functools.partial(attention_parent, width // HEAD, lengths, segments),
        grid=(groups,),
        in_specs=[SMEM] * 2
        + [step_block(array) for array in (window, *partial, near, far)]
        + [whole_block(piece) for piece in toks]
        + [step_block(bias)],
        out_specs=[step_block(out) for out in outs],
        out_shape=[in_hbm(outs[0]), *outs[1:]],
        scratch_shapes=[pltpu.VMEM((2 * depth, toks[0].shape[2]), BF16)],
        compiler_params=params(18),
        cost_estimate=cost(130),
        name="attention_parent",
    )(*scalars[:2], window, *partial, *held(near, far), *toks, bias)


def attend_back(lengths, segments, bank, scalars, window, parent, ctx, dctx, lse, near, far):
    groups, rows, columns = window.shape
    depth = near.shape[1]
    feat = depth // 2
    outs = (jax.ShapeDtypeStruct(window.shape, BF16), jax.ShapeDtypeStruct(parent.shape, BF16))
    sends = [jax.ShapeDtypeStruct((n, feat, columns), BF16) for n in (1, 2, 1)]
    return pl.pallas_call(
        functools.partial(attention_backward, rows // 3 // HEAD, lengths, segments, bank),
        grid=(groups,),
        in_specs=[SMEM] * 3 + [step_block(array) for array in (window, parent, ctx, dctx, lse, near, far)],
        out_specs=[step_block(out) for out in outs] + [whole_block(out) for out in sends],
        out_shape=[*map(in_hbm, outs), *sends],
        scratch_shapes=[pltpu.VMEM((2 * depth, columns), F32)],
        compiler_params=params(24),
        cost_estimate=cost(200),
        name="attention_backward",
    )(*scalars, *held(window, parent, ctx), dctx, lse, *held(near, far))


def swap(array, axis, mask):
    count = lax.axis_size(axis)
    return lax.ppermute(array, axis, [(i, i ^ mask) for i in range(count)])


SMEM = pl.BlockSpec(memory_space=pltpu.SMEM)
VMEM = pl.BlockSpec(memory_space=pltpu.VMEM)
HBM = pl.BlockSpec(memory_space=pltpu.HBM)
ORDER = (0, 2, 1, 3)
SENDS = ((0, 0), (1, 0), (2, 0), (1, 1))


def at_distance(here_ref, lists, slot, j):
    distance = ORDER[slot]
    return static_of(here_ref[1], [lists[i ^ distance][j] for i in range(len(lists))])


def flipped(here_ref, part, half):
    return pl.multiple_of((part ^ here_ref[2]) * half, 32)


def spots(rows, columns, shift):
    return (
        lax.broadcasted_iota(jnp.int32, (rows, columns), 0) + shift
        == lax.broadcasted_iota(jnp.int32, (rows, columns), 1)
    ).astype(BF16)


def as_row(ref):
    return ref[...].astype(F32).reshape(1, ref.shape[0])


def fetch(pairs, sem):
    copies = [pltpu.make_async_copy(source, target, sem.at[i]) for i, (source, target) in enumerate(pairs)]
    for copy in copies:
        copy.start()
    for copy in copies:
        copy.wait()


def pack_weights_kernel(here_ref, *refs):
    count = 9
    inputs, half_ref = refs[:count], refs[count]
    held, turned_ref, sem = refs[count + 1 : -2], refs[-2], refs[-1]
    feat, width = inputs[0].shape
    half = feat // 2
    rows = pl.ds(flipped(here_ref, 0, half), half)
    small = [inputs[i] for i in (0, 1, 2, 3, 6, 7, 8)]
    fetch(
        [*zip(small, held)]
        + [(inputs[4 + i].at[rows, :], half_ref.at[pl.ds((1 + i) * half, half), :]) for i in range(2)],
        sem,
    )
    query_ref, key_ref, value_ref, out_ref, up_b_ref, query_b_ref, value_b_ref = held
    turned_ref[...] = tn(out_ref[...], spots(width, width, 0)).astype(BF16)
    for i, ref in enumerate((query_ref, key_ref, value_ref, turned_ref)):
        half_ref[:half, i * width : (i + 1) * width] = ref[rows, :]
    zero = jnp.zeros((1, width), F32)
    joint = [as_row(query_b_ref), zero, as_row(value_b_ref), zero]
    wide = (half_ref.shape[0] - 3 * half, half_ref.shape[1])
    index = lax.broadcasted_iota(jnp.int32, wide, 0)
    up_row = jnp.broadcast_to(as_row(up_b_ref), wide)
    joint_row = jnp.broadcast_to(jnp.concatenate(joint, axis=1), wide)
    half_ref[3 * half :] = jnp.where(index == 0, up_row, jnp.where(index == 1, joint_row, 0.0)).astype(BF16)


def pack_weights(here, query, key, value, out, up, down, *biases):
    feat, width = query.shape
    hidden = up.shape[1]
    inputs = (query, key, value, out, up, down, *biases)
    small = [query, key, value, out, *biases]
    return pl.pallas_call(
        pack_weights_kernel,
        in_specs=[SMEM] + [HBM] * len(inputs),
        out_specs=VMEM,
        out_shape=jax.ShapeDtypeStruct((3 * feat // 2 + 16, hidden), BF16),
        scratch_shapes=[pltpu.VMEM(array.shape, array.dtype) for array in small]
        + [pltpu.VMEM((feat, width), BF16), pltpu.SemaphoreType.DMA((len(inputs),))],
        compiler_params=params(6),
        cost_estimate=cost(0.1),
        name="pack_weights",
    )(here, *held(*inputs))


def pack_kernel(blocks, sided, here_ref, *refs):
    given = 1 + sided
    outs, held, sem = refs[given : given + 3], refs[given + 3 : given + 3 + given], refs[-1]
    fetch([*zip(refs[:given], held)], sem)
    source_ref = held[0]
    half = source_ref.shape[0] // 2
    count = len(blocks[0])
    if sided:
        mem_ref, vector_refs, side_ref = held[1], held[2:], refs[-2]
        bank = mem_ref.shape[0]
        vectors = jnp.concatenate([as_row(ref) for ref in vector_refs], axis=0)
        vectors = jnp.concatenate([vectors, jnp.zeros((8 - len(vector_refs), vectors.shape[1]), F32)], axis=0)
        side = tn(mem_ref[...], spots(bank, 128, 0)) + tn(vectors.astype(BF16), spots(8, 128, bank))
        side_ref[...] = side.astype(BF16)
    for slot, (out, place) in enumerate(SENDS):
        for part in range(2):
            low = flipped(here_ref, part, half)
            rows = slice(part * half, (part + 1) * half)
            for j in range(count):
                at = pl.multiple_of(at_distance(here_ref, blocks, slot, j) * 128, 128)
                outs[out][place, rows, j * 128 : (j + 1) * 128] = source_ref[pl.ds(low, half), pl.ds(at, 128)]
            if sided:
                outs[out][place, rows, count * 128 :] = side_ref[pl.ds(low, half), :]


def pack(blocks, here, source, *side):
    feat = source.shape[0]
    columns = len(blocks[0]) * 128 + (128 if side else 0)
    inputs = (source, *side)
    return pl.pallas_call(
        functools.partial(pack_kernel, blocks, len(side)),
        in_specs=[SMEM] + [HBM] * len(inputs),
        out_specs=[VMEM] * 3,
        out_shape=[jax.ShapeDtypeStruct((n, feat, columns), source.dtype) for n in (1, 2, 1)],
        scratch_shapes=[pltpu.VMEM(array.shape, array.dtype) for array in inputs]
        + ([pltpu.VMEM((feat, 128), BF16)] if side else [])
        + [pltpu.SemaphoreType.DMA((len(inputs),))],
        compiler_params=params(12),
        cost_estimate=cost(0.1),
        name="pack",
    )(here, *held(*inputs))


def exchange(keep, along, near):
    got = swap(along, "col", 2)
    return keep, got, swap(jnp.concatenate([near, got[1:]], axis=0), "col", 1)


def joined(pieces):
    keep, got, last = pieces
    return jnp.concatenate([keep, got[:1], last], axis=0)


PIECES = ((0, 0), (1, 0), (2, 0), (2, 1))


def parent_of(here_ref, parents_ref, segments, slot, j):
    return parents_ref[here_ref[0] * here_ref[3] + at_distance(here_ref, segments, slot, j)]


def pick_kernel(segments, here_ref, parents_ref, source_ref, *refs):
    outs, sem = refs[:3], refs[3]
    half = source_ref.shape[1] // 2
    seg_row = here_ref[3]
    pairs = []
    for slot, (out, place) in enumerate(SENDS):
        for j in range(len(segments[0])):
            seg = jnp.maximum(parent_of(here_ref, parents_ref, segments, slot, j), 0)
            row = lax.div(seg, seg_row)
            at = pl.multiple_of((seg - row * seg_row) * SEG, SEG)
            for part in range(2):
                rows = slice(part * half, (part + 1) * half)
                source = source_ref.at[row, pl.ds(flipped(here_ref, part, half), half), pl.ds(at, SEG)]
                pairs.append((source, outs[out].at[place, rows, pl.ds(j * SEG, SEG)]))
    fetch(pairs, sem)


def pick_parents(segments, here, parents, gathered):
    feat = gathered.shape[1]
    columns = len(segments[0]) * SEG
    return pl.pallas_call(
        functools.partial(pick_kernel, segments),
        in_specs=[SMEM, SMEM, HBM],
        out_specs=[VMEM] * 3,
        out_shape=[jax.ShapeDtypeStruct((n, feat, columns), gathered.dtype) for n in (1, 2, 1)],
        scratch_shapes=[pltpu.SemaphoreType.DMA((8 * len(segments[0]),))],
        compiler_params=params(8),
        cost_estimate=cost(1),
        name="pick_parents",
    )(here, parents, *held(gathered))


def add_parents_kernel(segments, seg_row, here_ref, parents_ref, *refs):
    pieces, given_ref, sum_ref, out_ref, sem = refs[:3], refs[3], refs[4], refs[5], refs[6]
    window = len(segments[0]) * SEG
    copies = []
    sum_ref[...] = jnp.zeros(sum_ref.shape, F32)
    for slot, (piece, place) in enumerate(PIECES):
        for j in range(len(segments[0])):
            seg = parent_of(here_ref, parents_ref, segments, slot, j)

            @pl.when(seg >= 0)
            def add(seg=seg, piece=piece, place=place, cols=slice(j * SEG, (j + 1) * SEG)):
                sum_ref[seg] += pieces[piece][place, :, cols].astype(F32)

    mem = sum(pieces[piece][place, :, window:].astype(F32) for piece, place in PIECES)
    for r in range(out_ref.shape[0]):
        for s in range(seg_row):
            out_ref[r, :, s * SEG : (s + 1) * SEG] = sum_ref[r * seg_row + s].astype(BF16)
        out_ref[r, :, seg_row * SEG :] = mem.astype(BF16)
        copies.append(pltpu.make_async_copy(out_ref.at[r], given_ref.at[r], sem.at[r]))
        copies[-1].start()
    for copy in copies:
        copy.wait()


def add_parents(segments, here, parents, pieces, rows, seg_row):
    feat, columns = pieces[0].shape[1:]
    bank = columns - len(segments[0]) * SEG
    return pl.pallas_call(
        functools.partial(add_parents_kernel, segments, seg_row),
        in_specs=[SMEM, SMEM, VMEM, VMEM, VMEM],
        out_specs=HBM,
        out_shape=pltpu.HBM((rows, feat, seg_row * SEG + bank), BF16),
        scratch_shapes=[
            pltpu.VMEM((rows * seg_row, feat, SEG), F32),
            pltpu.VMEM((rows, feat, seg_row * SEG + bank), BF16),
            pltpu.SemaphoreType.DMA((rows,)),
        ],
        compiler_params=params(28),
        cost_estimate=cost(60),
        name="add_parents",
    )(here, parents, *pieces)


def finish_kernel(blocks, here_ref, placed_ref, *refs):
    pieces, out_ref = refs[:3], refs[3]
    half = out_ref.shape[0] // 2
    for part in range(2):
        low = flipped(here_ref, part, half)
        rows = slice(part * half, (part + 1) * half)
        out_ref[pl.ds(low, half), :] = placed_ref[rows, : out_ref.shape[1]].astype(F32)
        for slot, (piece, place) in enumerate(PIECES):
            for j in range(len(blocks[0])):
                at = pl.multiple_of(at_distance(here_ref, blocks, slot, j) * 128, 128)
                out_ref[pl.ds(low, half), pl.ds(at, 128)] += pieces[piece][
                    place, rows, j * 128 : (j + 1) * 128
                ].astype(F32)


def finish_tokens(blocks, here, placed, pieces, columns):
    return pl.pallas_call(
        functools.partial(finish_kernel, blocks),
        in_specs=[SMEM, VMEM, VMEM, VMEM, VMEM],
        out_specs=VMEM,
        out_shape=jax.ShapeDtypeStruct((placed.shape[0], columns), F32),
        compiler_params=params(10),
        cost_estimate=cost(2.5),
        name="finish_tokens",
    )(here, placed, *pieces)


def place_kernel(blocks, here_ref, *refs):
    pieces, out_ref = refs[:3], refs[3]
    half = out_ref.shape[0] // 2
    for part in range(2):
        low = flipped(here_ref, part, half)
        rows = slice(part * half, (part + 1) * half)
        for slot, (piece, place) in enumerate(PIECES):
            for j in range(pieces[0].shape[2] // 128):
                at = pl.multiple_of(at_distance(here_ref, blocks, slot, j) * 128, 128)
                out_ref[pl.ds(low, half), pl.ds(at, 128)] = pieces[piece][place, rows, j * 128 : (j + 1) * 128]


def place(blocks, here, pieces, columns):
    return pl.pallas_call(
        functools.partial(place_kernel, blocks),
        in_specs=[SMEM, VMEM, VMEM, VMEM],
        out_specs=VMEM,
        out_shape=jax.ShapeDtypeStruct((pieces[0].shape[1], columns), pieces[0].dtype),
        compiler_params=params(6),
        cost_estimate=cost(1.7),
        name="place",
    )(here, *pieces)


def unpack_kernel(width, count, here_ref, mine_ref, other_ref, query_ref, key_ref, value_ref, out_ref, more_ref, all_ref):
    half = mine_ref.shape[0]
    all_ref[pl.ds(flipped(here_ref, 0, half), half), :] = mine_ref[...].astype(F32)
    all_ref[pl.ds(flipped(here_ref, 1, half), half), :] = other_ref[...].astype(F32)
    for i, ref in enumerate((query_ref, key_ref, value_ref)):
        ref[...] = all_ref[:, i * width : (i + 1) * width]
    out_ref[...] = all_ref[:, 3 * width : 4 * width].T
    rows = all_ref[:, 4 * width :].T
    more_ref[...] = rows[: more_ref.shape[0]]


def unpack(here, mine, other, width, count):
    feat = 2 * mine.shape[0]
    square = jax.ShapeDtypeStruct((feat, width), F32)
    return pl.pallas_call(
        functools.partial(unpack_kernel, width, count),
        in_specs=[SMEM, VMEM, VMEM],
        out_specs=[VMEM] * 5,
        out_shape=[square] * 3 + [jax.ShapeDtypeStruct((width, feat), F32), jax.ShapeDtypeStruct((24, feat), F32)],
        scratch_shapes=[pltpu.VMEM((feat, mine.shape[1]), F32)],
        compiler_params=params(4),
        cost_estimate=cost(2),
        name="unpack",
    )(here, mine, other)


def gather_weights(half):
    return [half] + [swap(half, "row", n) for n in range(1, lax.axis_size("row"))]


def spread_weights(along, *gate):
    along = jnp.stack(along, axis=1)
    opposite = swap(along, "leaf", 1)
    across = after(swap(along, "col", 2), *gate)
    return along, opposite, across, swap(across, "leaf", 1)


def whole_weights(parts):
    near = jnp.stack(parts, axis=2)
    arrays, rows, blocks, depth, columns = near.shape
    near = near.reshape(arrays, rows, blocks * depth, columns)
    return near, swap(near, "col", 1)


def add_up(*terms):
    total = terms[0].astype(F32)
    for term in terms[1:]:
        total = total + term.astype(F32)
    return total


def reduce_blocks(keep):
    rows, features, columns = keep.shape
    return rows, 2, 2, features // 4, columns


def reduce_across(keep, near):
    shape = reduce_blocks(keep)
    return add_up(keep.reshape(shape)[:, :, 1], near.reshape(shape)[:, :, 1]).astype(BF16)


def reduce_y(keep, near):
    shape = reduce_blocks(keep)
    return add_up(keep.reshape(shape)[:, 1], near.reshape(shape)[:, 1]).astype(BF16)


def reduce_x(keep, near, got):
    shape = reduce_blocks(keep)
    return add_up(keep.reshape(shape)[:, 0, 1], near.reshape(shape)[:, 0, 1], got[:, 1]).astype(BF16)


def reduce_up(keep, near, across):
    shape = reduce_blocks(keep)
    return add_up(keep.reshape(shape)[:, 1, 0], near.reshape(shape)[:, 1, 0], across[:, 1]).astype(BF16)


def reduce_along(keep, near, across, up):
    shape = reduce_blocks(keep)
    mine = add_up(keep.reshape(shape)[:, 0, 0], near.reshape(shape)[:, 0, 0], across[:, 0], up)
    return [mine[n].astype(BF16) for n in range(shape[0])]


def reduce_rows(along, got):
    total = add_up(along[0], *got)
    mask = 2
    while mask < lax.axis_size("leaf"):
        total = add_up(total, swap(total.astype(BF16), "leaf", mask))
        mask *= 2
    return total.astype(BF16)


def reduce_corner(keep, near):
    shape = reduce_blocks(keep)
    middle = shape[0] // 2
    corner = add_up(keep.reshape(shape)[:, 1, 1], near.reshape(shape)[:, 1, 1]).astype(BF16)
    return corner[:middle], corner[middle:]


def reduce_edges(keep, near, by_leaf, by_col):
    shape = reduce_blocks(keep)
    middle = shape[0] // 2
    keep, near = keep.reshape(shape), near.reshape(shape)
    leaf = add_up(keep[:, 0, 1], near[:, 0, 1])
    leaf = jnp.concatenate([leaf[:middle], add_up(leaf[middle:], by_col)], axis=0).astype(BF16)
    along = add_up(keep[:, 1, 0], near[:, 1, 0])
    along = jnp.concatenate([add_up(along[:middle], by_leaf), along[middle:]], axis=0).astype(BF16)
    return leaf, along


def reduce_mine(keep, near, leaf, along):
    shape = reduce_blocks(keep)
    mine = add_up(keep.reshape(shape)[:, 0, 0], near.reshape(shape)[:, 0, 0], leaf, along)
    return [mine[n].astype(BF16) for n in range(shape[0])]


def send_rows(along):
    return [swap(block, "row", n) for n, block in enumerate(along) if n]


def norm_stats(values):
    center = jnp.mean(values, axis=0, keepdims=True)
    spread = jnp.mean(values * values, axis=0, keepdims=True) - center * center
    return center, lax.rsqrt(spread + EPSILON)


def norm_back(grad, normed, scale, gain):
    scaled = grad * gain
    return scale * (
        scaled
        - jnp.mean(scaled, axis=0, keepdims=True)
        - normed * jnp.mean(scaled * normed, axis=0, keepdims=True)
    )


def lane_sum(array):
    return jnp.sum(array, axis=-1, dtype=F32)


def on_device(
    tokens,
    memory,
    parents,
    memory_slots,
    query_weight,
    query_bias,
    key_weight,
    value_weight,
    value_bias,
    out_weight,
    out_bias,
    norm_gain,
    norm_shift,
    up_weight,
    up_bias,
    down_weight,
    down_bias,
    final_gain,
    final_shift,
    cotangent,
):
    rows, cols = lax.axis_size("row"), lax.axis_size("col")
    row, col = lax.axis_index("row"), lax.axis_index("col")
    feat, row_tokens = tokens.shape
    own = row_tokens // cols
    seg_row = row_tokens // SEG
    model = feat * cols
    width = query_weight.shape[1]
    hidden_width = up_weight.shape[1]
    bank = memory.shape[0]
    segments, ranges = plan_windows(own, cols)
    window = len(segments[0]) * SEG
    tail = 128
    lengths = tuple(min(SEG, own - j * SEG) for j in range(len(segments[0])))
    half = feat // 2
    parity = lax.axis_index("leaf") % 2
    here = jnp.stack([row, col, parity, jnp.int32(seg_row)]).astype(jnp.int32)
    blocks = [[b for a, n in ranges[i] for b in range(a // 128, (a + n) // 128)] for i in range(cols)]
    own_blocks = [each[: own // 128] for each in blocks]
    scalars = (here, parents, memory_slots)

    weight_half = pack_weights(
        here, query_weight, key_weight, value_weight, out_weight, up_weight, down_weight, up_bias, query_bias, value_bias
    )
    along = gather_weights(weight_half)

    vectors = (out_bias, norm_gain, norm_shift, down_bias, final_gain, final_shift)
    token_sends = pack(blocks, here, after(tokens, weight_half), memory, *vectors)
    cot_sends = pack(own_blocks, here, after(cotangent, token_sends))
    token_got = swap(token_sends[1], "col", 2)
    along = after(along, cot_sends, token_got)
    everything = lax.all_gather(after(tokens, along), "row", axis=0)
    row_vectors = jnp.stack([piece[3 * half :] for piece in along])
    near_first, far_first = (array[0] for array in whole_weights(spread_weights([piece[:half][None] for piece in along])))
    token_last = swap(jnp.concatenate([token_sends[2], token_got[1:]], axis=0), "col", 1)
    tok_window = joined((token_sends[0], token_got, token_last)).reshape(model, window + tail)
    win = project(near_first, far_first, tok_window, row_vectors, 0, 3 * width, width)
    partial = attend_own(lengths, segments, bank, scalars, win)
    second_parts = spread_weights([piece[half : 3 * half].reshape(2, half, -1) for piece in along], partial)
    cot_keep, cot_along, cot_near = after(cot_sends, second_parts[2])
    cot_got = swap(cot_along, "col", 2)
    cot_near = jnp.concatenate([cot_near, cot_got[1:]], axis=0)
    cot_pieces = cot_keep, cot_got, swap(cot_near, "col", 1)
    everything = after(everything, second_parts[2], cot_near)
    par_keep, par_along, par_near = pick_parents(segments, here, parents, everything)
    par_got = swap(par_along, "col", 2)
    near, far = whole_weights(after(second_parts, par_along))
    par_got = after(par_got, near)
    par_near = jnp.concatenate([par_near, par_got[1:]], axis=0)
    tok_parent = (par_keep, par_got, swap(par_near, "col", 1))
    par, ctx, lse = attend_parent(
        lengths, segments, scalars, win, partial, near_first, far_first, tok_parent, row_vectors
    )
    at = window + bank
    *result, active, upper_low, hidden_low, down_low, first_low, dctx, up_bias_grad, sums = mlp(
        at, ctx, tok_window, cot_pieces, near_first, far_first, near, far, row_vectors
    )
    result_keep, result_along, result_near = result
    dwin, dpar, par_keep, par_along, par_near = attend_back(
        lengths, segments, bank, scalars, win, par, ctx, dctx, lse, near_first, far_first
    )

    par_got = swap(par_along, "col", 2)
    down_keep, down_send, up_keep, up_send = hidden_grads(after(down_low, par_along), hidden_low, active, upper_low)
    down_near, up_near = swap(down_send, "col", 1), swap(up_send, "col", 1)
    par_got = after(par_got, up_send)
    par_near = jnp.concatenate([par_near, par_got[1:]], axis=0)
    placed = add_parents(segments, here, parents, (par_keep, par_got, swap(par_near, "col", 1)), rows, seg_row)
    down_across = reduce_across(after(down_keep, placed), down_near)
    up_along = reduce_y(after(up_keep, down_across), up_near)
    first_keep, first_send = first_grads(
        tok_window, tok_parent, dwin, dpar, after(first_low, up_along), ctx, up_bias_grad, sums
    )
    placed = lax.psum_scatter(placed, "row", scatter_dimension=0, tiled=False)
    first_near = swap(first_send, "col", 1)
    dtok = token_grads(near_first, far_first, dwin, after(first_low, first_send), window)
    corner = reduce_corner(after(first_keep, dtok), first_near)
    by_leaf, by_col = swap(corner[0], "leaf", 1), swap(corner[1], "col", 2)
    up_got = swap(up_along, "col", 2)
    up_across = reduce_x(after(up_keep, corner), up_near, up_got)
    down_across = swap(down_across, "leaf", 1)
    down_up = reduce_up(after(down_keep, up_across), down_near, down_across)
    edges = reduce_edges(after(first_keep, down_up), first_near, by_leaf, by_col)
    by_leaf, by_col = swap(edges[0], "leaf", 1), swap(edges[1], "col", 2)
    up_across = swap(up_across, "leaf", 1)
    up_rows = reduce_mine(after(up_keep, edges), up_near, up_got[:, 0], up_across)
    down_up = swap(down_up, "col", 2)
    down_rows = reduce_along(after(down_keep, up_rows), down_near, down_across, down_up)
    result_got = after(swap(result_along, "col", 2), down_rows)
    result_near = jnp.concatenate([result_near, result_got[1:]], axis=0)
    result_pieces = result_keep, result_got, swap(result_near, "col", 1)
    first_rows = reduce_mine(after(first_keep, down_rows), first_near, by_leaf, by_col)
    dtok_keep, dtok_along, dtok_near = dtok
    dtok_got = after(swap(after(dtok_along, edges), "col", 2), first_rows, result_near)
    dtok_near = jnp.concatenate([dtok_near, dtok_got[1:]], axis=0)
    layer_output = place(own_blocks, here, result_pieces, row_tokens)
    mem_sum = placed[:, row_tokens : row_tokens + bank].astype(F32)
    memory_grad = jnp.where(parity == 0, mem_sum, jnp.roll(mem_sum, half, axis=0)).T
    tokens_grad = finish_tokens(
        blocks, here, placed, (dtok_keep, dtok_got, swap(dtok_near, "col", 1)), row_tokens
    )
    down_got, up_got, first_got = send_rows(down_rows), send_rows(up_rows), send_rows(first_rows)
    down_rows, up_rows = after((down_rows, up_rows), first_rows)
    second_mine = jnp.concatenate([reduce_rows(down_rows, down_got), reduce_rows(up_rows, up_got)], axis=1)
    second_other = swap(second_mine, "leaf", 1)
    first_mine = reduce_rows(after(first_rows, second_mine, tokens_grad, memory_grad, layer_output), first_got)
    first_other = swap(first_mine, "leaf", 1)

    def in_order(mine, other):
        return jnp.where(
            parity == 0, jnp.concatenate([mine, other], axis=0), jnp.concatenate([other, mine], axis=0)
        ).astype(F32)

    second_total = in_order(second_mine, second_other)
    down_total, up_total = second_total[:, :hidden_width], second_total[:, hidden_width:]
    count = (2 * width + hidden_width) // half
    first_query, first_key, first_value, first_out, vectors = unpack(here, first_mine, first_other, width, count + 6)
    by_row = vectors[:count, :half].reshape(-1)
    by_col = vectors[count : count + 6]

    return (
        layer_output,
        tokens_grad,
        memory_grad,
        first_query,
        by_row[:width],
        first_key,
        first_value,
        by_row[width : 2 * width],
        first_out,
        by_col[0],
        by_col[1],
        by_col[2],
        up_total,
        by_row[2 * width :],
        down_total,
        by_col[3],
        by_col[4],
        by_col[5],
    )


def solution(mesh):
    return jax.shard_map(
        on_device,
        mesh=mesh,
        in_specs=(
            P("col", ("leaf", "row")),
            P("leaf", "col"),
            P("leaf"),
            P("leaf", None),
            P("col", "row"),
            P("row"),
            P("col", "row"),
            P("col", "row"),
            P("row"),
            P("row", "col"),
            P("col"),
            P("col"),
            P("col"),
            P("col", "row"),
            P("row"),
            P("col", "row"),
            P("col"),
            P("col"),
            P("col"),
            P("col", ("leaf", "row")),
        ),
        out_specs=(
            P("col", ("leaf", "row")),
            P("col", ("leaf", "row")),
            P("leaf", "col"),
            P("col", "row"),
            P("row"),
            P("col", "row"),
            P("col", "row"),
            P("row"),
            P("row", "col"),
            P("col"),
            P("col"),
            P("col"),
            P("col", "row"),
            P("row"),
            P("col", "row"),
            P("col"),
            P("col"),
            P("col"),
        ),
        check_vma=False,
    )
```

```python
import functools

import jax
import jax.numpy as jnp
import numpy as np
from jax import lax
from jax.experimental import pallas as pl
from jax.experimental.pallas import tpu as pltpu
from jax.sharding import PartitionSpec as P

HEAD = 64
SEG = 256
NEGATIVE = -1e30
EPSILON = 1e-05
EVERY = ("leaf", "row", "col")
BF16 = jnp.bfloat16
F32 = jnp.float32


def after(value, *others):
    return lax.optimization_barrier((value, others))[0]


def tn(left, right):
    return lax.dot_general(left, right, (((0,), (0,)), ((), ())), preferred_element_type=F32)


def nt(left, right):
    return lax.dot_general(left, right, (((1,), (1,)), ((), ())), preferred_element_type=F32)


def nn(left, right):
    return lax.dot_general(left, right, (((1,), (0,)), ((), ())), preferred_element_type=F32)


def plan_windows(own, count):
    segments, ranges = [], []
    for index in range(count):
        first, last = index * own, (index + 1) * own
        whole = [s for s in range(first // SEG, -(-last // SEG)) if s * SEG >= first and (s + 1) * SEG <= last]
        cut = [s for s in range(first // SEG, -(-last // SEG)) if s not in whole]
        pieces = [(s * SEG, SEG) for s in whole]
        for s in cut:
            low, high = max(first, s * SEG), min(last, (s + 1) * SEG)
            pieces.append((low, high - low))
            if low > s * SEG:
                pieces.append((s * SEG, low - s * SEG))
            if high < (s + 1) * SEG:
                pieces.append((high, (s + 1) * SEG - high))
        segments.append(whole + cut)
        ranges.append(pieces)
    return segments, ranges


def static_of(index, values):
    out = jnp.int32(values[0])
    for i, value in enumerate(values[1:], 1):
        out = jnp.where(index == i, jnp.int32(value), out)
    return out


def own_segments(segments, here_ref):
    return [
        here_ref[0] * here_ref[3] + static_of(here_ref[1], [lists[j] for lists in segments])
        for j in range(len(segments[0]))
    ]


def window_biases(segments, bank, here_ref, parents_ref, slots_ref):
    rows = lax.broadcasted_iota(jnp.int32, (bank, 1), 0)
    out = []
    for seg in own_segments(segments, here_ref):
        count = jnp.zeros((bank, 1), F32)
        for m in range(slots_ref.shape[1]):
            count = count + jnp.where(rows == slots_ref[seg, m], 1.0, 0.0)
        slot = jnp.where(count > 0, jnp.log(jnp.maximum(count, 1.0)), NEGATIVE)
        out.append((jnp.where(parents_ref[seg] >= 0, 0.0, NEGATIVE).astype(F32), slot))
    return out


def attention_own(
    head_count, lengths, segments, bank, here_ref, parents_ref, slots_ref, win_ref, mixed_ref, top_ref, total_ref
):
    width = head_count * HEAD
    window = len(lengths) * SEG
    biases = window_biases(segments, bank, here_ref, parents_ref, slots_ref)
    for head in range(head_count):
        low = head * HEAD
        key_mem = win_ref[0, width + low : width + low + HEAD, window : window + bank]
        value_mem = win_ref[0, 2 * width + low : 2 * width + low + HEAD, window : window + bank]
        for j, count in enumerate(lengths):
            cols = slice(j * SEG, (j + 1) * SEG)
            toks = slice(j * SEG, j * SEG + count)
            query = win_ref[0, low : low + HEAD, toks]
            own = tn(win_ref[0, width + low : width + low + HEAD, cols], query)
            mem = tn(key_mem, query) + biases[j][1]
            top = jnp.maximum(jnp.max(own, axis=0, keepdims=True), jnp.max(mem, axis=0, keepdims=True))
            own, mem = jnp.exp(own - top), jnp.exp(mem - top)
            mixed_ref[0, low : low + HEAD, toks] = nn(
                win_ref[0, 2 * width + low : 2 * width + low + HEAD, cols], own.astype(BF16)
            ) + nn(value_mem, mem.astype(BF16))
            top_ref[0, head : head + 1, toks] = top
            total_ref[0, head : head + 1, toks] = jnp.sum(own, axis=0, keepdims=True) + jnp.sum(
                mem, axis=0, keepdims=True
            )


def attention_parent(
    head_count,
    lengths,
    segments,
    here_ref,
    parents_ref,
    win_ref,
    mixed_ref,
    top_ref,
    total_ref,
    near_ref,
    far_ref,
    par_keep,
    par_got,
    par_last,
    bias_ref,
    par_ref,
    ctx_ref,
    lse_ref,
    toks_ref,
):
    width = head_count * HEAD
    depth = near_ref.shape[1]
    join_pieces((par_keep, par_got, par_last), toks_ref)
    both = tn(near_ref[0, :, width : 3 * width], toks_ref[:depth]) + tn(far_ref[0, :, width : 3 * width], toks_ref[depth:])
    par_ref[0] = (both + across_lanes(bias_ref[0], 1, width, 3 * width, both.shape[1])).astype(BF16)
    biases = [jnp.where(parents_ref[seg] >= 0, 0.0, NEGATIVE).astype(F32) for seg in own_segments(segments, here_ref)]
    for head in range(head_count):
        low = head * HEAD
        for j, count in enumerate(lengths):
            cols = slice(j * SEG, (j + 1) * SEG)
            toks = slice(j * SEG, j * SEG + count)
            par = tn(par_ref[0, low : low + HEAD, cols], win_ref[0, low : low + HEAD, toks]) + biases[j]
            first = top_ref[0, head : head + 1, toks]
            top = jnp.maximum(first, jnp.max(par, axis=0, keepdims=True))
            par = jnp.exp(par - top)
            scale = jnp.exp(first - top)
            total = total_ref[0, head : head + 1, toks] * scale + jnp.sum(par, axis=0, keepdims=True)
            mixed = mixed_ref[0, low : low + HEAD, toks] * scale
            mixed = mixed + nn(par_ref[0, width + low : width + low + HEAD, cols], par.astype(BF16))
            ctx_ref[0, low : low + HEAD, toks] = (mixed / total).astype(BF16)
            lse_ref[0, head : head + 1, toks] = top + jnp.log(total)


def attention_backward(
    head_count,
    lengths,
    segments,
    bank,
    here_ref,
    parents_ref,
    slots_ref,
    win_ref,
    par_ref,
    ctx_ref,
    dctx_ref,
    lse_ref,
    near_ref,
    far_ref,
    dwin_ref,
    dpar_ref,
    keep_ref,
    along_ref,
    close_ref,
    total_ref,
):
    width = head_count * HEAD
    biases = window_biases(segments, bank, here_ref, parents_ref, slots_ref)
    window = len(lengths) * SEG
    tail = win_ref.shape[2] - window
    for head in range(head_count):
        low = head * HEAD
        qs, ks, vs = (slice(part * width + low, part * width + low + HEAD) for part in range(3))
        key_mem = win_ref[0, ks, window : window + bank]
        value_mem = win_ref[0, vs, window : window + bank]
        dkey_mem = jnp.zeros((HEAD, bank), F32)
        dvalue_mem = jnp.zeros((HEAD, bank), F32)
        for j, count in enumerate(lengths):
            cols = slice(j * SEG, (j + 1) * SEG)
            tok = slice(j * SEG, j * SEG + count)
            query = win_ref[0, qs, tok]
            dctx = dctx_ref[0, low : low + HEAD, tok]
            lse = lse_ref[0, head : head + 1, tok]
            key_own, value_own = win_ref[0, ks, cols], win_ref[0, vs, cols]
            key_par, value_par = par_ref[0, low : low + HEAD, cols], par_ref[0, width + low : width + low + HEAD, cols]
            own = jnp.exp(tn(key_own, query) - lse)
            par = jnp.exp(tn(key_par, query) + biases[j][0] - lse)
            mem = jnp.exp(tn(key_mem, query) + biases[j][1] - lse)
            gown, gpar, gmem = tn(value_own, dctx), tn(value_par, dctx), tn(value_mem, dctx)
            ctx = ctx_ref[0, low : low + HEAD, tok].astype(F32)
            inner = jnp.sum(ctx * dctx.astype(F32), axis=0, keepdims=True)
            gown = (own * (gown - inner)).astype(BF16)
            gpar = (par * (gpar - inner)).astype(BF16)
            gmem = (mem * (gmem - inner)).astype(BF16)
            dquery = nn(key_own, gown) + nn(key_par, gpar) + nn(key_mem, gmem)
            dwin_ref[0, qs, tok] = (dquery * HEAD ** (-0.5)).astype(BF16)
            if count < SEG:
                dwin_ref[0, qs, j * SEG + count : (j + 1) * SEG] = jnp.zeros((HEAD, SEG - count), BF16)
            dwin_ref[0, ks, cols] = nt(query, gown).astype(BF16)
            dwin_ref[0, vs, cols] = nt(dctx, own.astype(BF16)).astype(BF16)
            dpar_ref[0, low : low + HEAD, cols] = nt(query, gpar).astype(BF16)
            dpar_ref[0, width + low : width + low + HEAD, cols] = nt(dctx, par.astype(BF16)).astype(BF16)
            dkey_mem += nt(query, gmem)
            dvalue_mem += nt(dctx, mem.astype(BF16))
        pad = jnp.zeros((HEAD, tail - bank), F32)
        dwin_ref[0, qs, window:] = jnp.zeros((HEAD, tail), BF16)
        dwin_ref[0, ks, window:] = jnp.concatenate([dkey_mem, pad], axis=1).astype(BF16)
        dwin_ref[0, vs, window:] = jnp.concatenate([dvalue_mem, pad], axis=1).astype(BF16)

    step, last = pl.program_id(0), pl.num_programs(0) - 1
    depth = near_ref.shape[1]
    grads = jnp.concatenate([dpar_ref[0], dwin_ref[0, width:, window:]], axis=1)
    near, far = nn(near_ref[0, :, width : 3 * width], grads), nn(far_ref[0, :, width : 3 * width], grads)

    @pl.when(step == 0)
    def begin():
        total_ref[:depth], total_ref[depth:] = near, far

    @pl.when(step > 0)
    def add():
        total_ref[:depth] += near
        total_ref[depth:] += far

    @pl.when(step == last)
    def finish():
        feat = keep_ref.shape[1]
        for i, out in enumerate((keep_ref.at[0], along_ref.at[0], close_ref.at[0], along_ref.at[1])):
            out[...] = total_ref[i * feat : (i + 1) * feat].astype(BF16)


def step_block(array):
    return pl.BlockSpec((1,) + array.shape[1:], lambda step, *_: (step, 0, 0))


def whole_block(array):
    return pl.BlockSpec(array.shape, lambda step, *_: (0,) * len(array.shape))


def cost(microseconds):
    return pl.CostEstimate(flops=int(microseconds * 1.0e9), bytes_accessed=0, transcendentals=0)


def held(*arrays):
    return tuple(pltpu.with_memory_space_constraint(array, pltpu.HBM) for array in arrays)


def in_hbm(shape):
    return pltpu.HBM(shape.shape, shape.dtype)


def params(mib):
    return pltpu.CompilerParams(vmem_limit_bytes=mib << 20)


def across_lanes(rows, index, low, high, columns):
    chosen = (lax.broadcasted_iota(jnp.int32, (rows.shape[0], 128), 0) == index).astype(BF16)
    column = tn(rows[:, low:high] if high - low < rows.shape[1] else rows, chosen)
    return jnp.concatenate([column] * (columns // 128), axis=1)


def join_pieces(refs, toks_ref):
    @pl.when(pl.program_id(0) == 0)
    def join():
        feat = refs[0].shape[1]
        for i, (piece, place) in enumerate(PIECES):
            toks_ref[i * feat : (i + 1) * feat] = refs[piece][place]


def project_kernel(low, high, scaled, near_ref, far_ref, *refs):
    depth = near_ref.shape[1]
    if len(refs) > 3:
        toks_ref, bias_ref, out_ref = refs[5], refs[3], refs[4]
        join_pieces(refs[:3], toks_ref)
    else:
        toks_ref, bias_ref, out_ref = refs
    out = tn(near_ref[0, :, low:high], toks_ref[:depth]) + tn(far_ref[0, :, low:high], toks_ref[depth:])
    out = (out + across_lanes(bias_ref[0], 1, low, high, out.shape[1])).astype(BF16)
    if scaled:
        out_ref[0, :scaled] = out[:scaled] * jnp.asarray(HEAD ** (-0.5), BF16)
        out_ref[0, scaled:] = out[scaled:]
    else:
        out_ref[0] = out


def project(near, far, toks, bias, low, high, scaled):
    groups, depth = near.shape[:2]
    pieces = toks if isinstance(toks, tuple) else (toks,)
    out = jax.ShapeDtypeStruct((groups, high - low, pieces[0].shape[-1]), BF16)
    return pl.pallas_call(
        functools.partial(project_kernel, low, high, scaled),
        grid=(groups,),
        in_specs=[step_block(near), step_block(far), *[whole_block(piece) for piece in pieces], step_block(bias)],
        scratch_shapes=[pltpu.VMEM((2 * depth, pieces[0].shape[-1]), BF16)] if len(pieces) > 1 else [],
        out_specs=step_block(out),
        out_shape=out,
        compiler_params=params(12),
        cost_estimate=cost(0.1),
        name="project",
    )(near, far, *pieces, bias)


def chunks(columns):
    return columns // 128


def mlp_kernel(
    at,
    ctx_ref,
    win_ref,
    cot_keep,
    cot_got,
    cot_last,
    near_first,
    far_first,
    near_ref,
    far_ref,
    bias_ref,
    keep_ref,
    along_ref,
    close_ref,
    active_ref,
    upper_ref,
    hidden_ref,
    low_ref,
    first_low_ref,
    dctx_ref,
    up_sum_ref,
    sums_ref,
    total_ref,
    wide_ref,
    parts_ref,
    normed_ref,
    scale_ref,
    slope_ref,
    columns_ref,
    out_ref,
    weights_ref,
    sem,
):
    step, groups = pl.program_id(0), slope_ref.shape[0]
    depth, width = near_ref.shape[2:]
    model, own = total_ref.shape
    feat = keep_ref.shape[1]
    heads = ctx_ref.shape[1]
    skip = out_ref.shape[3] - heads

    def weight_copies(block):
        return [
            pltpu.make_async_copy(
                source.at[which, block], weights_ref.at[which, side, block], sem.at[2 + 4 * block + 2 * which + side]
            )
            for which in range(2)
            for side, source in enumerate((near_ref, far_ref))
        ]

    first_copies = [
        pltpu.make_async_copy(
            source.at[:, :, pl.ds(width - out_ref.shape[3], out_ref.shape[3])], out_ref.at[side], sem.at[side]
        )
        for side, source in enumerate((near_first, far_first))
    ]

    def over_columns(body):
        def run(i, carry):
            body(pl.ds(pl.multiple_of(i * 128, 128), 128))
            return carry

        lax.fori_loop(0, own // 128, run, 0)

    def sum_parts(first):
        for i in range(3):
            sums_ref[:, first + i : first + i + 1] = jnp.sum(parts_ref[i], axis=1, keepdims=True)
        parts_ref[...] = jnp.zeros(parts_ref.shape, F32)

    @pl.when(step == 0)
    def start():
        for copy in first_copies:
            copy.start()
        for block in range(groups):
            for copy in weight_copies(block):
                copy.start()
        for i in range(6):
            columns_ref[i] = jnp.broadcast_to(win_ref[:, at + i : at + i + 1].astype(F32), (model, 128))
        parts_ref[...] = jnp.zeros(parts_ref.shape, F32)
        for copy in first_copies:
            copy.wait()
        for n in range(groups):
            near, far = nn(out_ref[0, n, :, skip:], ctx_ref[n]), nn(out_ref[1, n, :, skip:], ctx_ref[n])
            if n == 0:
                total_ref[:depth], total_ref[depth:] = near, far
            else:
                total_ref[:depth] += near
                total_ref[depth:] += far

        def body(cols):
            values = total_ref[:, cols] + columns_ref[0] + win_ref[:, cols].astype(F32)
            center, scale = norm_stats(values)
            normed = (values - center) * scale
            hidden = normed * columns_ref[1] + columns_ref[2]
            normed_ref[:, cols] = normed
            scale_ref[:, cols] = scale
            wide_ref[:, cols] = hidden
            hidden_ref[:, cols] = hidden.astype(BF16)

        over_columns(body)
        total_ref[...] = jnp.zeros(total_ref.shape, F32)

    @pl.when(step < groups)
    def forward():
        for block in range(groups):

            @pl.when(step == block)
            def arrive(block=block):
                for copy in weight_copies(block):
                    copy.wait()

        piece = width // 3
        for low in range(0, width, piece):
            rows = slice(low, low + piece)
            upper = tn(weights_ref[0, 0, step, :, rows], hidden_ref[:depth])
            upper = upper + tn(weights_ref[0, 1, step, :, rows], hidden_ref[depth:])
            upper = upper + across_lanes(bias_ref[0], 0, low, low + piece, own)
            phi = 0.5 * (1.0 + lax.erf(upper * np.float32(0.5**0.5)))
            active_ref[0, rows] = (upper * phi).astype(BF16)
            slope_ref[step, rows] = (
                phi + upper * jnp.exp(-0.5 * upper * upper) * np.float32(1.0 / np.sqrt(2.0 * np.pi))
            ).astype(BF16)
        active = active_ref[0]
        total_ref[:depth] += nn(weights_ref[1, 0, step], active)
        total_ref[depth:] += nn(weights_ref[1, 1, step], active)

    @pl.when(step == groups - 1)
    def turn():
        pieces = (cot_keep, cot_got, cot_last)

        def body(cols):
            values = total_ref[:, cols] + columns_ref[3] + wide_ref[:, cols]
            center, scale = norm_stats(values)
            normed = (values - center) * scale
            result = (normed * columns_ref[4] + columns_ref[5]).astype(BF16)
            keep_ref[0, :, cols] = result[:feat]
            along_ref[0, :, cols] = result[feat : 2 * feat]
            close_ref[0, :, cols] = result[2 * feat : 3 * feat]
            along_ref[1, :, cols] = result[3 * feat :]
            cot = jnp.concatenate([pieces[i][j, :, cols] for i, j in PIECES], axis=0).astype(F32)
            grad = norm_back(cot, normed, scale, columns_ref[4])
            total_ref[:, cols] = grad
            grad_low = grad.astype(BF16)
            low_ref[:, cols] = grad_low
            parts_ref[0] += grad_low.astype(F32)
            parts_ref[1] += cot * normed
            parts_ref[2] += cot

        over_columns(body)
        sum_parts(3)

    @pl.when(step >= groups)
    def backward():
        block = step - groups
        upper = tn(weights_ref[1, 0, block], low_ref[:depth]) + tn(weights_ref[1, 1, block], low_ref[depth:])
        upper = (upper * slope_ref[block].astype(F32)).astype(BF16)
        upper_ref[0] = upper
        up_sum_ref[0] = jnp.sum(upper.astype(F32), axis=1, keepdims=True)
        total_ref[:depth] += nn(weights_ref[0, 0, block], upper)
        total_ref[depth:] += nn(weights_ref[0, 1, block], upper)

    @pl.when(step == 2 * groups - 1)
    def finish():
        def body(cols):
            hidden_grad = total_ref[:, cols]
            normed = normed_ref[:, cols]
            first_low = norm_back(hidden_grad, normed, scale_ref[:, cols], columns_ref[1]).astype(BF16)
            first_low_ref[:, cols] = first_low
            parts_ref[0] += first_low.astype(F32)
            parts_ref[1] += hidden_grad * normed
            parts_ref[2] += hidden_grad

        over_columns(body)
        sum_parts(0)
        for n in range(groups):
            grads = tn(out_ref[0, n, :, skip:], first_low_ref[:depth]) + tn(out_ref[1, n, :, skip:], first_low_ref[depth:])
            dctx_ref[n] = grads.astype(BF16)


def once(array):
    return pl.BlockSpec(
        array.shape, lambda step, *_: (0,) * len(array.shape), pipeline_mode=pl.Buffered(1)
    )


def mlp(at, ctx, win, cot, near_first, far_first, near, far, bias):
    groups, depth, width = near.shape[1:]
    feat, own = cot[0].shape[1:]
    model = feat * 4
    out_columns = -(-ctx.shape[1] // 128) * 128

    def early(array):
        return pl.BlockSpec((1,) + array.shape[1:], lambda step, *_: (jnp.minimum(step, groups - 1), 0, 0))

    def late(array):
        return pl.BlockSpec((1,) + array.shape[1:], lambda step, *_: (jnp.maximum(step - groups, 0), 0, 0))

    outs = [
        jax.ShapeDtypeStruct((1, feat, own), BF16),
        jax.ShapeDtypeStruct((2, feat, own), BF16),
        jax.ShapeDtypeStruct((1, feat, own), BF16),
        jax.ShapeDtypeStruct((groups, width, own), BF16),
        jax.ShapeDtypeStruct((groups, width, own), BF16),
        jax.ShapeDtypeStruct((model, own), BF16),
        jax.ShapeDtypeStruct((model, own), BF16),
        jax.ShapeDtypeStruct((model, own), BF16),
        jax.ShapeDtypeStruct(ctx.shape, BF16),
        jax.ShapeDtypeStruct((groups, width, 1), F32),
        jax.ShapeDtypeStruct((model, 6), F32),
    ]
    return pl.pallas_call(
        functools.partial(mlp_kernel, at),
        grid=(2 * groups,),
        in_specs=[
            once(ctx),
            once(win),
            *[once(piece) for piece in cot],
            HBM,
            HBM,
            HBM,
            HBM,
            pl.BlockSpec((1,) + bias.shape[1:], lambda step, *_: (jnp.minimum(step, groups - 1), 0, 0)),
        ],
        out_specs=[early(o) if i == 3 else late(o) if i in (4, 9) else once(o) for i, o in enumerate(outs)],
        out_shape=[in_hbm(o) if i in (3, 4, 5, 6, 7) else o for i, o in enumerate(outs)],
        scratch_shapes=[
            pltpu.VMEM((model, own), F32),
            pltpu.VMEM((model, own), F32),
            pltpu.VMEM((3, model, 128), F32),
            pltpu.VMEM((model, own), F32),
            pltpu.VMEM((1, own), F32),
            pltpu.VMEM((groups, width, own), BF16),
            pltpu.VMEM((6, model, 128), F32),
            pltpu.VMEM((2, groups, depth, out_columns), BF16),
            pltpu.VMEM((2, 2, groups, depth, width), BF16),
            pltpu.SemaphoreType.DMA((2 + 4 * groups,)),
        ],
        compiler_params=params(44),
        cost_estimate=cost(400),
        name="mlp",
    )(ctx, win, *cot, near_first, far_first, near, far, bias)


def hidden_grad_kernel(low_ref, hidden_ref, active_ref, upper_ref, down_keep, down_send, up_keep, up_send):
    depth = down_keep.shape[1]
    for keep, send, left, right in (
        (down_keep, down_send, low_ref, active_ref),
        (up_keep, up_send, hidden_ref, upper_ref),
    ):
        keep[0] = nt(left[:depth], right[0]).astype(BF16)
        send[0] = nt(left[depth:], right[0]).astype(BF16)


def hidden_grads(low, hidden, active, upper):
    groups, width, own = active.shape
    out = jax.ShapeDtypeStruct((groups, low.shape[0] // 2, width), BF16)
    return pl.pallas_call(
        hidden_grad_kernel,
        grid=(groups,),
        in_specs=[whole_block(low), whole_block(hidden), step_block(active), step_block(upper)],
        out_specs=[step_block(out)] * 4,
        out_shape=[in_hbm(out)] * 4,
        compiler_params=params(14),
        cost_estimate=cost(100),
        name="hidden_grads",
    )(*held(low, hidden, active, upper))


def first_grad_kernel(
    width,
    win_ref,
    par_keep,
    par_got,
    par_last,
    dwin_ref,
    dpar_ref,
    low_ref,
    ctx_ref,
    up_ref,
    sums_ref,
    keep_ref,
    send_ref,
    par_ref,
):
    join_pieces((par_keep, par_got, par_last), par_ref)
    depth = keep_ref.shape[1]
    half = depth // 4
    query = jnp.sum(dwin_ref[0, :width].astype(F32), axis=1, keepdims=True)
    value = jnp.sum(dwin_ref[0, 2 * width :].astype(F32), axis=1, keepdims=True)
    value = value + jnp.sum(dpar_ref[0, width:].astype(F32), axis=1, keepdims=True)
    by_row = [array[i : i + half] for array in (query, value, up_ref[0]) for i in range(0, array.shape[0], half)]
    by_row = jnp.concatenate(by_row, axis=1)
    by_row = jnp.concatenate([by_row] * 4, axis=0)
    used = by_row.shape[1] + 6
    pad = jnp.zeros((depth, keep_ref.shape[2] - 4 * width - used), F32)
    for part, out_ref in enumerate((keep_ref, send_ref)):
        rows = slice(part * depth, (part + 1) * depth)
        win, par = win_ref[rows], par_ref[rows]
        out_ref[0, :, :width] = nt(win, dwin_ref[0, :width]).astype(BF16)
        for i in range(1, 3):
            grads = nt(win, dwin_ref[0, i * width : (i + 1) * width])
            grads = grads + nt(par, dpar_ref[0, (i - 1) * width : i * width])
            out_ref[0, :, i * width : (i + 1) * width] = grads.astype(BF16)
        out_ref[0, :, 3 * width : 4 * width] = nt(low_ref[rows], ctx_ref[0]).astype(BF16)
        extra = jnp.concatenate([by_row, sums_ref[rows], pad], axis=1)
        out_ref[0, :, 4 * width :] = extra.astype(BF16)


def first_grads(win, par, dwin, dpar, low, ctx, up_bias, sums):
    groups, width, own = ctx.shape
    out = jax.ShapeDtypeStruct((groups, low.shape[0] // 2, 4 * width + 128), BF16)
    return pl.pallas_call(
        functools.partial(first_grad_kernel, width),
        grid=(groups,),
        in_specs=[
            whole_block(win),
            *[whole_block(piece) for piece in par],
            step_block(dwin),
            step_block(dpar),
            whole_block(low),
            step_block(ctx),
            step_block(up_bias),
            whole_block(sums),
        ],
        out_specs=[step_block(out)] * 2,
        out_shape=[out] * 2,
        scratch_shapes=[pltpu.VMEM((low.shape[0], par[0].shape[2]), BF16)],
        compiler_params=params(16),
        cost_estimate=cost(15),
        name="first_grads",
    )(*held(win, *par, dwin, dpar, low, ctx), up_bias, sums)


def token_grad_kernel(high, near_ref, far_ref, dwin_ref, more_ref, keep_ref, along_ref, close_ref, total_ref):
    step, last = pl.program_id(0), pl.num_programs(0) - 1
    depth = near_ref.shape[1]
    own = more_ref.shape[1]

    @pl.when(step == 0)
    def start():
        total_ref[...] = jnp.zeros(total_ref.shape, F32)
        total_ref[:, :own] = more_ref[...].astype(F32)

    grads = dwin_ref[0]
    total_ref[:depth] += nn(near_ref[0, :, :high], grads)
    total_ref[depth:] += nn(far_ref[0, :, :high], grads)

    @pl.when(step == last)
    def finish():
        feat = keep_ref.shape[1]
        for i, out in enumerate((keep_ref.at[0], along_ref.at[0], close_ref.at[0], along_ref.at[1])):
            out[...] = total_ref[i * feat : (i + 1) * feat].astype(BF16)


def token_grads(near, far, dwin, more, columns):
    groups, depth = near.shape[:2]
    feat = depth // 2
    outs = [jax.ShapeDtypeStruct((n, feat, columns), BF16) for n in (1, 2, 1)]
    return pl.pallas_call(
        functools.partial(token_grad_kernel, dwin.shape[1]),
        grid=(groups,),
        in_specs=[
            step_block(near),
            step_block(far),
            pl.BlockSpec((1, dwin.shape[1], columns), lambda step: (step, 0, 0)),
            whole_block(more),
        ],
        out_specs=[whole_block(out) for out in outs],
        out_shape=outs,
        scratch_shapes=[pltpu.VMEM((2 * depth, columns), F32)],
        compiler_params=params(14),
        cost_estimate=cost(30),
        name="token_grads",
    )(near, far, dwin, more)


def attend_own(lengths, segments, bank, scalars, window):
    groups, rows, columns = window.shape
    width = rows // 3
    own = sum(lengths)
    outs = (
        jax.ShapeDtypeStruct((groups, width, own), F32),
        jax.ShapeDtypeStruct((groups, width // HEAD, own), F32),
        jax.ShapeDtypeStruct((groups, width // HEAD, own), F32),
    )
    return pl.pallas_call(
        functools.partial(attention_own, width // HEAD, lengths, segments, bank),
        grid=(groups,),
        in_specs=[SMEM] * 3 + [step_block(window)],
        out_specs=[step_block(out) for out in outs],
        out_shape=outs,
        compiler_params=params(14),
        cost_estimate=cost(0.1),
        name="attention_own",
    )(*scalars, window)


def attend_parent(lengths, segments, scalars, window, partial, near, far, toks, bias):
    groups, rows, columns = window.shape
    width = rows // 3
    depth = near.shape[1]
    outs = (
        jax.ShapeDtypeStruct((groups, 2 * width, toks[0].shape[2]), BF16),
        jax.ShapeDtypeStruct((groups, width, sum(lengths)), BF16),
        jax.ShapeDtypeStruct((groups, width // HEAD, sum(lengths)), F32),
    )
    return pl.pallas_call(
        functools.partial(attention_parent, width // HEAD, lengths, segments),
        grid=(groups,),
        in_specs=[SMEM] * 2
        + [step_block(array) for array in (window, *partial, near, far)]
        + [whole_block(piece) for piece in toks]
        + [step_block(bias)],
        out_specs=[step_block(out) for out in outs],
        out_shape=[in_hbm(outs[0]), *outs[1:]],
        scratch_shapes=[pltpu.VMEM((2 * depth, toks[0].shape[2]), BF16)],
        compiler_params=params(18),
        cost_estimate=cost(130),
        name="attention_parent",
    )(*scalars[:2], window, *partial, *held(near, far), *toks, bias)


def attend_back(lengths, segments, bank, scalars, window, parent, ctx, dctx, lse, near, far):
    groups, rows, columns = window.shape
    depth = near.shape[1]
    feat = depth // 2
    outs = (jax.ShapeDtypeStruct(window.shape, BF16), jax.ShapeDtypeStruct(parent.shape, BF16))
    sends = [jax.ShapeDtypeStruct((n, feat, columns), BF16) for n in (1, 2, 1)]
    return pl.pallas_call(
        functools.partial(attention_backward, rows // 3 // HEAD, lengths, segments, bank),
        grid=(groups,),
        in_specs=[SMEM] * 3 + [step_block(array) for array in (window, parent, ctx, dctx, lse, near, far)],
        out_specs=[step_block(out) for out in outs] + [whole_block(out) for out in sends],
        out_shape=[*map(in_hbm, outs), *sends],
        scratch_shapes=[pltpu.VMEM((2 * depth, columns), F32)],
        compiler_params=params(24),
        cost_estimate=cost(200),
        name="attention_backward",
    )(*scalars, *held(window, parent, ctx), dctx, lse, *held(near, far))


def swap(array, axis, mask):
    count = lax.axis_size(axis)
    return lax.ppermute(array, axis, [(i, i ^ mask) for i in range(count)])


SMEM = pl.BlockSpec(memory_space=pltpu.SMEM)
VMEM = pl.BlockSpec(memory_space=pltpu.VMEM)
HBM = pl.BlockSpec(memory_space=pltpu.HBM)
ORDER = (0, 2, 1, 3)
SENDS = ((0, 0), (1, 0), (2, 0), (1, 1))


def at_distance(here_ref, lists, slot, j):
    distance = ORDER[slot]
    return static_of(here_ref[1], [lists[i ^ distance][j] for i in range(len(lists))])


def flipped(here_ref, part, half):
    return pl.multiple_of((part ^ here_ref[2]) * half, 32)


def spots(rows, columns, shift):
    return (
        lax.broadcasted_iota(jnp.int32, (rows, columns), 0) + shift
        == lax.broadcasted_iota(jnp.int32, (rows, columns), 1)
    ).astype(BF16)


def as_row(ref):
    return ref[...].astype(F32).reshape(1, ref.shape[0])


def fetch(pairs, sem):
    copies = [pltpu.make_async_copy(source, target, sem.at[i]) for i, (source, target) in enumerate(pairs)]
    for copy in copies:
        copy.start()
    for copy in copies:
        copy.wait()


def pack_weights_kernel(here_ref, *refs):
    count = 9
    inputs, half_ref = refs[:count], refs[count]
    held, turned_ref, sem = refs[count + 1 : -2], refs[-2], refs[-1]
    feat, width = inputs[0].shape
    half = feat // 2
    rows = pl.ds(flipped(here_ref, 0, half), half)
    small = [inputs[i] for i in (0, 1, 2, 3, 6, 7, 8)]
    fetch(
        [*zip(small, held)]
        + [(inputs[4 + i].at[rows, :], half_ref.at[pl.ds((1 + i) * half, half), :]) for i in range(2)],
        sem,
    )
    query_ref, key_ref, value_ref, out_ref, up_b_ref, query_b_ref, value_b_ref = held
    turned_ref[...] = tn(out_ref[...], spots(width, width, 0)).astype(BF16)
    for i, ref in enumerate((query_ref, key_ref, value_ref, turned_ref)):
        half_ref[:half, i * width : (i + 1) * width] = ref[rows, :]
    zero = jnp.zeros((1, width), F32)
    joint = [as_row(query_b_ref), zero, as_row(value_b_ref), zero]
    wide = (half_ref.shape[0] - 3 * half, half_ref.shape[1])
    index = lax.broadcasted_iota(jnp.int32, wide, 0)
    up_row = jnp.broadcast_to(as_row(up_b_ref), wide)
    joint_row = jnp.broadcast_to(jnp.concatenate(joint, axis=1), wide)
    half_ref[3 * half :] = jnp.where(index == 0, up_row, jnp.where(index == 1, joint_row, 0.0)).astype(BF16)


def pack_weights(here, query, key, value, out, up, down, *biases):
    feat, width = query.shape
    hidden = up.shape[1]
    inputs = (query, key, value, out, up, down, *biases)
    small = [query, key, value, out, *biases]
    return pl.pallas_call(
        pack_weights_kernel,
        in_specs=[SMEM] + [HBM] * len(inputs),
        out_specs=VMEM,
        out_shape=jax.ShapeDtypeStruct((3 * feat // 2 + 8, hidden), BF16),
        scratch_shapes=[pltpu.VMEM(array.shape, array.dtype) for array in small]
        + [pltpu.VMEM((feat, width), BF16), pltpu.SemaphoreType.DMA((len(inputs),))],
        compiler_params=params(6),
        cost_estimate=cost(0.1),
        name="pack_weights",
    )(here, *held(*inputs))


def pack_kernel(blocks, sided, here_ref, *refs):
    given = 1 + sided
    outs, held, sem = refs[given : given + 3], refs[given + 3 : given + 3 + given], refs[-1]
    fetch([*zip(refs[:given], held)], sem)
    source_ref = held[0]
    half = source_ref.shape[0] // 2
    count = len(blocks[0])
    if sided:
        mem_ref, vector_refs, side_ref = held[1], held[2:], refs[-2]
        bank = mem_ref.shape[0]
        vectors = jnp.concatenate([as_row(ref) for ref in vector_refs], axis=0)
        vectors = jnp.concatenate([vectors, jnp.zeros((8 - len(vector_refs), vectors.shape[1]), F32)], axis=0)
        side = tn(mem_ref[...], spots(bank, 128, 0)) + tn(vectors.astype(BF16), spots(8, 128, bank))
        side_ref[...] = side.astype(BF16)
    for slot, (out, place) in enumerate(SENDS):
        for part in range(2):
            low = flipped(here_ref, part, half)
            rows = slice(part * half, (part + 1) * half)
            for j in range(count):
                at = pl.multiple_of(at_distance(here_ref, blocks, slot, j) * 128, 128)
                outs[out][place, rows, j * 128 : (j + 1) * 128] = source_ref[pl.ds(low, half), pl.ds(at, 128)]
            if sided:
                outs[out][place, rows, count * 128 :] = side_ref[pl.ds(low, half), :]


def pack(blocks, here, source, *side):
    feat = source.shape[0]
    columns = len(blocks[0]) * 128 + (128 if side else 0)
    inputs = (source, *side)
    return pl.pallas_call(
        functools.partial(pack_kernel, blocks, len(side)),
        in_specs=[SMEM] + [HBM] * len(inputs),
        out_specs=[VMEM] * 3,
        out_shape=[jax.ShapeDtypeStruct((n, feat, columns), source.dtype) for n in (1, 2, 1)],
        scratch_shapes=[pltpu.VMEM(array.shape, array.dtype) for array in inputs]
        + ([pltpu.VMEM((feat, 128), BF16)] if side else [])
        + [pltpu.SemaphoreType.DMA((len(inputs),))],
        compiler_params=params(12),
        cost_estimate=cost(0.1),
        name="pack",
    )(here, *held(*inputs))


def exchange(keep, along, near):
    got = swap(along, "col", 2)
    return keep, got, swap(jnp.concatenate([near, got[1:]], axis=0), "col", 1)


def joined(pieces):
    keep, got, last = pieces
    return jnp.concatenate([keep, got[:1], last], axis=0)


PIECES = ((0, 0), (1, 0), (2, 0), (2, 1))


def parent_of(here_ref, parents_ref, segments, slot, j):
    return parents_ref[here_ref[0] * here_ref[3] + at_distance(here_ref, segments, slot, j)]


def pick_kernel(segments, here_ref, parents_ref, source_ref, *refs):
    outs, sem = refs[:3], refs[3]
    half = source_ref.shape[1] // 2
    seg_row = here_ref[3]
    pairs = []
    for slot, (out, place) in enumerate(SENDS):
        for j in range(len(segments[0])):
            seg = jnp.maximum(parent_of(here_ref, parents_ref, segments, slot, j), 0)
            row = lax.div(seg, seg_row)
            at = pl.multiple_of((seg - row * seg_row) * SEG, SEG)
            for part in range(2):
                rows = slice(part * half, (part + 1) * half)
                source = source_ref.at[row, pl.ds(flipped(here_ref, part, half), half), pl.ds(at, SEG)]
                pairs.append((source, outs[out].at[place, rows, pl.ds(j * SEG, SEG)]))
    fetch(pairs, sem)


def pick_parents(segments, here, parents, gathered):
    feat = gathered.shape[1]
    columns = len(segments[0]) * SEG
    return pl.pallas_call(
        functools.partial(pick_kernel, segments),
        in_specs=[SMEM, SMEM, HBM],
        out_specs=[VMEM] * 3,
        out_shape=[jax.ShapeDtypeStruct((n, feat, columns), gathered.dtype) for n in (1, 2, 1)],
        scratch_shapes=[pltpu.SemaphoreType.DMA((8 * len(segments[0]),))],
        compiler_params=params(8),
        cost_estimate=cost(1),
        name="pick_parents",
    )(here, parents, *held(gathered))


def add_parents_kernel(segments, seg_row, here_ref, parents_ref, *refs):
    pieces, given_ref, sum_ref, out_ref, sem = refs[:3], refs[3], refs[4], refs[5], refs[6]
    window = len(segments[0]) * SEG
    copies = []
    sum_ref[...] = jnp.zeros(sum_ref.shape, F32)
    for slot, (piece, place) in enumerate(PIECES):
        for j in range(len(segments[0])):
            seg = parent_of(here_ref, parents_ref, segments, slot, j)

            @pl.when(seg >= 0)
            def add(seg=seg, piece=piece, place=place, cols=slice(j * SEG, (j + 1) * SEG)):
                sum_ref[seg] += pieces[piece][place, :, cols].astype(F32)

    mem = sum(pieces[piece][place, :, window:].astype(F32) for piece, place in PIECES)
    for r in range(out_ref.shape[0]):
        for s in range(seg_row):
            out_ref[r, :, s * SEG : (s + 1) * SEG] = sum_ref[r * seg_row + s].astype(BF16)
        out_ref[r, :, seg_row * SEG :] = mem.astype(BF16)
        copies.append(pltpu.make_async_copy(out_ref.at[r], given_ref.at[r], sem.at[r]))
        copies[-1].start()
    for copy in copies:
        copy.wait()


def add_parents(segments, here, parents, pieces, rows, seg_row):
    feat, columns = pieces[0].shape[1:]
    bank = columns - len(segments[0]) * SEG
    return pl.pallas_call(
        functools.partial(add_parents_kernel, segments, seg_row),
        in_specs=[SMEM, SMEM, VMEM, VMEM, VMEM],
        out_specs=HBM,
        out_shape=pltpu.HBM((rows, feat, seg_row * SEG + bank), BF16),
        scratch_shapes=[
            pltpu.VMEM((rows * seg_row, feat, SEG), F32),
            pltpu.VMEM((rows, feat, seg_row * SEG + bank), BF16),
            pltpu.SemaphoreType.DMA((rows,)),
        ],
        compiler_params=params(28),
        cost_estimate=cost(60),
        name="add_parents",
    )(here, parents, *pieces)


def finish_kernel(blocks, here_ref, placed_ref, *refs):
    pieces, out_ref = refs[:3], refs[3]
    half = out_ref.shape[0] // 2
    for part in range(2):
        low = flipped(here_ref, part, half)
        rows = slice(part * half, (part + 1) * half)
        out_ref[pl.ds(low, half), :] = placed_ref[rows, : out_ref.shape[1]].astype(F32)
        for slot, (piece, place) in enumerate(PIECES):
            for j in range(len(blocks[0])):
                at = pl.multiple_of(at_distance(here_ref, blocks, slot, j) * 128, 128)
                out_ref[pl.ds(low, half), pl.ds(at, 128)] += pieces[piece][
                    place, rows, j * 128 : (j + 1) * 128
                ].astype(F32)


def finish_tokens(blocks, here, placed, pieces, columns):
    return pl.pallas_call(
        functools.partial(finish_kernel, blocks),
        in_specs=[SMEM, VMEM, VMEM, VMEM, VMEM],
        out_specs=VMEM,
        out_shape=jax.ShapeDtypeStruct((placed.shape[0], columns), F32),
        compiler_params=params(10),
        cost_estimate=cost(2.5),
        name="finish_tokens",
    )(here, placed, *pieces)


def place_kernel(blocks, here_ref, *refs):
    pieces, out_ref = refs[:3], refs[3]
    half = out_ref.shape[0] // 2
    for part in range(2):
        low = flipped(here_ref, part, half)
        rows = slice(part * half, (part + 1) * half)
        for slot, (piece, place) in enumerate(PIECES):
            for j in range(pieces[0].shape[2] // 128):
                at = pl.multiple_of(at_distance(here_ref, blocks, slot, j) * 128, 128)
                out_ref[pl.ds(low, half), pl.ds(at, 128)] = pieces[piece][place, rows, j * 128 : (j + 1) * 128]


def place(blocks, here, pieces, columns):
    return pl.pallas_call(
        functools.partial(place_kernel, blocks),
        in_specs=[SMEM, VMEM, VMEM, VMEM],
        out_specs=VMEM,
        out_shape=jax.ShapeDtypeStruct((pieces[0].shape[1], columns), pieces[0].dtype),
        compiler_params=params(6),
        cost_estimate=cost(1.7),
        name="place",
    )(here, *pieces)


def unpack_kernel(width, count, here_ref, mine_ref, other_ref, query_ref, key_ref, value_ref, out_ref, more_ref, all_ref):
    half = mine_ref.shape[0]
    all_ref[pl.ds(flipped(here_ref, 0, half), half), :] = mine_ref[...].astype(F32)
    all_ref[pl.ds(flipped(here_ref, 1, half), half), :] = other_ref[...].astype(F32)
    for i, ref in enumerate((query_ref, key_ref, value_ref)):
        ref[...] = all_ref[:, i * width : (i + 1) * width]
    out_ref[...] = all_ref[:, 3 * width : 4 * width].T
    rows = all_ref[:, 4 * width :].T
    more_ref[...] = rows[: more_ref.shape[0]]


def unpack(here, mine, other, width, count):
    feat = 2 * mine.shape[0]
    square = jax.ShapeDtypeStruct((feat, width), F32)
    return pl.pallas_call(
        functools.partial(unpack_kernel, width, count),
        in_specs=[SMEM, VMEM, VMEM],
        out_specs=[VMEM] * 5,
        out_shape=[square] * 3 + [jax.ShapeDtypeStruct((width, feat), F32), jax.ShapeDtypeStruct((24, feat), F32)],
        scratch_shapes=[pltpu.VMEM((feat, mine.shape[1]), F32)],
        compiler_params=params(4),
        cost_estimate=cost(2),
        name="unpack",
    )(here, mine, other)


def gather_weights(half):
    return [half] + [swap(half, "row", n) for n in range(1, lax.axis_size("row"))]


def spread_weights(along, *gate):
    along = jnp.stack(along, axis=1)
    opposite = swap(along, "leaf", 1)
    across = after(swap(along, "col", 2), *gate)
    return along, opposite, across, swap(across, "leaf", 1)


def whole_weights(parts):
    near = jnp.stack(parts, axis=2)
    arrays, rows, blocks, depth, columns = near.shape
    near = near.reshape(arrays, rows, blocks * depth, columns)
    return near, swap(near, "col", 1)


def add_up(*terms):
    total = terms[0].astype(F32)
    for term in terms[1:]:
        total = total + term.astype(F32)
    return total


def reduce_blocks(keep):
    rows, features, columns = keep.shape
    return rows, 2, 2, features // 4, columns


def reduce_across(keep, near):
    shape = reduce_blocks(keep)
    return add_up(keep.reshape(shape)[:, :, 1], near.reshape(shape)[:, :, 1]).astype(BF16)


def reduce_y(keep, near):
    shape = reduce_blocks(keep)
    return add_up(keep.reshape(shape)[:, 1], near.reshape(shape)[:, 1]).astype(BF16)


def reduce_x(keep, near, got):
    shape = reduce_blocks(keep)
    return add_up(keep.reshape(shape)[:, 0, 1], near.reshape(shape)[:, 0, 1], got[:, 1]).astype(BF16)


def reduce_up(keep, near, across):
    shape = reduce_blocks(keep)
    return add_up(keep.reshape(shape)[:, 1, 0], near.reshape(shape)[:, 1, 0], across[:, 1]).astype(BF16)


def reduce_along(keep, near, across, up):
    shape = reduce_blocks(keep)
    mine = add_up(keep.reshape(shape)[:, 0, 0], near.reshape(shape)[:, 0, 0], across[:, 0], up)
    return [mine[n].astype(BF16) for n in range(shape[0])]


def reduce_rows(along, got):
    total = add_up(along[0], *got)
    mask = 2
    while mask < lax.axis_size("leaf"):
        total = add_up(total, swap(total.astype(BF16), "leaf", mask))
        mask *= 2
    return total.astype(BF16)


def reduce_corner(keep, near):
    shape = reduce_blocks(keep)
    middle = shape[0] // 2
    corner = add_up(keep.reshape(shape)[:, 1, 1], near.reshape(shape)[:, 1, 1]).astype(BF16)
    return corner[:middle], corner[middle:]


def reduce_edges(keep, near, by_leaf, by_col):
    shape = reduce_blocks(keep)
    middle = shape[0] // 2
    keep, near = keep.reshape(shape), near.reshape(shape)
    leaf = add_up(keep[:, 0, 1], near[:, 0, 1])
    leaf = jnp.concatenate([leaf[:middle], add_up(leaf[middle:], by_col)], axis=0).astype(BF16)
    along = add_up(keep[:, 1, 0], near[:, 1, 0])
    along = jnp.concatenate([add_up(along[:middle], by_leaf), along[middle:]], axis=0).astype(BF16)
    return leaf, along


def reduce_mine(keep, near, leaf, along):
    shape = reduce_blocks(keep)
    mine = add_up(keep.reshape(shape)[:, 0, 0], near.reshape(shape)[:, 0, 0], leaf, along)
    return [mine[n].astype(BF16) for n in range(shape[0])]


def send_rows(along):
    return [swap(block, "row", n) for n, block in enumerate(along) if n]


def norm_stats(values):
    center = jnp.mean(values, axis=0, keepdims=True)
    spread = jnp.mean(values * values, axis=0, keepdims=True) - center * center
    return center, lax.rsqrt(spread + EPSILON)


def norm_back(grad, normed, scale, gain):
    scaled = grad * gain
    return scale * (
        scaled
        - jnp.mean(scaled, axis=0, keepdims=True)
        - normed * jnp.mean(scaled * normed, axis=0, keepdims=True)
    )


def lane_sum(array):
    return jnp.sum(array, axis=-1, dtype=F32)


def on_device(
    tokens,
    memory,
    parents,
    memory_slots,
    query_weight,
    query_bias,
    key_weight,
    value_weight,
    value_bias,
    out_weight,
    out_bias,
    norm_gain,
    norm_shift,
    up_weight,
    up_bias,
    down_weight,
    down_bias,
    final_gain,
    final_shift,
    cotangent,
):
    rows, cols = lax.axis_size("row"), lax.axis_size("col")
    row, col = lax.axis_index("row"), lax.axis_index("col")
    feat, row_tokens = tokens.shape
    own = row_tokens // cols
    seg_row = row_tokens // SEG
    model = feat * cols
    width = query_weight.shape[1]
    hidden_width = up_weight.shape[1]
    bank = memory.shape[0]
    segments, ranges = plan_windows(own, cols)
    window = len(segments[0]) * SEG
    tail = 128
    lengths = tuple(min(SEG, own - j * SEG) for j in range(len(segments[0])))
    half = feat // 2
    parity = lax.axis_index("leaf") % 2
    here = jnp.stack([row, col, parity, jnp.int32(seg_row)]).astype(jnp.int32)
    blocks = [[b for a, n in ranges[i] for b in range(a // 128, (a + n) // 128)] for i in range(cols)]
    own_blocks = [each[: own // 128] for each in blocks]
    scalars = (here, parents, memory_slots)

    weight_half = pack_weights(
        here, query_weight, key_weight, value_weight, out_weight, up_weight, down_weight, up_bias, query_bias, value_bias
    )
    along = gather_weights(weight_half)

    vectors = (out_bias, norm_gain, norm_shift, down_bias, final_gain, final_shift)
    token_sends = pack(blocks, here, after(tokens, weight_half), memory, *vectors)
    cot_sends = pack(own_blocks, here, after(cotangent, token_sends))
    token_got = swap(token_sends[1], "col", 2)
    along = after(along, cot_sends)
    everything = lax.all_gather(after(tokens, along), "row", axis=0)
    row_vectors = jnp.stack([piece[3 * half :] for piece in along])
    first_parts = spread_weights([piece[:half][None] for piece in along])
    near_first, far_first = (array[0] for array in whole_weights(after(first_parts, token_got)))
    token_last = swap(jnp.concatenate([token_sends[2], token_got[1:]], axis=0), "col", 1)
    tok_window = joined((token_sends[0], token_got, token_last)).reshape(model, window + tail)
    win = project(near_first, far_first, tok_window, row_vectors, 0, 3 * width, width)
    partial = attend_own(lengths, segments, bank, scalars, win)
    second_parts = spread_weights([piece[half : 3 * half].reshape(2, half, -1) for piece in along], partial)
    cot_keep, cot_along, cot_near = after(cot_sends, second_parts[2])
    cot_got = swap(cot_along, "col", 2)
    cot_near = jnp.concatenate([cot_near, cot_got[1:]], axis=0)
    cot_pieces = cot_keep, cot_got, swap(cot_near, "col", 1)
    everything = after(everything, second_parts[2], cot_near)
    par_keep, par_along, par_near = pick_parents(segments, here, parents, everything)
    par_got = swap(par_along, "col", 2)
    near, far = whole_weights(after(second_parts, par_along))
    par_got = after(par_got, near)
    par_near = jnp.concatenate([par_near, par_got[1:]], axis=0)
    tok_parent = (par_keep, par_got, swap(par_near, "col", 1))
    par, ctx, lse = attend_parent(
        lengths, segments, scalars, win, partial, near_first, far_first, tok_parent, row_vectors
    )
    at = window + bank
    *result, active, upper_low, hidden_low, down_low, first_low, dctx, up_bias_grad, sums = mlp(
        at, ctx, tok_window, cot_pieces, near_first, far_first, near, far, row_vectors
    )
    result_keep, result_along, result_near = result
    dwin, dpar, par_keep, par_along, par_near = attend_back(
        lengths, segments, bank, scalars, win, par, ctx, dctx, lse, near_first, far_first
    )

    par_got = swap(par_along, "col", 2)
    down_keep, down_send, up_keep, up_send = hidden_grads(after(down_low, par_along), hidden_low, active, upper_low)
    down_near, up_near = swap(down_send, "col", 1), swap(up_send, "col", 1)
    par_got = after(par_got, up_send)
    par_near = jnp.concatenate([par_near, par_got[1:]], axis=0)
    placed = add_parents(segments, here, parents, (par_keep, par_got, swap(par_near, "col", 1)), rows, seg_row)
    down_across = reduce_across(after(down_keep, placed), down_near)
    up_along = reduce_y(after(up_keep, down_across), up_near)
    first_keep, first_send = first_grads(
        tok_window, tok_parent, dwin, dpar, after(first_low, up_along), ctx, up_bias_grad, sums
    )
    placed = lax.psum_scatter(placed, "row", scatter_dimension=0, tiled=False)
    first_near = swap(first_send, "col", 1)
    dtok = token_grads(near_first, far_first, dwin, after(first_low, first_send), window)
    corner = reduce_corner(after(first_keep, dtok), first_near)
    by_leaf, by_col = swap(corner[0], "leaf", 1), swap(corner[1], "col", 2)
    up_got = swap(up_along, "col", 2)
    up_across = reduce_x(after(up_keep, corner), up_near, up_got)
    down_across = swap(down_across, "leaf", 1)
    down_up = reduce_up(after(down_keep, up_across), down_near, down_across)
    edges = reduce_edges(after(first_keep, down_up), first_near, by_leaf, by_col)
    by_leaf, by_col = swap(edges[0], "leaf", 1), swap(edges[1], "col", 2)
    up_across = swap(up_across, "leaf", 1)
    up_rows = reduce_mine(after(up_keep, edges), up_near, up_got[:, 0], up_across)
    down_up = swap(down_up, "col", 2)
    down_rows = reduce_along(after(down_keep, up_rows), down_near, down_across, down_up)
    result_got = after(swap(result_along, "col", 2), down_rows)
    result_near = jnp.concatenate([result_near, result_got[1:]], axis=0)
    result_pieces = result_keep, result_got, swap(result_near, "col", 1)
    first_rows = reduce_mine(after(first_keep, down_rows), first_near, by_leaf, by_col)
    dtok_keep, dtok_along, dtok_near = dtok
    dtok_got = after(swap(after(dtok_along, edges), "col", 2), first_rows, result_near)
    dtok_near = jnp.concatenate([dtok_near, dtok_got[1:]], axis=0)
    layer_output = place(own_blocks, here, result_pieces, row_tokens)
    mem_sum = placed[:, row_tokens : row_tokens + bank].astype(F32)
    memory_grad = jnp.where(parity == 0, mem_sum, jnp.roll(mem_sum, half, axis=0)).T
    tokens_grad = finish_tokens(
        blocks, here, placed, (dtok_keep, dtok_got, swap(dtok_near, "col", 1)), row_tokens
    )
    down_got, up_got, first_got = send_rows(down_rows), send_rows(up_rows), send_rows(first_rows)
    down_rows, up_rows = after((down_rows, up_rows), first_rows)
    second_mine = jnp.concatenate([reduce_rows(down_rows, down_got), reduce_rows(up_rows, up_got)], axis=1)
    second_other = swap(second_mine, "leaf", 1)
    first_mine = reduce_rows(after(first_rows, second_mine, tokens_grad, memory_grad, layer_output), first_got)
    first_other = swap(first_mine, "leaf", 1)

    def in_order(mine, other):
        return jnp.where(
            parity == 0, jnp.concatenate([mine, other], axis=0), jnp.concatenate([other, mine], axis=0)
        ).astype(F32)

    second_total = in_order(second_mine, second_other)
    down_total, up_total = second_total[:, :hidden_width], second_total[:, hidden_width:]
    count = (2 * width + hidden_width) // half
    first_query, first_key, first_value, first_out, vectors = unpack(here, first_mine, first_other, width, count + 6)
    by_row = vectors[:count, :half].reshape(-1)
    by_col = vectors[count : count + 6]

    return (
        layer_output,
        tokens_grad,
        memory_grad,
        first_query,
        by_row[:width],
        first_key,
        first_value,
        by_row[width : 2 * width],
        first_out,
        by_col[0],
        by_col[1],
        by_col[2],
        up_total,
        by_row[2 * width :],
        down_total,
        by_col[3],
        by_col[4],
        by_col[5],
    )


def solution(mesh):
    return jax.shard_map(
        on_device,
        mesh=mesh,
        in_specs=(
            P("col", ("leaf", "row")),
            P("leaf", "col"),
            P("leaf"),
            P("leaf", None),
            P("col", "row"),
            P("row"),
            P("col", "row"),
            P("col", "row"),
            P("row"),
            P("row", "col"),
            P("col"),
            P("col"),
            P("col"),
            P("col", "row"),
            P("row"),
            P("col", "row"),
            P("col"),
            P("col"),
            P("col"),
            P("col", ("leaf", "row")),
        ),
        out_specs=(
            P("col", ("leaf", "row")),
            P("col", ("leaf", "row")),
            P("leaf", "col"),
            P("col", "row"),
            P("row"),
            P("col", "row"),
            P("col", "row"),
            P("row"),
            P("row", "col"),
            P("col"),
            P("col"),
            P("col"),
            P("col", "row"),
            P("row"),
            P("col", "row"),
            P("col"),
            P("col"),
            P("col"),
        ),
        check_vma=False,
    )
```

```python
import functools

import jax
import jax.numpy as jnp
import numpy as np
from jax import lax
from jax.experimental import pallas as pl
from jax.experimental.pallas import tpu as pltpu
from jax.sharding import PartitionSpec as P

HEAD = 64
SEG = 256
NEGATIVE = -1e30
EPSILON = 1e-05
EVERY = ("leaf", "row", "col")
BF16 = jnp.bfloat16
F32 = jnp.float32


def after(value, *others):
    return lax.optimization_barrier((value, others))[0]


def tn(left, right):
    return lax.dot_general(left, right, (((0,), (0,)), ((), ())), preferred_element_type=F32)


def nt(left, right):
    return lax.dot_general(left, right, (((1,), (1,)), ((), ())), preferred_element_type=F32)


def nn(left, right):
    return lax.dot_general(left, right, (((1,), (0,)), ((), ())), preferred_element_type=F32)


def plan_windows(own, count):
    segments, ranges = [], []
    for index in range(count):
        first, last = index * own, (index + 1) * own
        whole = [s for s in range(first // SEG, -(-last // SEG)) if s * SEG >= first and (s + 1) * SEG <= last]
        cut = [s for s in range(first // SEG, -(-last // SEG)) if s not in whole]
        pieces = [(s * SEG, SEG) for s in whole]
        for s in cut:
            low, high = max(first, s * SEG), min(last, (s + 1) * SEG)
            pieces.append((low, high - low))
            if low > s * SEG:
                pieces.append((s * SEG, low - s * SEG))
            if high < (s + 1) * SEG:
                pieces.append((high, (s + 1) * SEG - high))
        segments.append(whole + cut)
        ranges.append(pieces)
    return segments, ranges


def static_of(index, values):
    out = jnp.int32(values[0])
    for i, value in enumerate(values[1:], 1):
        out = jnp.where(index == i, jnp.int32(value), out)
    return out


def own_segments(segments, here_ref):
    return [
        here_ref[0] * here_ref[3] + static_of(here_ref[1], [lists[j] for lists in segments])
        for j in range(len(segments[0]))
    ]


def window_biases(segments, bank, here_ref, parents_ref, slots_ref):
    rows = lax.broadcasted_iota(jnp.int32, (bank, 1), 0)
    out = []
    for seg in own_segments(segments, here_ref):
        count = jnp.zeros((bank, 1), F32)
        for m in range(slots_ref.shape[1]):
            count = count + jnp.where(rows == slots_ref[seg, m], 1.0, 0.0)
        slot = jnp.where(count > 0, jnp.log(jnp.maximum(count, 1.0)), NEGATIVE)
        out.append((jnp.where(parents_ref[seg] >= 0, 0.0, NEGATIVE).astype(F32), slot))
    return out


def attention_own(
    head_count, lengths, segments, bank, here_ref, parents_ref, slots_ref, win_ref, mixed_ref, top_ref, total_ref
):
    width = head_count * HEAD
    window = len(lengths) * SEG
    biases = window_biases(segments, bank, here_ref, parents_ref, slots_ref)
    for head in range(head_count):
        low = head * HEAD
        key_mem = win_ref[0, width + low : width + low + HEAD, window : window + bank]
        value_mem = win_ref[0, 2 * width + low : 2 * width + low + HEAD, window : window + bank]
        for j, count in enumerate(lengths):
            cols = slice(j * SEG, (j + 1) * SEG)
            toks = slice(j * SEG, j * SEG + count)
            query = win_ref[0, low : low + HEAD, toks]
            own = tn(win_ref[0, width + low : width + low + HEAD, cols], query)
            mem = tn(key_mem, query) + biases[j][1]
            top = jnp.maximum(jnp.max(own, axis=0, keepdims=True), jnp.max(mem, axis=0, keepdims=True))
            own, mem = jnp.exp(own - top), jnp.exp(mem - top)
            mixed_ref[0, low : low + HEAD, toks] = nn(
                win_ref[0, 2 * width + low : 2 * width + low + HEAD, cols], own.astype(BF16)
            ) + nn(value_mem, mem.astype(BF16))
            top_ref[0, head : head + 1, toks] = top
            total_ref[0, head : head + 1, toks] = jnp.sum(own, axis=0, keepdims=True) + jnp.sum(
                mem, axis=0, keepdims=True
            )


def attention_parent(
    head_count,
    lengths,
    segments,
    here_ref,
    parents_ref,
    win_ref,
    mixed_ref,
    top_ref,
    total_ref,
    turned_ref,
    par_keep,
    par_got,
    par_last,
    bias_ref,
    par_ref,
    ctx_ref,
    lse_ref,
    toks_ref,
):
    width = head_count * HEAD
    join_pieces((par_keep, par_got, par_last), toks_ref)
    both = nn(turned_ref[0], toks_ref[...])
    par_ref[0] = (both + across_lanes(bias_ref[0], 1, width, 3 * width, both.shape[1])).astype(BF16)
    biases = [jnp.where(parents_ref[seg] >= 0, 0.0, NEGATIVE).astype(F32) for seg in own_segments(segments, here_ref)]
    for head in range(head_count):
        low = head * HEAD
        for j, count in enumerate(lengths):
            cols = slice(j * SEG, (j + 1) * SEG)
            toks = slice(j * SEG, j * SEG + count)
            par = tn(par_ref[0, low : low + HEAD, cols], win_ref[0, low : low + HEAD, toks]) + biases[j]
            first = top_ref[0, head : head + 1, toks]
            top = jnp.maximum(first, jnp.max(par, axis=0, keepdims=True))
            par = jnp.exp(par - top)
            scale = jnp.exp(first - top)
            total = total_ref[0, head : head + 1, toks] * scale + jnp.sum(par, axis=0, keepdims=True)
            mixed = mixed_ref[0, low : low + HEAD, toks] * scale
            mixed = mixed + nn(par_ref[0, width + low : width + low + HEAD, cols], par.astype(BF16))
            ctx_ref[0, low : low + HEAD, toks] = (mixed / total).astype(BF16)
            lse_ref[0, head : head + 1, toks] = top + jnp.log(total)


def attention_backward(
    head_count,
    lengths,
    segments,
    bank,
    here_ref,
    parents_ref,
    slots_ref,
    win_ref,
    par_ref,
    ctx_ref,
    dctx_ref,
    lse_ref,
    near_ref,
    far_ref,
    dwin_ref,
    dpar_ref,
    keep_ref,
    along_ref,
    close_ref,
    total_ref,
):
    width = head_count * HEAD
    biases = window_biases(segments, bank, here_ref, parents_ref, slots_ref)
    window = len(lengths) * SEG
    tail = win_ref.shape[2] - window
    for head in range(head_count):
        low = head * HEAD
        qs, ks, vs = (slice(part * width + low, part * width + low + HEAD) for part in range(3))
        key_mem = win_ref[0, ks, window : window + bank]
        value_mem = win_ref[0, vs, window : window + bank]
        dkey_mem = jnp.zeros((HEAD, bank), F32)
        dvalue_mem = jnp.zeros((HEAD, bank), F32)
        for j, count in enumerate(lengths):
            cols = slice(j * SEG, (j + 1) * SEG)
            tok = slice(j * SEG, j * SEG + count)
            query = win_ref[0, qs, tok]
            dctx = dctx_ref[0, low : low + HEAD, tok]
            lse = lse_ref[0, head : head + 1, tok]
            key_own, value_own = win_ref[0, ks, cols], win_ref[0, vs, cols]
            key_par, value_par = par_ref[0, low : low + HEAD, cols], par_ref[0, width + low : width + low + HEAD, cols]
            own = jnp.exp(tn(key_own, query) - lse)
            par = jnp.exp(tn(key_par, query) + biases[j][0] - lse)
            mem = jnp.exp(tn(key_mem, query) + biases[j][1] - lse)
            gown, gpar, gmem = tn(value_own, dctx), tn(value_par, dctx), tn(value_mem, dctx)
            ctx = ctx_ref[0, low : low + HEAD, tok].astype(F32)
            inner = jnp.sum(ctx * dctx.astype(F32), axis=0, keepdims=True)
            gown = (own * (gown - inner)).astype(BF16)
            gpar = (par * (gpar - inner)).astype(BF16)
            gmem = (mem * (gmem - inner)).astype(BF16)
            dquery = nn(key_own, gown) + nn(key_par, gpar) + nn(key_mem, gmem)
            dwin_ref[0, qs, tok] = (dquery * HEAD ** (-0.5)).astype(BF16)
            if count < SEG:
                dwin_ref[0, qs, j * SEG + count : (j + 1) * SEG] = jnp.zeros((HEAD, SEG - count), BF16)
            dwin_ref[0, ks, cols] = nt(query, gown).astype(BF16)
            dwin_ref[0, vs, cols] = nt(dctx, own.astype(BF16)).astype(BF16)
            dpar_ref[0, low : low + HEAD, cols] = nt(query, gpar).astype(BF16)
            dpar_ref[0, width + low : width + low + HEAD, cols] = nt(dctx, par.astype(BF16)).astype(BF16)
            dkey_mem += nt(query, gmem)
            dvalue_mem += nt(dctx, mem.astype(BF16))
        pad = jnp.zeros((HEAD, tail - bank), F32)
        dwin_ref[0, qs, window:] = jnp.zeros((HEAD, tail), BF16)
        dwin_ref[0, ks, window:] = jnp.concatenate([dkey_mem, pad], axis=1).astype(BF16)
        dwin_ref[0, vs, window:] = jnp.concatenate([dvalue_mem, pad], axis=1).astype(BF16)

    step, last = pl.program_id(0), pl.num_programs(0) - 1
    depth = near_ref.shape[1]
    grads = jnp.concatenate([dpar_ref[0], dwin_ref[0, width:, window:]], axis=1)
    near, far = nn(near_ref[0, :, width : 3 * width], grads), nn(far_ref[0, :, width : 3 * width], grads)

    @pl.when(step == 0)
    def begin():
        total_ref[:depth], total_ref[depth:] = near, far

    @pl.when(step > 0)
    def add():
        total_ref[:depth] += near
        total_ref[depth:] += far

    @pl.when(step == last)
    def finish():
        feat = keep_ref.shape[1]
        for i, out in enumerate((keep_ref.at[0], along_ref.at[0], close_ref.at[0], along_ref.at[1])):
            out[...] = total_ref[i * feat : (i + 1) * feat].astype(BF16)


def step_block(array):
    return pl.BlockSpec((1,) + array.shape[1:], lambda step, *_: (step, 0, 0))


def whole_block(array):
    return pl.BlockSpec(array.shape, lambda step, *_: (0,) * len(array.shape))


def cost(microseconds):
    return pl.CostEstimate(flops=int(microseconds * 1.0e9), bytes_accessed=0, transcendentals=0)


def held(*arrays):
    return tuple(pltpu.with_memory_space_constraint(array, pltpu.HBM) for array in arrays)


def in_hbm(shape):
    return pltpu.HBM(shape.shape, shape.dtype)


def params(mib):
    return pltpu.CompilerParams(vmem_limit_bytes=mib << 20)


def across_lanes(rows, index, low, high, columns):
    chosen = (lax.broadcasted_iota(jnp.int32, (rows.shape[0], 128), 0) == index).astype(BF16)
    column = tn(rows[:, low:high] if high - low < rows.shape[1] else rows, chosen)
    return jnp.concatenate([column] * (columns // 128), axis=1)


def join_pieces(refs, toks_ref):
    @pl.when(pl.program_id(0) == 0)
    def join():
        feat = refs[0].shape[1]
        for i, (piece, place) in enumerate(PIECES):
            toks_ref[i * feat : (i + 1) * feat] = refs[piece][place]


def project_kernel(low, high, scaled, near_ref, far_ref, *refs):
    depth = near_ref.shape[1]
    if len(refs) > 3:
        toks_ref, bias_ref, out_ref = refs[5], refs[3], refs[4]
        join_pieces(refs[:3], toks_ref)
    else:
        toks_ref, bias_ref, out_ref = refs
    out = tn(near_ref[0, :, low:high], toks_ref[:depth]) + tn(far_ref[0, :, low:high], toks_ref[depth:])
    out = (out + across_lanes(bias_ref[0], 1, low, high, out.shape[1])).astype(BF16)
    if scaled:
        out_ref[0, :scaled] = out[:scaled] * jnp.asarray(HEAD ** (-0.5), BF16)
        out_ref[0, scaled:] = out[scaled:]
    else:
        out_ref[0] = out


def project(near, far, toks, bias, low, high, scaled):
    groups, depth = near.shape[:2]
    pieces = toks if isinstance(toks, tuple) else (toks,)
    out = jax.ShapeDtypeStruct((groups, high - low, pieces[0].shape[-1]), BF16)
    return pl.pallas_call(
        functools.partial(project_kernel, low, high, scaled),
        grid=(groups,),
        in_specs=[step_block(near), step_block(far), *[whole_block(piece) for piece in pieces], step_block(bias)],
        scratch_shapes=[pltpu.VMEM((2 * depth, pieces[0].shape[-1]), BF16)] if len(pieces) > 1 else [],
        out_specs=step_block(out),
        out_shape=out,
        compiler_params=params(12),
        cost_estimate=cost(0.1),
        name="project",
    )(near, far, *pieces, bias)


def chunks(columns):
    return columns // 128


def mlp_kernel(
    at,
    ctx_ref,
    win_ref,
    cot_keep,
    cot_got,
    cot_last,
    near_first,
    far_first,
    near_ref,
    far_ref,
    bias_ref,
    keep_ref,
    along_ref,
    close_ref,
    active_ref,
    upper_ref,
    hidden_ref,
    low_ref,
    first_low_ref,
    dctx_ref,
    up_sum_ref,
    sums_ref,
    total_ref,
    wide_ref,
    parts_ref,
    normed_ref,
    scale_ref,
    slope_ref,
    columns_ref,
    out_ref,
    weights_ref,
    sem,
):
    step, groups = pl.program_id(0), slope_ref.shape[0]
    depth, width = near_ref.shape[2:]
    model, own = total_ref.shape
    feat = keep_ref.shape[1]
    heads = ctx_ref.shape[1]
    skip = out_ref.shape[3] - heads

    def weight_copies(block):
        return [
            pltpu.make_async_copy(
                source.at[which, block], weights_ref.at[which, side, block], sem.at[2 + 4 * block + 2 * which + side]
            )
            for which in range(2)
            for side, source in enumerate((near_ref, far_ref))
        ]

    first_copies = [
        pltpu.make_async_copy(
            source.at[:, :, pl.ds(width - out_ref.shape[3], out_ref.shape[3])], out_ref.at[side], sem.at[side]
        )
        for side, source in enumerate((near_first, far_first))
    ]

    def over_columns(body):
        def run(i, carry):
            body(pl.ds(pl.multiple_of(i * 128, 128), 128))
            return carry

        lax.fori_loop(0, own // 128, run, 0)

    def sum_parts(first):
        for i in range(3):
            sums_ref[:, first + i : first + i + 1] = jnp.sum(parts_ref[i], axis=1, keepdims=True)
        parts_ref[...] = jnp.zeros(parts_ref.shape, F32)

    @pl.when(step == 0)
    def start():
        for copy in first_copies:
            copy.start()
        for block in range(groups):
            for copy in weight_copies(block):
                copy.start()
        for i in range(6):
            columns_ref[i] = jnp.broadcast_to(win_ref[:, at + i : at + i + 1].astype(F32), (model, 128))
        parts_ref[...] = jnp.zeros(parts_ref.shape, F32)
        for copy in first_copies:
            copy.wait()
        for n in range(groups):
            near, far = nn(out_ref[0, n, :, skip:], ctx_ref[n]), nn(out_ref[1, n, :, skip:], ctx_ref[n])
            if n == 0:
                total_ref[:depth], total_ref[depth:] = near, far
            else:
                total_ref[:depth] += near
                total_ref[depth:] += far

        def body(cols):
            values = total_ref[:, cols] + columns_ref[0] + win_ref[:, cols].astype(F32)
            center, scale = norm_stats(values)
            normed = (values - center) * scale
            hidden = normed * columns_ref[1] + columns_ref[2]
            normed_ref[:, cols] = normed
            scale_ref[:, cols] = scale
            wide_ref[:, cols] = hidden
            hidden_ref[:, cols] = hidden.astype(BF16)

        over_columns(body)
        total_ref[...] = jnp.zeros(total_ref.shape, F32)

    @pl.when(step < groups)
    def forward():
        for block in range(groups):

            @pl.when(step == block)
            def arrive(block=block):
                for copy in weight_copies(block):
                    copy.wait()

        piece = width // 3
        for low in range(0, width, piece):
            rows = slice(low, low + piece)
            upper = tn(weights_ref[0, 0, step, :, rows], hidden_ref[:depth])
            upper = upper + tn(weights_ref[0, 1, step, :, rows], hidden_ref[depth:])
            upper = upper + across_lanes(bias_ref[0], 0, low, low + piece, own)
            phi = 0.5 * (1.0 + lax.erf(upper * np.float32(0.5**0.5)))
            active_ref[0, rows] = (upper * phi).astype(BF16)
            slope_ref[step, rows] = (
                phi + upper * jnp.exp(-0.5 * upper * upper) * np.float32(1.0 / np.sqrt(2.0 * np.pi))
            ).astype(BF16)
        active = active_ref[0]
        total_ref[:depth] += nn(weights_ref[1, 0, step], active)
        total_ref[depth:] += nn(weights_ref[1, 1, step], active)

    @pl.when(step == groups - 1)
    def turn():
        pieces = (cot_keep, cot_got, cot_last)

        def body(cols):
            values = total_ref[:, cols] + columns_ref[3] + wide_ref[:, cols]
            center, scale = norm_stats(values)
            normed = (values - center) * scale
            result = (normed * columns_ref[4] + columns_ref[5]).astype(BF16)
            keep_ref[0, :, cols] = result[:feat]
            along_ref[0, :, cols] = result[feat : 2 * feat]
            close_ref[0, :, cols] = result[2 * feat : 3 * feat]
            along_ref[1, :, cols] = result[3 * feat :]
            cot = jnp.concatenate([pieces[i][j, :, cols] for i, j in PIECES], axis=0).astype(F32)
            grad = norm_back(cot, normed, scale, columns_ref[4])
            total_ref[:, cols] = grad
            grad_low = grad.astype(BF16)
            low_ref[:, cols] = grad_low
            parts_ref[0] += grad_low.astype(F32)
            parts_ref[1] += cot * normed
            parts_ref[2] += cot

        over_columns(body)
        sum_parts(3)

    @pl.when(step >= groups)
    def backward():
        block = step - groups
        upper = tn(weights_ref[1, 0, block], low_ref[:depth]) + tn(weights_ref[1, 1, block], low_ref[depth:])
        upper = (upper * slope_ref[block].astype(F32)).astype(BF16)
        upper_ref[0] = upper
        up_sum_ref[0] = jnp.sum(upper.astype(F32), axis=1, keepdims=True)
        total_ref[:depth] += nn(weights_ref[0, 0, block], upper)
        total_ref[depth:] += nn(weights_ref[0, 1, block], upper)

    @pl.when(step == 2 * groups - 1)
    def finish():
        def body(cols):
            hidden_grad = total_ref[:, cols]
            normed = normed_ref[:, cols]
            first_low = norm_back(hidden_grad, normed, scale_ref[:, cols], columns_ref[1]).astype(BF16)
            first_low_ref[:, cols] = first_low
            parts_ref[0] += first_low.astype(F32)
            parts_ref[1] += hidden_grad * normed
            parts_ref[2] += hidden_grad

        over_columns(body)
        sum_parts(0)
        for n in range(groups):
            grads = tn(out_ref[0, n, :, skip:], first_low_ref[:depth]) + tn(out_ref[1, n, :, skip:], first_low_ref[depth:])
            dctx_ref[n] = grads.astype(BF16)


def once(array):
    return pl.BlockSpec(
        array.shape, lambda step, *_: (0,) * len(array.shape), pipeline_mode=pl.Buffered(1)
    )


def mlp(at, ctx, win, cot, near_first, far_first, near, far, bias):
    groups, depth, width = near.shape[1:]
    feat, own = cot[0].shape[1:]
    model = feat * 4
    out_columns = -(-ctx.shape[1] // 128) * 128

    def early(array):
        return pl.BlockSpec((1,) + array.shape[1:], lambda step, *_: (jnp.minimum(step, groups - 1), 0, 0))

    def late(array):
        return pl.BlockSpec((1,) + array.shape[1:], lambda step, *_: (jnp.maximum(step - groups, 0), 0, 0))

    outs = [
        jax.ShapeDtypeStruct((1, feat, own), BF16),
        jax.ShapeDtypeStruct((2, feat, own), BF16),
        jax.ShapeDtypeStruct((1, feat, own), BF16),
        jax.ShapeDtypeStruct((groups, width, own), BF16),
        jax.ShapeDtypeStruct((groups, width, own), BF16),
        jax.ShapeDtypeStruct((model, own), BF16),
        jax.ShapeDtypeStruct((model, own), BF16),
        jax.ShapeDtypeStruct((model, own), BF16),
        jax.ShapeDtypeStruct(ctx.shape, BF16),
        jax.ShapeDtypeStruct((groups, width, 1), F32),
        jax.ShapeDtypeStruct((model, 6), F32),
    ]
    return pl.pallas_call(
        functools.partial(mlp_kernel, at),
        grid=(2 * groups,),
        in_specs=[
            once(ctx),
            once(win),
            *[once(piece) for piece in cot],
            HBM,
            HBM,
            HBM,
            HBM,
            pl.BlockSpec((1,) + bias.shape[1:], lambda step, *_: (jnp.minimum(step, groups - 1), 0, 0)),
        ],
        out_specs=[early(o) if i == 3 else late(o) if i in (4, 9) else once(o) for i, o in enumerate(outs)],
        out_shape=[in_hbm(o) if i in (3, 4, 5, 6, 7) else o for i, o in enumerate(outs)],
        scratch_shapes=[
            pltpu.VMEM((model, own), F32),
            pltpu.VMEM((model, own), F32),
            pltpu.VMEM((3, model, 128), F32),
            pltpu.VMEM((model, own), F32),
            pltpu.VMEM((1, own), F32),
            pltpu.VMEM((groups, width, own), BF16),
            pltpu.VMEM((6, model, 128), F32),
            pltpu.VMEM((2, groups, depth, out_columns), BF16),
            pltpu.VMEM((2, 2, groups, depth, width), BF16),
            pltpu.SemaphoreType.DMA((2 + 4 * groups,)),
        ],
        compiler_params=params(44),
        cost_estimate=cost(400),
        name="mlp",
    )(ctx, win, *cot, near_first, far_first, near, far, bias)


def hidden_grad_kernel(low_ref, hidden_ref, active_ref, upper_ref, down_keep, down_send, up_keep, up_send):
    depth = down_keep.shape[1]
    for keep, send, left, right in (
        (down_keep, down_send, low_ref, active_ref),
        (up_keep, up_send, hidden_ref, upper_ref),
    ):
        keep[0] = nt(left[:depth], right[0]).astype(BF16)
        send[0] = nt(left[depth:], right[0]).astype(BF16)


def hidden_grads(low, hidden, active, upper):
    groups, width, own = active.shape
    out = jax.ShapeDtypeStruct((groups, low.shape[0] // 2, width), BF16)
    return pl.pallas_call(
        hidden_grad_kernel,
        grid=(groups,),
        in_specs=[whole_block(low), whole_block(hidden), step_block(active), step_block(upper)],
        out_specs=[step_block(out)] * 4,
        out_shape=[in_hbm(out)] * 4,
        compiler_params=params(14),
        cost_estimate=cost(100),
        name="hidden_grads",
    )(*held(low, hidden, active, upper))


def first_grad_kernel(
    width,
    win_ref,
    par_keep,
    par_got,
    par_last,
    dwin_ref,
    dpar_ref,
    low_ref,
    ctx_ref,
    up_ref,
    sums_ref,
    keep_ref,
    send_ref,
    par_ref,
):
    join_pieces((par_keep, par_got, par_last), par_ref)
    depth = keep_ref.shape[1]
    half = depth // 4
    query = jnp.sum(dwin_ref[0, :width].astype(F32), axis=1, keepdims=True)
    value = jnp.sum(dwin_ref[0, 2 * width :].astype(F32), axis=1, keepdims=True)
    value = value + jnp.sum(dpar_ref[0, width:].astype(F32), axis=1, keepdims=True)
    by_row = [array[i : i + half] for array in (query, value, up_ref[0]) for i in range(0, array.shape[0], half)]
    by_row = jnp.concatenate(by_row, axis=1)
    by_row = jnp.concatenate([by_row] * 4, axis=0)
    used = by_row.shape[1] + 6
    pad = jnp.zeros((depth, keep_ref.shape[2] - 4 * width - used), F32)
    for part, out_ref in enumerate((keep_ref, send_ref)):
        rows = slice(part * depth, (part + 1) * depth)
        win, par = win_ref[rows], par_ref[rows]
        out_ref[0, :, :width] = nt(win, dwin_ref[0, :width]).astype(BF16)
        for i in range(1, 3):
            grads = nt(win, dwin_ref[0, i * width : (i + 1) * width])
            grads = grads + nt(par, dpar_ref[0, (i - 1) * width : i * width])
            out_ref[0, :, i * width : (i + 1) * width] = grads.astype(BF16)
        out_ref[0, :, 3 * width : 4 * width] = nt(low_ref[rows], ctx_ref[0]).astype(BF16)
        extra = jnp.concatenate([by_row, sums_ref[rows], pad], axis=1)
        out_ref[0, :, 4 * width :] = extra.astype(BF16)


def first_grads(win, par, dwin, dpar, low, ctx, up_bias, sums):
    groups, width, own = ctx.shape
    out = jax.ShapeDtypeStruct((groups, low.shape[0] // 2, 4 * width + 128), BF16)
    return pl.pallas_call(
        functools.partial(first_grad_kernel, width),
        grid=(groups,),
        in_specs=[
            whole_block(win),
            *[whole_block(piece) for piece in par],
            step_block(dwin),
            step_block(dpar),
            whole_block(low),
            step_block(ctx),
            step_block(up_bias),
            whole_block(sums),
        ],
        out_specs=[step_block(out)] * 2,
        out_shape=[out] * 2,
        scratch_shapes=[pltpu.VMEM((low.shape[0], par[0].shape[2]), BF16)],
        compiler_params=params(16),
        cost_estimate=cost(15),
        name="first_grads",
    )(*held(win, *par, dwin, dpar, low, ctx), up_bias, sums)


def token_grad_kernel(high, near_ref, far_ref, dwin_ref, more_ref, keep_ref, along_ref, close_ref, total_ref):
    step, last = pl.program_id(0), pl.num_programs(0) - 1
    depth = near_ref.shape[1]
    own = more_ref.shape[1]

    @pl.when(step == 0)
    def start():
        total_ref[...] = jnp.zeros(total_ref.shape, F32)
        total_ref[:, :own] = more_ref[...].astype(F32)

    grads = dwin_ref[0]
    total_ref[:depth] += nn(near_ref[0, :, :high], grads)
    total_ref[depth:] += nn(far_ref[0, :, :high], grads)

    @pl.when(step == last)
    def finish():
        feat = keep_ref.shape[1]
        for i, out in enumerate((keep_ref.at[0], along_ref.at[0], close_ref.at[0], along_ref.at[1])):
            out[...] = total_ref[i * feat : (i + 1) * feat].astype(BF16)


def token_grads(near, far, dwin, more, columns):
    groups, depth = near.shape[:2]
    feat = depth // 2
    outs = [jax.ShapeDtypeStruct((n, feat, columns), BF16) for n in (1, 2, 1)]
    return pl.pallas_call(
        functools.partial(token_grad_kernel, dwin.shape[1]),
        grid=(groups,),
        in_specs=[
            step_block(near),
            step_block(far),
            pl.BlockSpec((1, dwin.shape[1], columns), lambda step: (step, 0, 0)),
            whole_block(more),
        ],
        out_specs=[whole_block(out) for out in outs],
        out_shape=outs,
        scratch_shapes=[pltpu.VMEM((2 * depth, columns), F32)],
        compiler_params=params(14),
        cost_estimate=cost(30),
        name="token_grads",
    )(near, far, dwin, more)


def turn_kernel(low, near_ref, far_ref, out_ref):
    depth = near_ref.shape[1]
    out_ref[0, :, :depth] = tn(near_ref[0, :, low : low + out_ref.shape[1]], spots(depth, depth, 0)).astype(BF16)
    out_ref[0, :, depth:] = tn(far_ref[0, :, low : low + out_ref.shape[1]], spots(depth, depth, 0)).astype(BF16)


def turn_weights(near, far, low, count):
    groups, depth = near.shape[:2]
    out = jax.ShapeDtypeStruct((groups, count, 2 * depth), BF16)
    return pl.pallas_call(
        functools.partial(turn_kernel, low),
        grid=(groups,),
        in_specs=[step_block(near), step_block(far)],
        out_specs=step_block(out),
        out_shape=out,
        compiler_params=params(12),
        cost_estimate=cost(0.1),
        name="turn_weights",
    )(near, far)


def attend_own(lengths, segments, bank, scalars, window):
    groups, rows, columns = window.shape
    width = rows // 3
    own = sum(lengths)
    outs = (
        jax.ShapeDtypeStruct((groups, width, own), F32),
        jax.ShapeDtypeStruct((groups, width // HEAD, own), F32),
        jax.ShapeDtypeStruct((groups, width // HEAD, own), F32),
    )
    return pl.pallas_call(
        functools.partial(attention_own, width // HEAD, lengths, segments, bank),
        grid=(groups,),
        in_specs=[SMEM] * 3 + [step_block(window)],
        out_specs=[step_block(out) for out in outs],
        out_shape=outs,
        compiler_params=params(14),
        cost_estimate=cost(0.1),
        name="attention_own",
    )(*scalars, window)


def attend_parent(lengths, segments, scalars, window, partial, turned, toks, bias):
    groups, rows, columns = window.shape
    width = rows // 3
    model = turned.shape[2]
    outs = (
        jax.ShapeDtypeStruct((groups, 2 * width, toks[0].shape[2]), BF16),
        jax.ShapeDtypeStruct((groups, width, sum(lengths)), BF16),
        jax.ShapeDtypeStruct((groups, width // HEAD, sum(lengths)), F32),
    )
    return pl.pallas_call(
        functools.partial(attention_parent, width // HEAD, lengths, segments),
        grid=(groups,),
        in_specs=[SMEM] * 2
        + [step_block(array) for array in (window, *partial, turned)]
        + [whole_block(piece) for piece in toks]
        + [step_block(bias)],
        out_specs=[step_block(out) for out in outs],
        out_shape=[in_hbm(outs[0]), *outs[1:]],
        scratch_shapes=[pltpu.VMEM((model, toks[0].shape[2]), BF16)],
        compiler_params=params(18),
        cost_estimate=cost(130),
        name="attention_parent",
    )(*scalars[:2], window, *partial, turned, *toks, bias)


def attend_back(lengths, segments, bank, scalars, window, parent, ctx, dctx, lse, near, far):
    groups, rows, columns = window.shape
    depth = near.shape[1]
    feat = depth // 2
    outs = (jax.ShapeDtypeStruct(window.shape, BF16), jax.ShapeDtypeStruct(parent.shape, BF16))
    sends = [jax.ShapeDtypeStruct((n, feat, columns), BF16) for n in (1, 2, 1)]
    return pl.pallas_call(
        functools.partial(attention_backward, rows // 3 // HEAD, lengths, segments, bank),
        grid=(groups,),
        in_specs=[SMEM] * 3 + [step_block(array) for array in (window, parent, ctx, dctx, lse, near, far)],
        out_specs=[step_block(out) for out in outs] + [whole_block(out) for out in sends],
        out_shape=[*map(in_hbm, outs), *sends],
        scratch_shapes=[pltpu.VMEM((2 * depth, columns), F32)],
        compiler_params=params(24),
        cost_estimate=cost(200),
        name="attention_backward",
    )(*scalars, *held(window, parent, ctx), dctx, lse, *held(near, far))


def swap(array, axis, mask):
    count = lax.axis_size(axis)
    return lax.ppermute(array, axis, [(i, i ^ mask) for i in range(count)])


SMEM = pl.BlockSpec(memory_space=pltpu.SMEM)
VMEM = pl.BlockSpec(memory_space=pltpu.VMEM)
HBM = pl.BlockSpec(memory_space=pltpu.HBM)
ORDER = (0, 2, 1, 3)
SENDS = ((0, 0), (1, 0), (2, 0), (1, 1))


def at_distance(here_ref, lists, slot, j):
    distance = ORDER[slot]
    return static_of(here_ref[1], [lists[i ^ distance][j] for i in range(len(lists))])


def flipped(here_ref, part, half):
    return pl.multiple_of((part ^ here_ref[2]) * half, 32)


def spots(rows, columns, shift):
    return (
        lax.broadcasted_iota(jnp.int32, (rows, columns), 0) + shift
        == lax.broadcasted_iota(jnp.int32, (rows, columns), 1)
    ).astype(BF16)


def as_row(ref):
    return ref[...].astype(F32).reshape(1, ref.shape[0])


def fetch(pairs, sem):
    copies = [pltpu.make_async_copy(source, target, sem.at[i]) for i, (source, target) in enumerate(pairs)]
    for copy in copies:
        copy.start()
    for copy in copies:
        copy.wait()


def pack_weights_kernel(here_ref, *refs):
    count = 9
    inputs, half_ref = refs[:count], refs[count]
    held, turned_ref, sem = refs[count + 1 : -2], refs[-2], refs[-1]
    feat, width = inputs[0].shape
    half = feat // 2
    rows = pl.ds(flipped(here_ref, 0, half), half)
    small = [inputs[i] for i in (0, 1, 2, 3, 6, 7, 8)]
    fetch(
        [*zip(small, held)]
        + [(inputs[4 + i].at[rows, :], half_ref.at[pl.ds((1 + i) * half, half), :]) for i in range(2)],
        sem,
    )
    query_ref, key_ref, value_ref, out_ref, up_b_ref, query_b_ref, value_b_ref = held
    turned_ref[...] = tn(out_ref[...], spots(width, width, 0)).astype(BF16)
    for i, ref in enumerate((query_ref, key_ref, value_ref, turned_ref)):
        half_ref[:half, i * width : (i + 1) * width] = ref[rows, :]
    zero = jnp.zeros((1, width), F32)
    joint = [as_row(query_b_ref), zero, as_row(value_b_ref), zero]
    wide = (half_ref.shape[0] - 3 * half, half_ref.shape[1])
    index = lax.broadcasted_iota(jnp.int32, wide, 0)
    up_row = jnp.broadcast_to(as_row(up_b_ref), wide)
    joint_row = jnp.broadcast_to(jnp.concatenate(joint, axis=1), wide)
    half_ref[3 * half :] = jnp.where(index == 0, up_row, jnp.where(index == 1, joint_row, 0.0)).astype(BF16)


def pack_weights(here, query, key, value, out, up, down, *biases):
    feat, width = query.shape
    hidden = up.shape[1]
    inputs = (query, key, value, out, up, down, *biases)
    small = [query, key, value, out, *biases]
    return pl.pallas_call(
        pack_weights_kernel,
        in_specs=[SMEM] + [HBM] * len(inputs),
        out_specs=VMEM,
        out_shape=jax.ShapeDtypeStruct((3 * feat // 2 + 8, hidden), BF16),
        scratch_shapes=[pltpu.VMEM(array.shape, array.dtype) for array in small]
        + [pltpu.VMEM((feat, width), BF16), pltpu.SemaphoreType.DMA((len(inputs),))],
        compiler_params=params(6),
        cost_estimate=cost(0.1),
        name="pack_weights",
    )(here, *held(*inputs))


def pack_kernel(blocks, sided, here_ref, *refs):
    given = 1 + sided
    outs, held, sem = refs[given : given + 3], refs[given + 3 : given + 3 + given], refs[-1]
    fetch([*zip(refs[:given], held)], sem)
    source_ref = held[0]
    half = source_ref.shape[0] // 2
    count = len(blocks[0])
    if sided:
        mem_ref, vector_refs, side_ref = held[1], held[2:], refs[-2]
        bank = mem_ref.shape[0]
        vectors = jnp.concatenate([as_row(ref) for ref in vector_refs], axis=0)
        vectors = jnp.concatenate([vectors, jnp.zeros((8 - len(vector_refs), vectors.shape[1]), F32)], axis=0)
        side = tn(mem_ref[...], spots(bank, 128, 0)) + tn(vectors.astype(BF16), spots(8, 128, bank))
        side_ref[...] = side.astype(BF16)
    for slot, (out, place) in enumerate(SENDS):
        for part in range(2):
            low = flipped(here_ref, part, half)
            rows = slice(part * half, (part + 1) * half)
            for j in range(count):
                at = pl.multiple_of(at_distance(here_ref, blocks, slot, j) * 128, 128)
                outs[out][place, rows, j * 128 : (j + 1) * 128] = source_ref[pl.ds(low, half), pl.ds(at, 128)]
            if sided:
                outs[out][place, rows, count * 128 :] = side_ref[pl.ds(low, half), :]


def pack(blocks, here, source, *side):
    feat = source.shape[0]
    columns = len(blocks[0]) * 128 + (128 if side else 0)
    inputs = (source, *side)
    return pl.pallas_call(
        functools.partial(pack_kernel, blocks, len(side)),
        in_specs=[SMEM] + [HBM] * len(inputs),
        out_specs=[VMEM] * 3,
        out_shape=[jax.ShapeDtypeStruct((n, feat, columns), source.dtype) for n in (1, 2, 1)],
        scratch_shapes=[pltpu.VMEM(array.shape, array.dtype) for array in inputs]
        + ([pltpu.VMEM((feat, 128), BF16)] if side else [])
        + [pltpu.SemaphoreType.DMA((len(inputs),))],
        compiler_params=params(12),
        cost_estimate=cost(0.1),
        name="pack",
    )(here, *held(*inputs))


def exchange(keep, along, near):
    got = swap(along, "col", 2)
    return keep, got, swap(jnp.concatenate([near, got[1:]], axis=0), "col", 1)


def joined(pieces):
    keep, got, last = pieces
    return jnp.concatenate([keep, got[:1], last], axis=0)


PIECES = ((0, 0), (1, 0), (2, 0), (2, 1))


def parent_of(here_ref, parents_ref, segments, slot, j):
    return parents_ref[here_ref[0] * here_ref[3] + at_distance(here_ref, segments, slot, j)]


def pick_kernel(segments, here_ref, parents_ref, source_ref, *refs):
    outs, sem = refs[:3], refs[3]
    half = source_ref.shape[1] // 2
    seg_row = here_ref[3]
    pairs = []
    for slot, (out, place) in enumerate(SENDS):
        for j in range(len(segments[0])):
            seg = jnp.maximum(parent_of(here_ref, parents_ref, segments, slot, j), 0)
            row = lax.div(seg, seg_row)
            at = pl.multiple_of((seg - row * seg_row) * SEG, SEG)
            for part in range(2):
                rows = slice(part * half, (part + 1) * half)
                source = source_ref.at[row, pl.ds(flipped(here_ref, part, half), half), pl.ds(at, SEG)]
                pairs.append((source, outs[out].at[place, rows, pl.ds(j * SEG, SEG)]))
    fetch(pairs, sem)


def pick_parents(segments, here, parents, gathered):
    feat = gathered.shape[1]
    columns = len(segments[0]) * SEG
    return pl.pallas_call(
        functools.partial(pick_kernel, segments),
        in_specs=[SMEM, SMEM, HBM],
        out_specs=[VMEM] * 3,
        out_shape=[jax.ShapeDtypeStruct((n, feat, columns), gathered.dtype) for n in (1, 2, 1)],
        scratch_shapes=[pltpu.SemaphoreType.DMA((8 * len(segments[0]),))],
        compiler_params=params(8),
        cost_estimate=cost(1),
        name="pick_parents",
    )(here, parents, *held(gathered))


def add_parents_kernel(segments, seg_row, here_ref, parents_ref, *refs):
    pieces, given_ref, sum_ref, out_ref, sem = refs[:3], refs[3], refs[4], refs[5], refs[6]
    window = len(segments[0]) * SEG
    copies = []
    sum_ref[...] = jnp.zeros(sum_ref.shape, F32)
    for slot, (piece, place) in enumerate(PIECES):
        for j in range(len(segments[0])):
            seg = parent_of(here_ref, parents_ref, segments, slot, j)

            @pl.when(seg >= 0)
            def add(seg=seg, piece=piece, place=place, cols=slice(j * SEG, (j + 1) * SEG)):
                sum_ref[seg] += pieces[piece][place, :, cols].astype(F32)

    mem = sum(pieces[piece][place, :, window:].astype(F32) for piece, place in PIECES)
    for r in range(out_ref.shape[0]):
        for s in range(seg_row):
            out_ref[r, :, s * SEG : (s + 1) * SEG] = sum_ref[r * seg_row + s].astype(BF16)
        out_ref[r, :, seg_row * SEG :] = mem.astype(BF16)
        copies.append(pltpu.make_async_copy(out_ref.at[r], given_ref.at[r], sem.at[r]))
        copies[-1].start()
    for copy in copies:
        copy.wait()


def add_parents(segments, here, parents, pieces, rows, seg_row):
    feat, columns = pieces[0].shape[1:]
    bank = columns - len(segments[0]) * SEG
    return pl.pallas_call(
        functools.partial(add_parents_kernel, segments, seg_row),
        in_specs=[SMEM, SMEM, VMEM, VMEM, VMEM],
        out_specs=HBM,
        out_shape=pltpu.HBM((rows, feat, seg_row * SEG + bank), BF16),
        scratch_shapes=[
            pltpu.VMEM((rows * seg_row, feat, SEG), F32),
            pltpu.VMEM((rows, feat, seg_row * SEG + bank), BF16),
            pltpu.SemaphoreType.DMA((rows,)),
        ],
        compiler_params=params(28),
        cost_estimate=cost(60),
        name="add_parents",
    )(here, parents, *pieces)


def finish_kernel(blocks, here_ref, placed_ref, *refs):
    pieces, out_ref = refs[:3], refs[3]
    half = out_ref.shape[0] // 2
    for part in range(2):
        low = flipped(here_ref, part, half)
        rows = slice(part * half, (part + 1) * half)
        out_ref[pl.ds(low, half), :] = placed_ref[rows, : out_ref.shape[1]].astype(F32)
        for slot, (piece, place) in enumerate(PIECES):
            for j in range(len(blocks[0])):
                at = pl.multiple_of(at_distance(here_ref, blocks, slot, j) * 128, 128)
                out_ref[pl.ds(low, half), pl.ds(at, 128)] += pieces[piece][
                    place, rows, j * 128 : (j + 1) * 128
                ].astype(F32)


def finish_tokens(blocks, here, placed, pieces, columns):
    return pl.pallas_call(
        functools.partial(finish_kernel, blocks),
        in_specs=[SMEM, VMEM, VMEM, VMEM, VMEM],
        out_specs=VMEM,
        out_shape=jax.ShapeDtypeStruct((placed.shape[0], columns), F32),
        compiler_params=params(10),
        cost_estimate=cost(2.5),
        name="finish_tokens",
    )(here, placed, *pieces)


def place_kernel(blocks, here_ref, *refs):
    pieces, out_ref = refs[:3], refs[3]
    half = out_ref.shape[0] // 2
    for part in range(2):
        low = flipped(here_ref, part, half)
        rows = slice(part * half, (part + 1) * half)
        for slot, (piece, place) in enumerate(PIECES):
            for j in range(pieces[0].shape[2] // 128):
                at = pl.multiple_of(at_distance(here_ref, blocks, slot, j) * 128, 128)
                out_ref[pl.ds(low, half), pl.ds(at, 128)] = pieces[piece][place, rows, j * 128 : (j + 1) * 128]


def place(blocks, here, pieces, columns):
    return pl.pallas_call(
        functools.partial(place_kernel, blocks),
        in_specs=[SMEM, VMEM, VMEM, VMEM],
        out_specs=VMEM,
        out_shape=jax.ShapeDtypeStruct((pieces[0].shape[1], columns), pieces[0].dtype),
        compiler_params=params(6),
        cost_estimate=cost(1.7),
        name="place",
    )(here, *pieces)


def unpack_kernel(width, count, here_ref, mine_ref, other_ref, *refs):
    weights, out_ref, by_row, by_col, all_ref = refs[:3], refs[3], refs[4:7], refs[7:13], refs[13]
    half = mine_ref.shape[0]
    all_ref[pl.ds(flipped(here_ref, 0, half), half), :] = mine_ref[...].astype(F32)
    all_ref[pl.ds(flipped(here_ref, 1, half), half), :] = other_ref[...].astype(F32)
    for i, ref in enumerate(weights):
        ref[...] = all_ref[:, i * width : (i + 1) * width]
    out_ref[...] = all_ref[:, 3 * width : 4 * width].T
    rows = all_ref[:, 4 * width :].T
    flat = jnp.concatenate([rows[i : i + 1, :half] for i in range(count)], axis=1)
    at = 0
    for ref in by_row:
        size = ref.shape[0]
        ref[...] = flat[:, at : at + size].reshape(size)
        at += size
    for i, ref in enumerate(by_col):
        ref[...] = rows[count + i : count + i + 1].reshape(ref.shape[0])


def unpack(here, mine, other, width, hidden):
    feat = 2 * mine.shape[0]
    count = (2 * width + hidden) // mine.shape[0]
    shapes = [(feat, width)] * 3 + [(width, feat)] + [(width,), (width,), (hidden,)] + [(feat,)] * 6
    return pl.pallas_call(
        functools.partial(unpack_kernel, width, count),
        in_specs=[SMEM, VMEM, VMEM],
        out_specs=[VMEM] * len(shapes),
        out_shape=[jax.ShapeDtypeStruct(shape, F32) for shape in shapes],
        scratch_shapes=[pltpu.VMEM((feat, mine.shape[1]), F32)],
        compiler_params=params(4),
        cost_estimate=cost(2),
        name="unpack",
    )(here, mine, other)


def gather_weights(half):
    return [half] + [swap(half, "row", n) for n in range(1, lax.axis_size("row"))]


def spread_weights(along, *gate):
    along = jnp.stack(along, axis=1)
    opposite = swap(along, "leaf", 1)
    across = after(swap(along, "col", 2), *gate)
    return along, opposite, across, swap(across, "leaf", 1)


def whole_weights(parts):
    near = jnp.stack(parts, axis=2)
    arrays, rows, blocks, depth, columns = near.shape
    near = near.reshape(arrays, rows, blocks * depth, columns)
    return near, swap(near, "col", 1)


def add_up(*terms):
    total = terms[0].astype(F32)
    for term in terms[1:]:
        total = total + term.astype(F32)
    return total


def reduce_blocks(keep):
    rows, features, columns = keep.shape
    return rows, 2, 2, features // 4, columns


def reduce_across(keep, near):
    shape = reduce_blocks(keep)
    return add_up(keep.reshape(shape)[:, :, 1], near.reshape(shape)[:, :, 1]).astype(BF16)


def reduce_y(keep, near):
    shape = reduce_blocks(keep)
    return add_up(keep.reshape(shape)[:, 1], near.reshape(shape)[:, 1]).astype(BF16)


def reduce_x(keep, near, got):
    shape = reduce_blocks(keep)
    return add_up(keep.reshape(shape)[:, 0, 1], near.reshape(shape)[:, 0, 1], got[:, 1]).astype(BF16)


def reduce_up(keep, near, across):
    shape = reduce_blocks(keep)
    return add_up(keep.reshape(shape)[:, 1, 0], near.reshape(shape)[:, 1, 0], across[:, 1]).astype(BF16)


def reduce_along(keep, near, across, up):
    shape = reduce_blocks(keep)
    mine = add_up(keep.reshape(shape)[:, 0, 0], near.reshape(shape)[:, 0, 0], across[:, 0], up)
    return [mine[n].astype(BF16) for n in range(shape[0])]


def reduce_rows(along, got):
    total = add_up(along[0], *got)
    mask = 2
    while mask < lax.axis_size("leaf"):
        total = add_up(total, swap(total.astype(BF16), "leaf", mask))
        mask *= 2
    return total.astype(BF16)


def reduce_corner(keep, near):
    shape = reduce_blocks(keep)
    middle = shape[0] // 2
    corner = add_up(keep.reshape(shape)[:, 1, 1], near.reshape(shape)[:, 1, 1]).astype(BF16)
    return corner[:middle], corner[middle:]


def reduce_edges(keep, near, by_leaf, by_col):
    shape = reduce_blocks(keep)
    middle = shape[0] // 2
    keep, near = keep.reshape(shape), near.reshape(shape)
    leaf = add_up(keep[:, 0, 1], near[:, 0, 1])
    leaf = jnp.concatenate([leaf[:middle], add_up(leaf[middle:], by_col)], axis=0).astype(BF16)
    along = add_up(keep[:, 1, 0], near[:, 1, 0])
    along = jnp.concatenate([add_up(along[:middle], by_leaf), along[middle:]], axis=0).astype(BF16)
    return leaf, along


def reduce_mine(keep, near, leaf, along):
    shape = reduce_blocks(keep)
    mine = add_up(keep.reshape(shape)[:, 0, 0], near.reshape(shape)[:, 0, 0], leaf, along)
    return [mine[n].astype(BF16) for n in range(shape[0])]


def send_rows(along):
    return [swap(block, "row", n) for n, block in enumerate(along) if n]


def norm_stats(values):
    center = jnp.mean(values, axis=0, keepdims=True)
    spread = jnp.mean(values * values, axis=0, keepdims=True) - center * center
    return center, lax.rsqrt(spread + EPSILON)


def norm_back(grad, normed, scale, gain):
    scaled = grad * gain
    return scale * (
        scaled
        - jnp.mean(scaled, axis=0, keepdims=True)
        - normed * jnp.mean(scaled * normed, axis=0, keepdims=True)
    )


def lane_sum(array):
    return jnp.sum(array, axis=-1, dtype=F32)


def on_device(
    tokens,
    memory,
    parents,
    memory_slots,
    query_weight,
    query_bias,
    key_weight,
    value_weight,
    value_bias,
    out_weight,
    out_bias,
    norm_gain,
    norm_shift,
    up_weight,
    up_bias,
    down_weight,
    down_bias,
    final_gain,
    final_shift,
    cotangent,
):
    rows, cols = lax.axis_size("row"), lax.axis_size("col")
    row, col = lax.axis_index("row"), lax.axis_index("col")
    feat, row_tokens = tokens.shape
    own = row_tokens // cols
    seg_row = row_tokens // SEG
    model = feat * cols
    width = query_weight.shape[1]
    hidden_width = up_weight.shape[1]
    bank = memory.shape[0]
    segments, ranges = plan_windows(own, cols)
    window = len(segments[0]) * SEG
    tail = 128
    lengths = tuple(min(SEG, own - j * SEG) for j in range(len(segments[0])))
    half = feat // 2
    parity = lax.axis_index("leaf") % 2
    here = jnp.stack([row, col, parity, jnp.int32(seg_row)]).astype(jnp.int32)
    blocks = [[b for a, n in ranges[i] for b in range(a // 128, (a + n) // 128)] for i in range(cols)]
    own_blocks = [each[: own // 128] for each in blocks]
    scalars = (here, parents, memory_slots)

    weight_half = pack_weights(
        here, query_weight, key_weight, value_weight, out_weight, up_weight, down_weight, up_bias, query_bias, value_bias
    )
    along = gather_weights(weight_half)

    vectors = (out_bias, norm_gain, norm_shift, down_bias, final_gain, final_shift)
    token_sends = pack(blocks, here, after(tokens, weight_half), memory, *vectors)
    cot_sends = pack(own_blocks, here, after(cotangent, token_sends))
    token_got = swap(token_sends[1], "col", 2)
    along = after(along, cot_sends)
    everything = lax.all_gather(after(tokens, along), "row", axis=0)
    row_vectors = jnp.stack([piece[3 * half :] for piece in along])
    first_parts = spread_weights([piece[:half][None] for piece in along])
    near_first, far_first = (array[0] for array in whole_weights(after(first_parts, token_got)))
    token_last = swap(jnp.concatenate([token_sends[2], token_got[1:]], axis=0), "col", 1)
    tok_window = joined((token_sends[0], token_got, token_last)).reshape(model, window + tail)
    win = project(near_first, far_first, tok_window, row_vectors, 0, 3 * width, width)
    partial = attend_own(lengths, segments, bank, scalars, win)
    second_parts = spread_weights([piece[half : 3 * half].reshape(2, half, -1) for piece in along], partial)
    cot_keep, cot_along, cot_near = after(cot_sends, second_parts[2])
    cot_got = swap(cot_along, "col", 2)
    cot_near = jnp.concatenate([cot_near, cot_got[1:]], axis=0)
    cot_pieces = cot_keep, cot_got, swap(cot_near, "col", 1)
    turned = turn_weights(after(near_first, second_parts[2]), far_first, width, 2 * width)
    everything = after(everything, second_parts[2], cot_near, turned)
    par_keep, par_along, par_near = pick_parents(segments, here, parents, everything)
    par_got = swap(par_along, "col", 2)
    near, far = whole_weights(after(second_parts, par_along))
    par_got = after(par_got, near)
    par_near = jnp.concatenate([par_near, par_got[1:]], axis=0)
    tok_parent = (par_keep, par_got, swap(par_near, "col", 1))
    par, ctx, lse = attend_parent(
        lengths, segments, scalars, win, partial, turned, tok_parent, row_vectors
    )
    at = window + bank
    *result, active, upper_low, hidden_low, down_low, first_low, dctx, up_bias_grad, sums = mlp(
        at, ctx, tok_window, cot_pieces, near_first, far_first, near, far, row_vectors
    )
    result_keep, result_along, result_near = result
    dwin, dpar, par_keep, par_along, par_near = attend_back(
        lengths, segments, bank, scalars, win, par, ctx, dctx, lse, near_first, far_first
    )

    par_got = swap(par_along, "col", 2)
    down_keep, down_send, up_keep, up_send = hidden_grads(after(down_low, par_along), hidden_low, active, upper_low)
    down_near, up_near = swap(down_send, "col", 1), swap(up_send, "col", 1)
    par_got = after(par_got, up_send)
    par_near = jnp.concatenate([par_near, par_got[1:]], axis=0)
    placed = add_parents(segments, here, parents, (par_keep, par_got, swap(par_near, "col", 1)), rows, seg_row)
    down_across = reduce_across(after(down_keep, placed), down_near)
    up_along = reduce_y(after(up_keep, down_across), up_near)
    first_keep, first_send = first_grads(
        tok_window, tok_parent, dwin, dpar, after(first_low, up_along), ctx, up_bias_grad, sums
    )
    placed = lax.psum_scatter(placed, "row", scatter_dimension=0, tiled=False)
    first_near = swap(first_send, "col", 1)
    dtok = token_grads(near_first, far_first, dwin, after(first_low, first_send), window)
    corner = reduce_corner(after(first_keep, dtok), first_near)
    by_leaf, by_col = swap(corner[0], "leaf", 1), swap(corner[1], "col", 2)
    up_got = swap(up_along, "col", 2)
    up_across = reduce_x(after(up_keep, corner), up_near, up_got)
    down_across = swap(down_across, "leaf", 1)
    down_up = reduce_up(after(down_keep, up_across), down_near, down_across)
    edges = reduce_edges(after(first_keep, down_up), first_near, by_leaf, by_col)
    by_leaf, by_col = swap(edges[0], "leaf", 1), swap(edges[1], "col", 2)
    up_across = swap(up_across, "leaf", 1)
    up_rows = reduce_mine(after(up_keep, edges), up_near, up_got[:, 0], up_across)
    down_up = swap(down_up, "col", 2)
    down_rows = reduce_along(after(down_keep, up_rows), down_near, down_across, down_up)
    result_got = after(swap(result_along, "col", 2), down_rows)
    result_near = jnp.concatenate([result_near, result_got[1:]], axis=0)
    result_pieces = result_keep, result_got, swap(result_near, "col", 1)
    first_rows = reduce_mine(after(first_keep, down_rows), first_near, by_leaf, by_col)
    dtok_keep, dtok_along, dtok_near = dtok
    dtok_got = after(swap(after(dtok_along, edges), "col", 2), first_rows, result_near)
    dtok_near = jnp.concatenate([dtok_near, dtok_got[1:]], axis=0)
    layer_output = place(own_blocks, here, result_pieces, row_tokens)
    mem_sum = placed[:, row_tokens : row_tokens + bank].astype(F32)
    memory_grad = jnp.where(parity == 0, mem_sum, jnp.roll(mem_sum, half, axis=0)).T
    tokens_grad = finish_tokens(
        blocks, here, placed, (dtok_keep, dtok_got, swap(dtok_near, "col", 1)), row_tokens
    )
    down_got, up_got, first_got = send_rows(down_rows), send_rows(up_rows), send_rows(first_rows)
    down_rows, up_rows = after((down_rows, up_rows), first_rows)
    second_mine = jnp.concatenate([reduce_rows(down_rows, down_got), reduce_rows(up_rows, up_got)], axis=1)
    second_other = swap(second_mine, "leaf", 1)
    first_mine = reduce_rows(after(first_rows, second_mine, tokens_grad, memory_grad, layer_output), first_got)
    first_other = swap(first_mine, "leaf", 1)

    def in_order(mine, other):
        return jnp.where(
            parity == 0, jnp.concatenate([mine, other], axis=0), jnp.concatenate([other, mine], axis=0)
        ).astype(F32)

    second_total = in_order(second_mine, second_other)
    down_total, up_total = second_total[:, :hidden_width], second_total[:, hidden_width:]
    first_query, first_key, first_value, first_out, query_sum, value_sum, up_sum, *by_col = unpack(
        here, first_mine, first_other, width, hidden_width
    )

    return (
        layer_output,
        tokens_grad,
        memory_grad,
        first_query,
        query_sum,
        first_key,
        first_value,
        value_sum,
        first_out,
        by_col[0],
        by_col[1],
        by_col[2],
        up_total,
        up_sum,
        down_total,
        by_col[3],
        by_col[4],
        by_col[5],
    )


def solution(mesh):
    return jax.shard_map(
        on_device,
        mesh=mesh,
        in_specs=(
            P("col", ("leaf", "row")),
            P("leaf", "col"),
            P("leaf"),
            P("leaf", None),
            P("col", "row"),
            P("row"),
            P("col", "row"),
            P("col", "row"),
            P("row"),
            P("row", "col"),
            P("col"),
            P("col"),
            P("col"),
            P("col", "row"),
            P("row"),
            P("col", "row"),
            P("col"),
            P("col"),
            P("col"),
            P("col", ("leaf", "row")),
        ),
        out_specs=(
            P("col", ("leaf", "row")),
            P("col", ("leaf", "row")),
            P("leaf", "col"),
            P("col", "row"),
            P("row"),
            P("col", "row"),
            P("col", "row"),
            P("row"),
            P("row", "col"),
            P("col"),
            P("col"),
            P("col"),
            P("col", "row"),
            P("row"),
            P("col", "row"),
            P("col"),
            P("col"),
            P("col"),
        ),
        check_vma=False,
    )
```

```python
import functools

import jax
import jax.numpy as jnp
import numpy as np
from jax import lax
from jax.experimental import pallas as pl
from jax.experimental.pallas import tpu as pltpu
from jax.sharding import PartitionSpec as P

HEAD = 64
SEG = 256
NEGATIVE = -1e30
EPSILON = 1e-05
EVERY = ("leaf", "row", "col")
BF16 = jnp.bfloat16
F32 = jnp.float32


def after(value, *others):
    return lax.optimization_barrier((value, others))[0]


def tn(left, right):
    return lax.dot_general(left, right, (((0,), (0,)), ((), ())), preferred_element_type=F32)


def nt(left, right):
    return lax.dot_general(left, right, (((1,), (1,)), ((), ())), preferred_element_type=F32)


def nn(left, right):
    return lax.dot_general(left, right, (((1,), (0,)), ((), ())), preferred_element_type=F32)


def plan_windows(own, count):
    segments, ranges = [], []
    for index in range(count):
        first, last = index * own, (index + 1) * own
        whole = [s for s in range(first // SEG, -(-last // SEG)) if s * SEG >= first and (s + 1) * SEG <= last]
        cut = [s for s in range(first // SEG, -(-last // SEG)) if s not in whole]
        pieces = [(s * SEG, SEG) for s in whole]
        for s in cut:
            low, high = max(first, s * SEG), min(last, (s + 1) * SEG)
            pieces.append((low, high - low))
            if low > s * SEG:
                pieces.append((s * SEG, low - s * SEG))
            if high < (s + 1) * SEG:
                pieces.append((high, (s + 1) * SEG - high))
        segments.append(whole + cut)
        ranges.append(pieces)
    return segments, ranges


def static_of(index, values):
    out = jnp.int32(values[0])
    for i, value in enumerate(values[1:], 1):
        out = jnp.where(index == i, jnp.int32(value), out)
    return out


def own_segments(segments, here_ref):
    return [
        here_ref[0] * here_ref[3] + static_of(here_ref[1], [lists[j] for lists in segments])
        for j in range(len(segments[0]))
    ]


def window_biases(segments, bank, here_ref, parents_ref, slots_ref):
    rows = lax.broadcasted_iota(jnp.int32, (bank, 1), 0)
    out = []
    for seg in own_segments(segments, here_ref):
        count = jnp.zeros((bank, 1), F32)
        for m in range(slots_ref.shape[1]):
            count = count + jnp.where(rows == slots_ref[seg, m], 1.0, 0.0)
        slot = jnp.where(count > 0, jnp.log(jnp.maximum(count, 1.0)), NEGATIVE)
        out.append((jnp.where(parents_ref[seg] >= 0, 0.0, NEGATIVE).astype(F32), slot))
    return out


def attention_own(
    head_count, lengths, segments, bank, here_ref, parents_ref, slots_ref, win_ref, mixed_ref, top_ref, total_ref
):
    width = head_count * HEAD
    window = len(lengths) * SEG
    biases = window_biases(segments, bank, here_ref, parents_ref, slots_ref)
    for head in range(head_count):
        low = head * HEAD
        key_mem = win_ref[0, width + low : width + low + HEAD, window : window + bank]
        value_mem = win_ref[0, 2 * width + low : 2 * width + low + HEAD, window : window + bank]
        for j, count in enumerate(lengths):
            cols = slice(j * SEG, (j + 1) * SEG)
            toks = slice(j * SEG, j * SEG + count)
            query = win_ref[0, low : low + HEAD, toks]
            own = tn(win_ref[0, width + low : width + low + HEAD, cols], query)
            mem = tn(key_mem, query) + biases[j][1]
            top = jnp.maximum(jnp.max(own, axis=0, keepdims=True), jnp.max(mem, axis=0, keepdims=True))
            own, mem = jnp.exp(own - top), jnp.exp(mem - top)
            mixed_ref[0, low : low + HEAD, toks] = nn(
                win_ref[0, 2 * width + low : 2 * width + low + HEAD, cols], own.astype(BF16)
            ) + nn(value_mem, mem.astype(BF16))
            top_ref[0, head : head + 1, toks] = top
            total_ref[0, head : head + 1, toks] = jnp.sum(own, axis=0, keepdims=True) + jnp.sum(
                mem, axis=0, keepdims=True
            )


def attention_parent(
    head_count,
    lengths,
    segments,
    here_ref,
    parents_ref,
    win_ref,
    mixed_ref,
    top_ref,
    total_ref,
    turned_ref,
    par_keep,
    par_got,
    par_last,
    bias_ref,
    par_ref,
    ctx_ref,
    lse_ref,
    toks_ref,
):
    width = head_count * HEAD
    join_pieces((par_keep, par_got, par_last), toks_ref)
    both = nn(turned_ref[0], toks_ref[...])
    par_ref[0] = (both + across_lanes(bias_ref[0], 1, width, 3 * width, both.shape[1])).astype(BF16)
    biases = [jnp.where(parents_ref[seg] >= 0, 0.0, NEGATIVE).astype(F32) for seg in own_segments(segments, here_ref)]
    for head in range(head_count):
        low = head * HEAD
        for j, count in enumerate(lengths):
            cols = slice(j * SEG, (j + 1) * SEG)
            toks = slice(j * SEG, j * SEG + count)
            par = tn(par_ref[0, low : low + HEAD, cols], win_ref[0, low : low + HEAD, toks]) + biases[j]
            first = top_ref[0, head : head + 1, toks]
            top = jnp.maximum(first, jnp.max(par, axis=0, keepdims=True))
            par = jnp.exp(par - top)
            scale = jnp.exp(first - top)
            total = total_ref[0, head : head + 1, toks] * scale + jnp.sum(par, axis=0, keepdims=True)
            mixed = mixed_ref[0, low : low + HEAD, toks] * scale
            mixed = mixed + nn(par_ref[0, width + low : width + low + HEAD, cols], par.astype(BF16))
            ctx_ref[0, low : low + HEAD, toks] = (mixed / total).astype(BF16)
            lse_ref[0, head : head + 1, toks] = top + jnp.log(total)


def attention_backward(
    head_count,
    lengths,
    segments,
    bank,
    here_ref,
    parents_ref,
    slots_ref,
    win_ref,
    par_ref,
    ctx_ref,
    dctx_ref,
    lse_ref,
    near_ref,
    far_ref,
    dwin_ref,
    dpar_ref,
    keep_ref,
    along_ref,
    close_ref,
    total_ref,
):
    width = head_count * HEAD
    biases = window_biases(segments, bank, here_ref, parents_ref, slots_ref)
    window = len(lengths) * SEG
    tail = win_ref.shape[2] - window
    for head in range(head_count):
        low = head * HEAD
        qs, ks, vs = (slice(part * width + low, part * width + low + HEAD) for part in range(3))
        key_mem = win_ref[0, ks, window : window + bank]
        value_mem = win_ref[0, vs, window : window + bank]
        dkey_mem = jnp.zeros((HEAD, bank), F32)
        dvalue_mem = jnp.zeros((HEAD, bank), F32)
        for j, count in enumerate(lengths):
            cols = slice(j * SEG, (j + 1) * SEG)
            tok = slice(j * SEG, j * SEG + count)
            query = win_ref[0, qs, tok]
            dctx = dctx_ref[0, low : low + HEAD, tok]
            lse = lse_ref[0, head : head + 1, tok]
            key_own, value_own = win_ref[0, ks, cols], win_ref[0, vs, cols]
            key_par, value_par = par_ref[0, low : low + HEAD, cols], par_ref[0, width + low : width + low + HEAD, cols]
            own = jnp.exp(tn(key_own, query) - lse)
            par = jnp.exp(tn(key_par, query) + biases[j][0] - lse)
            mem = jnp.exp(tn(key_mem, query) + biases[j][1] - lse)
            gown, gpar, gmem = tn(value_own, dctx), tn(value_par, dctx), tn(value_mem, dctx)
            ctx = ctx_ref[0, low : low + HEAD, tok].astype(F32)
            inner = jnp.sum(ctx * dctx.astype(F32), axis=0, keepdims=True)
            gown = (own * (gown - inner)).astype(BF16)
            gpar = (par * (gpar - inner)).astype(BF16)
            gmem = (mem * (gmem - inner)).astype(BF16)
            dquery = nn(key_own, gown) + nn(key_par, gpar) + nn(key_mem, gmem)
            dwin_ref[0, qs, tok] = (dquery * HEAD ** (-0.5)).astype(BF16)
            if count < SEG:
                dwin_ref[0, qs, j * SEG + count : (j + 1) * SEG] = jnp.zeros((HEAD, SEG - count), BF16)
            dwin_ref[0, ks, cols] = nt(query, gown).astype(BF16)
            dwin_ref[0, vs, cols] = nt(dctx, own.astype(BF16)).astype(BF16)
            dpar_ref[0, low : low + HEAD, cols] = nt(query, gpar).astype(BF16)
            dpar_ref[0, width + low : width + low + HEAD, cols] = nt(dctx, par.astype(BF16)).astype(BF16)
            dkey_mem += nt(query, gmem)
            dvalue_mem += nt(dctx, mem.astype(BF16))
        pad = jnp.zeros((HEAD, tail - bank), F32)
        dwin_ref[0, qs, window:] = jnp.zeros((HEAD, tail), BF16)
        dwin_ref[0, ks, window:] = jnp.concatenate([dkey_mem, pad], axis=1).astype(BF16)
        dwin_ref[0, vs, window:] = jnp.concatenate([dvalue_mem, pad], axis=1).astype(BF16)

    step, last = pl.program_id(0), pl.num_programs(0) - 1
    depth = near_ref.shape[1]
    grads = jnp.concatenate([dpar_ref[0], dwin_ref[0, width:, window:]], axis=1)
    near, far = nn(near_ref[0, :, width : 3 * width], grads), nn(far_ref[0, :, width : 3 * width], grads)

    @pl.when(step == 0)
    def begin():
        total_ref[:depth], total_ref[depth:] = near, far

    @pl.when(step > 0)
    def add():
        total_ref[:depth] += near
        total_ref[depth:] += far

    @pl.when(step == last)
    def finish():
        feat = keep_ref.shape[1]
        for i, out in enumerate((keep_ref.at[0], along_ref.at[0], close_ref.at[0], along_ref.at[1])):
            out[...] = total_ref[i * feat : (i + 1) * feat].astype(BF16)


def step_block(array):
    return pl.BlockSpec((1,) + array.shape[1:], lambda step, *_: (step, 0, 0))


def whole_block(array):
    return pl.BlockSpec(array.shape, lambda step, *_: (0,) * len(array.shape))


def cost(microseconds):
    return pl.CostEstimate(flops=int(microseconds * 1.0e9), bytes_accessed=0, transcendentals=0)


def held(*arrays):
    return tuple(pltpu.with_memory_space_constraint(array, pltpu.HBM) for array in arrays)


def in_hbm(shape):
    return pltpu.HBM(shape.shape, shape.dtype)


def params(mib):
    return pltpu.CompilerParams(vmem_limit_bytes=mib << 20)


def across_lanes(rows, index, low, high, columns):
    chosen = (lax.broadcasted_iota(jnp.int32, (rows.shape[0], 128), 0) == index).astype(BF16)
    column = tn(rows[:, low:high] if high - low < rows.shape[1] else rows, chosen)
    return jnp.concatenate([column] * (columns // 128), axis=1)


def join_pieces(refs, toks_ref):
    @pl.when(pl.program_id(0) == 0)
    def join():
        feat = refs[0].shape[1]
        for i, (piece, place) in enumerate(PIECES):
            toks_ref[i * feat : (i + 1) * feat] = refs[piece][place]


def project_kernel(low, high, scaled, near_ref, far_ref, *refs):
    depth = near_ref.shape[1]
    if len(refs) > 3:
        toks_ref, bias_ref, out_ref = refs[5], refs[3], refs[4]
        join_pieces(refs[:3], toks_ref)
    else:
        toks_ref, bias_ref, out_ref = refs
    out = tn(near_ref[0, :, low:high], toks_ref[:depth]) + tn(far_ref[0, :, low:high], toks_ref[depth:])
    out = (out + across_lanes(bias_ref[0], 1, low, high, out.shape[1])).astype(BF16)
    if scaled:
        out_ref[0, :scaled] = out[:scaled] * jnp.asarray(HEAD ** (-0.5), BF16)
        out_ref[0, scaled:] = out[scaled:]
    else:
        out_ref[0] = out


def project(near, far, toks, bias, low, high, scaled):
    groups, depth = near.shape[:2]
    pieces = toks if isinstance(toks, tuple) else (toks,)
    out = jax.ShapeDtypeStruct((groups, high - low, pieces[0].shape[-1]), BF16)
    return pl.pallas_call(
        functools.partial(project_kernel, low, high, scaled),
        grid=(groups,),
        in_specs=[step_block(near), step_block(far), *[whole_block(piece) for piece in pieces], step_block(bias)],
        scratch_shapes=[pltpu.VMEM((2 * depth, pieces[0].shape[-1]), BF16)] if len(pieces) > 1 else [],
        out_specs=step_block(out),
        out_shape=out,
        compiler_params=params(12),
        cost_estimate=cost(0.1),
        name="project",
    )(near, far, *pieces, bias)


def chunks(columns):
    return columns // 128


def mlp_kernel(
    at,
    ctx_ref,
    win_ref,
    cot_keep,
    cot_got,
    cot_last,
    near_first,
    far_first,
    near_ref,
    far_ref,
    bias_ref,
    keep_ref,
    along_ref,
    close_ref,
    active_ref,
    upper_ref,
    hidden_ref,
    low_ref,
    first_low_ref,
    dctx_ref,
    up_sum_ref,
    sums_ref,
    total_ref,
    wide_ref,
    parts_ref,
    normed_ref,
    scale_ref,
    slope_ref,
    columns_ref,
    out_ref,
    weights_ref,
    sem,
):
    step, groups = pl.program_id(0), slope_ref.shape[0]
    depth, width = near_ref.shape[2:]
    model, own = total_ref.shape
    feat = keep_ref.shape[1]
    heads = ctx_ref.shape[1]
    skip = out_ref.shape[3] - heads

    def weight_copies(block):
        return [
            pltpu.make_async_copy(
                source.at[which, block], weights_ref.at[which, side, block], sem.at[2 + 4 * block + 2 * which + side]
            )
            for which in range(2)
            for side, source in enumerate((near_ref, far_ref))
        ]

    first_copies = [
        pltpu.make_async_copy(
            source.at[:, :, pl.ds(width - out_ref.shape[3], out_ref.shape[3])], out_ref.at[side], sem.at[side]
        )
        for side, source in enumerate((near_first, far_first))
    ]

    def over_columns(body):
        def run(i, carry):
            body(pl.ds(pl.multiple_of(i * 128, 128), 128))
            return carry

        lax.fori_loop(0, own // 128, run, 0)

    def sum_parts(first):
        for i in range(3):
            sums_ref[:, first + i : first + i + 1] = jnp.sum(parts_ref[i], axis=1, keepdims=True)
        parts_ref[...] = jnp.zeros(parts_ref.shape, F32)

    @pl.when(step == 0)
    def start():
        for copy in first_copies:
            copy.start()
        for block in range(groups):
            for copy in weight_copies(block):
                copy.start()
        for i in range(6):
            columns_ref[i] = jnp.broadcast_to(win_ref[:, at + i : at + i + 1].astype(F32), (model, 128))
        parts_ref[...] = jnp.zeros(parts_ref.shape, F32)
        for copy in first_copies:
            copy.wait()
        for n in range(groups):
            near, far = nn(out_ref[0, n, :, skip:], ctx_ref[n]), nn(out_ref[1, n, :, skip:], ctx_ref[n])
            if n == 0:
                total_ref[:depth], total_ref[depth:] = near, far
            else:
                total_ref[:depth] += near
                total_ref[depth:] += far

        def body(cols):
            values = total_ref[:, cols] + columns_ref[0] + win_ref[:, cols].astype(F32)
            center, scale = norm_stats(values)
            normed = (values - center) * scale
            hidden = normed * columns_ref[1] + columns_ref[2]
            normed_ref[:, cols] = normed
            scale_ref[:, cols] = scale
            wide_ref[:, cols] = hidden
            hidden_ref[:, cols] = hidden.astype(BF16)

        over_columns(body)
        total_ref[...] = jnp.zeros(total_ref.shape, F32)

    @pl.when(step < groups)
    def forward():
        for block in range(groups):

            @pl.when(step == block)
            def arrive(block=block):
                for copy in weight_copies(block):
                    copy.wait()

        piece = width // 3
        for low in range(0, width, piece):
            rows = slice(low, low + piece)
            upper = tn(weights_ref[0, 0, step, :, rows], hidden_ref[:depth])
            upper = upper + tn(weights_ref[0, 1, step, :, rows], hidden_ref[depth:])
            upper = upper + across_lanes(bias_ref[0], 0, low, low + piece, own)
            phi = 0.5 * (1.0 + lax.erf(upper * np.float32(0.5**0.5)))
            active_ref[0, rows] = (upper * phi).astype(BF16)
            slope_ref[step, rows] = (
                phi + upper * jnp.exp(-0.5 * upper * upper) * np.float32(1.0 / np.sqrt(2.0 * np.pi))
            ).astype(BF16)
        active = active_ref[0]
        total_ref[:depth] += nn(weights_ref[1, 0, step], active)
        total_ref[depth:] += nn(weights_ref[1, 1, step], active)

    @pl.when(step == groups - 1)
    def turn():
        pieces = (cot_keep, cot_got, cot_last)

        def body(cols):
            values = total_ref[:, cols] + columns_ref[3] + wide_ref[:, cols]
            center, scale = norm_stats(values)
            normed = (values - center) * scale
            result = (normed * columns_ref[4] + columns_ref[5]).astype(BF16)
            keep_ref[0, :, cols] = result[:feat]
            along_ref[0, :, cols] = result[feat : 2 * feat]
            close_ref[0, :, cols] = result[2 * feat : 3 * feat]
            along_ref[1, :, cols] = result[3 * feat :]
            cot = jnp.concatenate([pieces[i][j, :, cols] for i, j in PIECES], axis=0).astype(F32)
            grad = norm_back(cot, normed, scale, columns_ref[4])
            total_ref[:, cols] = grad
            grad_low = grad.astype(BF16)
            low_ref[:, cols] = grad_low
            parts_ref[0] += grad_low.astype(F32)
            parts_ref[1] += cot * normed
            parts_ref[2] += cot

        over_columns(body)
        sum_parts(3)

    @pl.when(step >= groups)
    def backward():
        block = step - groups
        upper = tn(weights_ref[1, 0, block], low_ref[:depth]) + tn(weights_ref[1, 1, block], low_ref[depth:])
        upper = (upper * slope_ref[block].astype(F32)).astype(BF16)
        upper_ref[0] = upper
        up_sum_ref[0] = jnp.sum(upper.astype(F32), axis=1, keepdims=True)
        total_ref[:depth] += nn(weights_ref[0, 0, block], upper)
        total_ref[depth:] += nn(weights_ref[0, 1, block], upper)

    @pl.when(step == 2 * groups - 1)
    def finish():
        def body(cols):
            hidden_grad = total_ref[:, cols]
            normed = normed_ref[:, cols]
            first_low = norm_back(hidden_grad, normed, scale_ref[:, cols], columns_ref[1]).astype(BF16)
            first_low_ref[:, cols] = first_low
            parts_ref[0] += first_low.astype(F32)
            parts_ref[1] += hidden_grad * normed
            parts_ref[2] += hidden_grad

        over_columns(body)
        sum_parts(0)
        for n in range(groups):
            grads = tn(out_ref[0, n, :, skip:], first_low_ref[:depth]) + tn(out_ref[1, n, :, skip:], first_low_ref[depth:])
            dctx_ref[n] = grads.astype(BF16)


def once(array):
    return pl.BlockSpec(
        array.shape, lambda step, *_: (0,) * len(array.shape), pipeline_mode=pl.Buffered(1)
    )


def mlp(at, ctx, win, cot, near_first, far_first, near, far, bias):
    groups, depth, width = near.shape[1:]
    feat, own = cot[0].shape[1:]
    model = feat * 4
    out_columns = -(-ctx.shape[1] // 128) * 128

    def early(array):
        return pl.BlockSpec((1,) + array.shape[1:], lambda step, *_: (jnp.minimum(step, groups - 1), 0, 0))

    def late(array):
        return pl.BlockSpec((1,) + array.shape[1:], lambda step, *_: (jnp.maximum(step - groups, 0), 0, 0))

    outs = [
        jax.ShapeDtypeStruct((1, feat, own), BF16),
        jax.ShapeDtypeStruct((2, feat, own), BF16),
        jax.ShapeDtypeStruct((1, feat, own), BF16),
        jax.ShapeDtypeStruct((groups, width, own), BF16),
        jax.ShapeDtypeStruct((groups, width, own), BF16),
        jax.ShapeDtypeStruct((model, own), BF16),
        jax.ShapeDtypeStruct((model, own), BF16),
        jax.ShapeDtypeStruct((model, own), BF16),
        jax.ShapeDtypeStruct(ctx.shape, BF16),
        jax.ShapeDtypeStruct((groups, width, 1), F32),
        jax.ShapeDtypeStruct((model, 6), F32),
    ]
    return pl.pallas_call(
        functools.partial(mlp_kernel, at),
        grid=(2 * groups,),
        in_specs=[
            once(ctx),
            once(win),
            *[once(piece) for piece in cot],
            HBM,
            HBM,
            HBM,
            HBM,
            pl.BlockSpec((1,) + bias.shape[1:], lambda step, *_: (jnp.minimum(step, groups - 1), 0, 0)),
        ],
        out_specs=[early(o) if i == 3 else late(o) if i in (4, 9) else once(o) for i, o in enumerate(outs)],
        out_shape=[in_hbm(o) if i in (3, 4, 5, 6, 7) else o for i, o in enumerate(outs)],
        scratch_shapes=[
            pltpu.VMEM((model, own), F32),
            pltpu.VMEM((model, own), F32),
            pltpu.VMEM((3, model, 128), F32),
            pltpu.VMEM((model, own), F32),
            pltpu.VMEM((1, own), F32),
            pltpu.VMEM((groups, width, own), BF16),
            pltpu.VMEM((6, model, 128), F32),
            pltpu.VMEM((2, groups, depth, out_columns), BF16),
            pltpu.VMEM((2, 2, groups, depth, width), BF16),
            pltpu.SemaphoreType.DMA((2 + 4 * groups,)),
        ],
        compiler_params=params(44),
        cost_estimate=cost(400),
        name="mlp",
    )(ctx, win, *cot, near_first, far_first, near, far, bias)


def hidden_grad_kernel(low_ref, hidden_ref, active_ref, upper_ref, down_keep, down_send, up_keep, up_send):
    depth = down_keep.shape[1]
    for keep, send, left, right in (
        (down_keep, down_send, low_ref, active_ref),
        (up_keep, up_send, hidden_ref, upper_ref),
    ):
        keep[0] = nt(left[:depth], right[0]).astype(BF16)
        send[0] = nt(left[depth:], right[0]).astype(BF16)


def hidden_grads(low, hidden, active, upper):
    groups, width, own = active.shape
    out = jax.ShapeDtypeStruct((groups, low.shape[0] // 2, width), BF16)
    return pl.pallas_call(
        hidden_grad_kernel,
        grid=(groups,),
        in_specs=[whole_block(low), whole_block(hidden), step_block(active), step_block(upper)],
        out_specs=[step_block(out)] * 4,
        out_shape=[in_hbm(out)] * 4,
        compiler_params=params(14),
        cost_estimate=cost(100),
        name="hidden_grads",
    )(*held(low, hidden, active, upper))


def first_grad_kernel(
    width,
    win_ref,
    par_keep,
    par_got,
    par_last,
    dwin_ref,
    dpar_ref,
    low_ref,
    ctx_ref,
    up_ref,
    sums_ref,
    keep_ref,
    send_ref,
    par_ref,
):
    join_pieces((par_keep, par_got, par_last), par_ref)
    depth = keep_ref.shape[1]
    half = depth // 4
    query = jnp.sum(dwin_ref[0, :width].astype(F32), axis=1, keepdims=True)
    value = jnp.sum(dwin_ref[0, 2 * width :].astype(F32), axis=1, keepdims=True)
    value = value + jnp.sum(dpar_ref[0, width:].astype(F32), axis=1, keepdims=True)
    by_row = [array[i : i + half] for array in (query, value, up_ref[0]) for i in range(0, array.shape[0], half)]
    by_row = jnp.concatenate(by_row, axis=1)
    by_row = jnp.concatenate([by_row] * 4, axis=0)
    used = by_row.shape[1] + 6
    pad = jnp.zeros((depth, keep_ref.shape[2] - 4 * width - used), F32)
    for part, out_ref in enumerate((keep_ref, send_ref)):
        rows = slice(part * depth, (part + 1) * depth)
        win, par = win_ref[rows], par_ref[rows]
        out_ref[0, :, :width] = nt(win, dwin_ref[0, :width]).astype(BF16)
        for i in range(1, 3):
            grads = nt(win, dwin_ref[0, i * width : (i + 1) * width])
            grads = grads + nt(par, dpar_ref[0, (i - 1) * width : i * width])
            out_ref[0, :, i * width : (i + 1) * width] = grads.astype(BF16)
        out_ref[0, :, 3 * width : 4 * width] = nt(low_ref[rows], ctx_ref[0]).astype(BF16)
        extra = jnp.concatenate([by_row, sums_ref[rows], pad], axis=1)
        out_ref[0, :, 4 * width :] = extra.astype(BF16)


def first_grads(win, par, dwin, dpar, low, ctx, up_bias, sums):
    groups, width, own = ctx.shape
    out = jax.ShapeDtypeStruct((groups, low.shape[0] // 2, 4 * width + 128), BF16)
    return pl.pallas_call(
        functools.partial(first_grad_kernel, width),
        grid=(groups,),
        in_specs=[
            whole_block(win),
            *[whole_block(piece) for piece in par],
            step_block(dwin),
            step_block(dpar),
            whole_block(low),
            step_block(ctx),
            step_block(up_bias),
            whole_block(sums),
        ],
        out_specs=[step_block(out)] * 2,
        out_shape=[out] * 2,
        scratch_shapes=[pltpu.VMEM((low.shape[0], par[0].shape[2]), BF16)],
        compiler_params=params(16),
        cost_estimate=cost(15),
        name="first_grads",
    )(*held(win, *par, dwin, dpar, low, ctx), up_bias, sums)


def token_grad_kernel(high, near_ref, far_ref, dwin_ref, more_ref, keep_ref, along_ref, close_ref, total_ref):
    step, last = pl.program_id(0), pl.num_programs(0) - 1
    depth = near_ref.shape[1]
    own = more_ref.shape[1]

    @pl.when(step == 0)
    def start():
        total_ref[...] = jnp.zeros(total_ref.shape, F32)
        total_ref[:, :own] = more_ref[...].astype(F32)

    grads = dwin_ref[0]
    total_ref[:depth] += nn(near_ref[0, :, :high], grads)
    total_ref[depth:] += nn(far_ref[0, :, :high], grads)

    @pl.when(step == last)
    def finish():
        feat = keep_ref.shape[1]
        for i, out in enumerate((keep_ref.at[0], along_ref.at[0], close_ref.at[0], along_ref.at[1])):
            out[...] = total_ref[i * feat : (i + 1) * feat].astype(BF16)


def token_grads(near, far, dwin, more, columns):
    groups, depth = near.shape[:2]
    feat = depth // 2
    outs = [jax.ShapeDtypeStruct((n, feat, columns), BF16) for n in (1, 2, 1)]
    return pl.pallas_call(
        functools.partial(token_grad_kernel, dwin.shape[1]),
        grid=(groups,),
        in_specs=[
            step_block(near),
            step_block(far),
            pl.BlockSpec((1, dwin.shape[1], columns), lambda step: (step, 0, 0)),
            whole_block(more),
        ],
        out_specs=[whole_block(out) for out in outs],
        out_shape=outs,
        scratch_shapes=[pltpu.VMEM((2 * depth, columns), F32)],
        compiler_params=params(14),
        cost_estimate=cost(30),
        name="token_grads",
    )(near, far, dwin, more)


def turn_kernel(low, near_ref, far_ref, out_ref):
    depth = near_ref.shape[1]
    out_ref[0, :, :depth] = tn(near_ref[0, :, low : low + out_ref.shape[1]], spots(depth, depth, 0)).astype(BF16)
    out_ref[0, :, depth:] = tn(far_ref[0, :, low : low + out_ref.shape[1]], spots(depth, depth, 0)).astype(BF16)


def turn_weights(near, far, low, count):
    groups, depth = near.shape[:2]
    out = jax.ShapeDtypeStruct((groups, count, 2 * depth), BF16)
    return pl.pallas_call(
        functools.partial(turn_kernel, low),
        grid=(groups,),
        in_specs=[step_block(near), step_block(far)],
        out_specs=step_block(out),
        out_shape=out,
        compiler_params=params(12),
        cost_estimate=cost(0.1),
        name="turn_weights",
    )(near, far)


def attend_own(lengths, segments, bank, scalars, window):
    groups, rows, columns = window.shape
    width = rows // 3
    own = sum(lengths)
    outs = (
        jax.ShapeDtypeStruct((groups, width, own), F32),
        jax.ShapeDtypeStruct((groups, width // HEAD, own), F32),
        jax.ShapeDtypeStruct((groups, width // HEAD, own), F32),
    )
    return pl.pallas_call(
        functools.partial(attention_own, width // HEAD, lengths, segments, bank),
        grid=(groups,),
        in_specs=[SMEM] * 3 + [step_block(window)],
        out_specs=[step_block(out) for out in outs],
        out_shape=outs,
        compiler_params=params(14),
        cost_estimate=cost(0.1),
        name="attention_own",
    )(*scalars, window)


def attend_parent(lengths, segments, scalars, window, partial, turned, toks, bias):
    groups, rows, columns = window.shape
    width = rows // 3
    model = turned.shape[2]
    outs = (
        jax.ShapeDtypeStruct((groups, 2 * width, toks[0].shape[2]), BF16),
        jax.ShapeDtypeStruct((groups, width, sum(lengths)), BF16),
        jax.ShapeDtypeStruct((groups, width // HEAD, sum(lengths)), F32),
    )
    return pl.pallas_call(
        functools.partial(attention_parent, width // HEAD, lengths, segments),
        grid=(groups,),
        in_specs=[SMEM] * 2
        + [step_block(array) for array in (window, *partial, turned)]
        + [whole_block(piece) for piece in toks]
        + [step_block(bias)],
        out_specs=[step_block(out) for out in outs],
        out_shape=[in_hbm(outs[0]), *outs[1:]],
        scratch_shapes=[pltpu.VMEM((model, toks[0].shape[2]), BF16)],
        compiler_params=params(36),
        cost_estimate=cost(130),
        name="attention_parent",
    )(*scalars[:2], *held(window), *partial, turned, *toks, bias)


def attend_back(lengths, segments, bank, scalars, window, parent, ctx, dctx, lse, near, far):
    groups, rows, columns = window.shape
    depth = near.shape[1]
    feat = depth // 2
    outs = (jax.ShapeDtypeStruct(window.shape, BF16), jax.ShapeDtypeStruct(parent.shape, BF16))
    sends = [jax.ShapeDtypeStruct((n, feat, columns), BF16) for n in (1, 2, 1)]
    return pl.pallas_call(
        functools.partial(attention_backward, rows // 3 // HEAD, lengths, segments, bank),
        grid=(groups,),
        in_specs=[SMEM] * 3 + [step_block(array) for array in (window, parent, ctx, dctx, lse, near, far)],
        out_specs=[step_block(out) for out in outs] + [whole_block(out) for out in sends],
        out_shape=[*map(in_hbm, outs), *sends],
        scratch_shapes=[pltpu.VMEM((2 * depth, columns), F32)],
        compiler_params=params(24),
        cost_estimate=cost(200),
        name="attention_backward",
    )(*scalars, *held(window, parent, ctx), dctx, lse, *held(near, far))


def swap(array, axis, mask):
    count = lax.axis_size(axis)
    return lax.ppermute(array, axis, [(i, i ^ mask) for i in range(count)])


SMEM = pl.BlockSpec(memory_space=pltpu.SMEM)
VMEM = pl.BlockSpec(memory_space=pltpu.VMEM)
HBM = pl.BlockSpec(memory_space=pltpu.HBM)
ORDER = (0, 2, 1, 3)
SENDS = ((0, 0), (1, 0), (2, 0), (1, 1))


def at_distance(here_ref, lists, slot, j):
    distance = ORDER[slot]
    return static_of(here_ref[1], [lists[i ^ distance][j] for i in range(len(lists))])


def flipped(here_ref, part, half):
    return pl.multiple_of((part ^ here_ref[2]) * half, 32)


def spots(rows, columns, shift):
    return (
        lax.broadcasted_iota(jnp.int32, (rows, columns), 0) + shift
        == lax.broadcasted_iota(jnp.int32, (rows, columns), 1)
    ).astype(BF16)


def as_row(ref):
    return ref[...].astype(F32).reshape(1, ref.shape[0])


def fetch(pairs, sem):
    copies = [pltpu.make_async_copy(source, target, sem.at[i]) for i, (source, target) in enumerate(pairs)]
    for copy in copies:
        copy.start()
    for copy in copies:
        copy.wait()


def pack_weights_kernel(here_ref, *refs):
    count = 9
    inputs, half_ref = refs[:count], refs[count]
    held, turned_ref, sem = refs[count + 1 : -2], refs[-2], refs[-1]
    feat, width = inputs[0].shape
    half = feat // 2
    rows = pl.ds(flipped(here_ref, 0, half), half)
    small = [inputs[i] for i in (0, 1, 2, 3, 6, 7, 8)]
    fetch(
        [*zip(small, held)]
        + [(inputs[4 + i].at[rows, :], half_ref.at[pl.ds((1 + i) * half, half), :]) for i in range(2)],
        sem,
    )
    query_ref, key_ref, value_ref, out_ref, up_b_ref, query_b_ref, value_b_ref = held
    turned_ref[...] = tn(out_ref[...], spots(width, width, 0)).astype(BF16)
    for i, ref in enumerate((query_ref, key_ref, value_ref, turned_ref)):
        half_ref[:half, i * width : (i + 1) * width] = ref[rows, :]
    zero = jnp.zeros((1, width), F32)
    joint = [as_row(query_b_ref), zero, as_row(value_b_ref), zero]
    wide = (half_ref.shape[0] - 3 * half, half_ref.shape[1])
    index = lax.broadcasted_iota(jnp.int32, wide, 0)
    up_row = jnp.broadcast_to(as_row(up_b_ref), wide)
    joint_row = jnp.broadcast_to(jnp.concatenate(joint, axis=1), wide)
    half_ref[3 * half :] = jnp.where(index == 0, up_row, jnp.where(index == 1, joint_row, 0.0)).astype(BF16)


def pack_weights(here, query, key, value, out, up, down, *biases):
    feat, width = query.shape
    hidden = up.shape[1]
    inputs = (query, key, value, out, up, down, *biases)
    small = [query, key, value, out, *biases]
    return pl.pallas_call(
        pack_weights_kernel,
        in_specs=[SMEM] + [HBM] * len(inputs),
        out_specs=VMEM,
        out_shape=jax.ShapeDtypeStruct((3 * feat // 2 + 8, hidden), BF16),
        scratch_shapes=[pltpu.VMEM(array.shape, array.dtype) for array in small]
        + [pltpu.VMEM((feat, width), BF16), pltpu.SemaphoreType.DMA((len(inputs),))],
        compiler_params=params(6),
        cost_estimate=cost(0.1),
        name="pack_weights",
    )(here, *held(*inputs))


def pack_kernel(blocks, sided, here_ref, *refs):
    given = 1 + sided
    outs, held, sem = refs[given : given + 3], refs[given + 3 : given + 3 + given], refs[-1]
    fetch([*zip(refs[:given], held)], sem)
    source_ref = held[0]
    half = source_ref.shape[0] // 2
    count = len(blocks[0])
    if sided:
        mem_ref, vector_refs, side_ref = held[1], held[2:], refs[-2]
        bank = mem_ref.shape[0]
        vectors = jnp.concatenate([as_row(ref) for ref in vector_refs], axis=0)
        vectors = jnp.concatenate([vectors, jnp.zeros((8 - len(vector_refs), vectors.shape[1]), F32)], axis=0)
        side = tn(mem_ref[...], spots(bank, 128, 0)) + tn(vectors.astype(BF16), spots(8, 128, bank))
        side_ref[...] = side.astype(BF16)
    for slot, (out, place) in enumerate(SENDS):
        for part in range(2):
            low = flipped(here_ref, part, half)
            rows = slice(part * half, (part + 1) * half)
            for j in range(count):
                at = pl.multiple_of(at_distance(here_ref, blocks, slot, j) * 128, 128)
                outs[out][place, rows, j * 128 : (j + 1) * 128] = source_ref[pl.ds(low, half), pl.ds(at, 128)]
            if sided:
                outs[out][place, rows, count * 128 :] = side_ref[pl.ds(low, half), :]


def pack(blocks, here, source, *side):
    feat = source.shape[0]
    columns = len(blocks[0]) * 128 + (128 if side else 0)
    inputs = (source, *side)
    return pl.pallas_call(
        functools.partial(pack_kernel, blocks, len(side)),
        in_specs=[SMEM] + [HBM] * len(inputs),
        out_specs=[VMEM] * 3,
        out_shape=[jax.ShapeDtypeStruct((n, feat, columns), source.dtype) for n in (1, 2, 1)],
        scratch_shapes=[pltpu.VMEM(array.shape, array.dtype) for array in inputs]
        + ([pltpu.VMEM((feat, 128), BF16)] if side else [])
        + [pltpu.SemaphoreType.DMA((len(inputs),))],
        compiler_params=params(12),
        cost_estimate=cost(0.1),
        name="pack",
    )(here, *held(*inputs))


def exchange(keep, along, near):
    got = swap(along, "col", 2)
    return keep, got, swap(jnp.concatenate([near, got[1:]], axis=0), "col", 1)


def joined(pieces):
    keep, got, last = pieces
    return jnp.concatenate([keep, got[:1], last], axis=0)


PIECES = ((0, 0), (1, 0), (2, 0), (2, 1))


def parent_of(here_ref, parents_ref, segments, slot, j):
    return parents_ref[here_ref[0] * here_ref[3] + at_distance(here_ref, segments, slot, j)]


def pick_kernel(segments, here_ref, parents_ref, source_ref, *refs):
    outs, sem = refs[:3], refs[3]
    half = source_ref.shape[1] // 2
    seg_row = here_ref[3]
    pairs = []
    for slot, (out, place) in enumerate(SENDS):
        for j in range(len(segments[0])):
            seg = jnp.maximum(parent_of(here_ref, parents_ref, segments, slot, j), 0)
            row = lax.div(seg, seg_row)
            at = pl.multiple_of((seg - row * seg_row) * SEG, SEG)
            for part in range(2):
                rows = slice(part * half, (part + 1) * half)
                source = source_ref.at[row, pl.ds(flipped(here_ref, part, half), half), pl.ds(at, SEG)]
                pairs.append((source, outs[out].at[place, rows, pl.ds(j * SEG, SEG)]))
    fetch(pairs, sem)


def pick_parents(segments, here, parents, gathered):
    feat = gathered.shape[1]
    columns = len(segments[0]) * SEG
    return pl.pallas_call(
        functools.partial(pick_kernel, segments),
        in_specs=[SMEM, SMEM, HBM],
        out_specs=[VMEM] * 3,
        out_shape=[jax.ShapeDtypeStruct((n, feat, columns), gathered.dtype) for n in (1, 2, 1)],
        scratch_shapes=[pltpu.SemaphoreType.DMA((8 * len(segments[0]),))],
        compiler_params=params(8),
        cost_estimate=cost(1),
        name="pick_parents",
    )(here, parents, *held(gathered))


def add_parents_kernel(segments, seg_row, here_ref, parents_ref, *refs):
    pieces, given_ref, out_ref, sem = refs[:3], refs[3], refs[4], refs[5]
    window = len(segments[0]) * SEG
    out_ref[:, :, : seg_row * SEG] = jnp.zeros((out_ref.shape[0], out_ref.shape[1], seg_row * SEG), BF16)
    for slot, (piece, place) in enumerate(PIECES):
        for j in range(len(segments[0])):
            seg = parent_of(here_ref, parents_ref, segments, slot, j)

            @pl.when(seg >= 0)
            def add(seg=seg, piece=piece, place=place, cols=slice(j * SEG, (j + 1) * SEG)):
                row = lax.div(seg, jnp.int32(seg_row))
                at = pl.ds(pl.multiple_of((seg - row * seg_row) * SEG, SEG), SEG)
                total = out_ref[row, :, at].astype(F32) + pieces[piece][place, :, cols].astype(F32)
                out_ref[row, :, at] = total.astype(BF16)

    mem = sum(pieces[piece][place, :, window:].astype(F32) for piece, place in PIECES).astype(BF16)
    copies = []
    for r in range(out_ref.shape[0]):
        out_ref[r, :, seg_row * SEG :] = mem
        copies.append(pltpu.make_async_copy(out_ref.at[r], given_ref.at[r], sem.at[r]))
        copies[-1].start()
    for copy in copies:
        copy.wait()


def add_parents(segments, here, parents, pieces, rows, seg_row):
    feat, columns = pieces[0].shape[1:]
    bank = columns - len(segments[0]) * SEG
    return pl.pallas_call(
        functools.partial(add_parents_kernel, segments, seg_row),
        in_specs=[SMEM, SMEM, VMEM, VMEM, VMEM],
        out_specs=HBM,
        out_shape=pltpu.HBM((rows, feat, seg_row * SEG + bank), BF16),
        scratch_shapes=[
            pltpu.VMEM((rows, feat, seg_row * SEG + bank), BF16),
            pltpu.SemaphoreType.DMA((rows,)),
        ],
        compiler_params=params(16),
        cost_estimate=cost(60),
        name="add_parents",
    )(here, parents, *pieces)


def finish_kernel(blocks, here_ref, placed_ref, *refs):
    pieces, out_ref = refs[:3], refs[3]
    half = out_ref.shape[0] // 2
    for part in range(2):
        low = flipped(here_ref, part, half)
        rows = slice(part * half, (part + 1) * half)
        out_ref[pl.ds(low, half), :] = placed_ref[rows, : out_ref.shape[1]].astype(F32)
        for slot, (piece, place) in enumerate(PIECES):
            for j in range(len(blocks[0])):
                at = pl.multiple_of(at_distance(here_ref, blocks, slot, j) * 128, 128)
                out_ref[pl.ds(low, half), pl.ds(at, 128)] += pieces[piece][
                    place, rows, j * 128 : (j + 1) * 128
                ].astype(F32)


def finish_tokens(blocks, here, placed, pieces, columns):
    return pl.pallas_call(
        functools.partial(finish_kernel, blocks),
        in_specs=[SMEM, VMEM, VMEM, VMEM, VMEM],
        out_specs=VMEM,
        out_shape=jax.ShapeDtypeStruct((placed.shape[0], columns), F32),
        compiler_params=params(10),
        cost_estimate=cost(2.5),
        name="finish_tokens",
    )(here, placed, *pieces)


def place_kernel(blocks, here_ref, *refs):
    pieces, out_ref = refs[:3], refs[3]
    half = out_ref.shape[0] // 2
    for part in range(2):
        low = flipped(here_ref, part, half)
        rows = slice(part * half, (part + 1) * half)
        for slot, (piece, place) in enumerate(PIECES):
            for j in range(pieces[0].shape[2] // 128):
                at = pl.multiple_of(at_distance(here_ref, blocks, slot, j) * 128, 128)
                out_ref[pl.ds(low, half), pl.ds(at, 128)] = pieces[piece][place, rows, j * 128 : (j + 1) * 128]


def place(blocks, here, pieces, columns):
    return pl.pallas_call(
        functools.partial(place_kernel, blocks),
        in_specs=[SMEM, VMEM, VMEM, VMEM],
        out_specs=VMEM,
        out_shape=jax.ShapeDtypeStruct((pieces[0].shape[1], columns), pieces[0].dtype),
        compiler_params=params(6),
        cost_estimate=cost(1.7),
        name="place",
    )(here, *pieces)


def unpack_kernel(width, count, here_ref, mine_ref, other_ref, *refs):
    weights, out_ref, by_row, by_col, all_ref = refs[:3], refs[3], refs[4:7], refs[7:13], refs[13]
    half = mine_ref.shape[0]
    all_ref[pl.ds(flipped(here_ref, 0, half), half), :] = mine_ref[...].astype(F32)
    all_ref[pl.ds(flipped(here_ref, 1, half), half), :] = other_ref[...].astype(F32)
    for i, ref in enumerate(weights):
        ref[...] = all_ref[:, i * width : (i + 1) * width]
    out_ref[...] = all_ref[:, 3 * width : 4 * width].T
    rows = all_ref[:, 4 * width :].T
    flat = jnp.concatenate([rows[i : i + 1, :half] for i in range(count)], axis=1)
    at = 0
    for ref in by_row:
        size = ref.shape[0]
        ref[...] = flat[:, at : at + size].reshape(size)
        at += size
    for i, ref in enumerate(by_col):
        ref[...] = rows[count + i : count + i + 1].reshape(ref.shape[0])


def unpack(here, mine, other, width, hidden):
    feat = 2 * mine.shape[0]
    count = (2 * width + hidden) // mine.shape[0]
    shapes = [(feat, width)] * 3 + [(width, feat)] + [(width,), (width,), (hidden,)] + [(feat,)] * 6
    return pl.pallas_call(
        functools.partial(unpack_kernel, width, count),
        in_specs=[SMEM, VMEM, VMEM],
        out_specs=[VMEM] * len(shapes),
        out_shape=[jax.ShapeDtypeStruct(shape, F32) for shape in shapes],
        scratch_shapes=[pltpu.VMEM((feat, mine.shape[1]), F32)],
        compiler_params=params(4),
        cost_estimate=cost(2),
        name="unpack",
    )(here, mine, other)


def gather_weights(half):
    return [half] + [swap(half, "row", n) for n in range(1, lax.axis_size("row"))]


def spread_weights(along, *gate):
    along = jnp.stack(along, axis=1)
    opposite = swap(along, "leaf", 1)
    across = after(swap(along, "col", 2), *gate)
    return along, opposite, across, swap(across, "leaf", 1)


def whole_weights(parts):
    near = jnp.stack(parts, axis=2)
    arrays, rows, blocks, depth, columns = near.shape
    near = near.reshape(arrays, rows, blocks * depth, columns)
    return near, swap(near, "col", 1)


def add_up(*terms):
    total = terms[0].astype(F32)
    for term in terms[1:]:
        total = total + term.astype(F32)
    return total


def reduce_blocks(keep):
    rows, features, columns = keep.shape
    return rows, 2, 2, features // 4, columns


def reduce_across(keep, near):
    shape = reduce_blocks(keep)
    return add_up(keep.reshape(shape)[:, :, 1], near.reshape(shape)[:, :, 1]).astype(BF16)


def reduce_y(keep, near):
    shape = reduce_blocks(keep)
    return add_up(keep.reshape(shape)[:, 1], near.reshape(shape)[:, 1]).astype(BF16)


def reduce_x(keep, near, got):
    shape = reduce_blocks(keep)
    return add_up(keep.reshape(shape)[:, 0, 1], near.reshape(shape)[:, 0, 1], got[:, 1]).astype(BF16)


def reduce_up(keep, near, across):
    shape = reduce_blocks(keep)
    return add_up(keep.reshape(shape)[:, 1, 0], near.reshape(shape)[:, 1, 0], across[:, 1]).astype(BF16)


def reduce_along(keep, near, across, up):
    shape = reduce_blocks(keep)
    mine = add_up(keep.reshape(shape)[:, 0, 0], near.reshape(shape)[:, 0, 0], across[:, 0], up)
    return [mine[n].astype(BF16) for n in range(shape[0])]


def reduce_rows(along, got):
    total = add_up(along[0], *got)
    mask = 2
    while mask < lax.axis_size("leaf"):
        total = add_up(total, swap(total.astype(BF16), "leaf", mask))
        mask *= 2
    return total.astype(BF16)


def reduce_corner(keep, near):
    shape = reduce_blocks(keep)
    middle = shape[0] // 2
    corner = add_up(keep.reshape(shape)[:, 1, 1], near.reshape(shape)[:, 1, 1]).astype(BF16)
    return corner[:middle], corner[middle:]


def reduce_edges(keep, near, by_leaf, by_col):
    shape = reduce_blocks(keep)
    middle = shape[0] // 2
    keep, near = keep.reshape(shape), near.reshape(shape)
    leaf = add_up(keep[:, 0, 1], near[:, 0, 1])
    leaf = jnp.concatenate([leaf[:middle], add_up(leaf[middle:], by_col)], axis=0).astype(BF16)
    along = add_up(keep[:, 1, 0], near[:, 1, 0])
    along = jnp.concatenate([add_up(along[:middle], by_leaf), along[middle:]], axis=0).astype(BF16)
    return leaf, along


def reduce_mine(keep, near, leaf, along):
    shape = reduce_blocks(keep)
    mine = add_up(keep.reshape(shape)[:, 0, 0], near.reshape(shape)[:, 0, 0], leaf, along)
    return [mine[n].astype(BF16) for n in range(shape[0])]


def send_rows(along):
    return [swap(block, "row", n) for n, block in enumerate(along) if n]


def norm_stats(values):
    center = jnp.mean(values, axis=0, keepdims=True)
    spread = jnp.mean(values * values, axis=0, keepdims=True) - center * center
    return center, lax.rsqrt(spread + EPSILON)


def norm_back(grad, normed, scale, gain):
    scaled = grad * gain
    return scale * (
        scaled
        - jnp.mean(scaled, axis=0, keepdims=True)
        - normed * jnp.mean(scaled * normed, axis=0, keepdims=True)
    )


def lane_sum(array):
    return jnp.sum(array, axis=-1, dtype=F32)


def on_device(
    tokens,
    memory,
    parents,
    memory_slots,
    query_weight,
    query_bias,
    key_weight,
    value_weight,
    value_bias,
    out_weight,
    out_bias,
    norm_gain,
    norm_shift,
    up_weight,
    up_bias,
    down_weight,
    down_bias,
    final_gain,
    final_shift,
    cotangent,
):
    rows, cols = lax.axis_size("row"), lax.axis_size("col")
    row, col = lax.axis_index("row"), lax.axis_index("col")
    feat, row_tokens = tokens.shape
    own = row_tokens // cols
    seg_row = row_tokens // SEG
    model = feat * cols
    width = query_weight.shape[1]
    hidden_width = up_weight.shape[1]
    bank = memory.shape[0]
    segments, ranges = plan_windows(own, cols)
    window = len(segments[0]) * SEG
    tail = 128
    lengths = tuple(min(SEG, own - j * SEG) for j in range(len(segments[0])))
    half = feat // 2
    parity = lax.axis_index("leaf") % 2
    here = jnp.stack([row, col, parity, jnp.int32(seg_row)]).astype(jnp.int32)
    blocks = [[b for a, n in ranges[i] for b in range(a // 128, (a + n) // 128)] for i in range(cols)]
    own_blocks = [each[: own // 128] for each in blocks]
    scalars = (here, parents, memory_slots)

    weight_half = pack_weights(
        here, query_weight, key_weight, value_weight, out_weight, up_weight, down_weight, up_bias, query_bias, value_bias
    )
    along = gather_weights(weight_half)

    vectors = (out_bias, norm_gain, norm_shift, down_bias, final_gain, final_shift)
    token_sends = pack(blocks, here, after(tokens, weight_half), memory, *vectors)
    cot_sends = pack(own_blocks, here, after(cotangent, token_sends))
    token_got = swap(token_sends[1], "col", 2)
    along = after(along, cot_sends)
    everything = lax.all_gather(after(tokens, along), "row", axis=0)
    row_vectors = jnp.stack([piece[3 * half :] for piece in along])
    first_parts = spread_weights([piece[:half][None] for piece in along])
    near_first, far_first = (array[0] for array in whole_weights(after(first_parts, token_got)))
    token_last = swap(jnp.concatenate([token_sends[2], token_got[1:]], axis=0), "col", 1)
    tok_window = joined((token_sends[0], token_got, token_last)).reshape(model, window + tail)
    win = project(near_first, far_first, tok_window, row_vectors, 0, 3 * width, width)
    partial = attend_own(lengths, segments, bank, scalars, win)
    second_parts = spread_weights([piece[half : 3 * half].reshape(2, half, -1) for piece in along], partial)
    cot_keep, cot_along, cot_near = after(cot_sends, second_parts[2])
    cot_got = swap(cot_along, "col", 2)
    cot_near = jnp.concatenate([cot_near, cot_got[1:]], axis=0)
    cot_pieces = cot_keep, cot_got, swap(cot_near, "col", 1)
    turned = turn_weights(after(near_first, second_parts[2]), far_first, width, 2 * width)
    everything = after(everything, second_parts[2], cot_near, turned)
    par_keep, par_along, par_near = pick_parents(segments, here, parents, everything)
    par_got = swap(par_along, "col", 2)
    near, far = whole_weights(after(second_parts, par_along))
    par_got = after(par_got, near)
    par_near = jnp.concatenate([par_near, par_got[1:]], axis=0)
    tok_parent = (par_keep, par_got, swap(par_near, "col", 1))
    par, ctx, lse = attend_parent(
        lengths, segments, scalars, win, partial, turned, tok_parent, row_vectors
    )
    at = window + bank
    *result, active, upper_low, hidden_low, down_low, first_low, dctx, up_bias_grad, sums = mlp(
        at, ctx, tok_window, cot_pieces, near_first, far_first, near, far, row_vectors
    )
    result_keep, result_along, result_near = result
    dwin, dpar, par_keep, par_along, par_near = attend_back(
        lengths, segments, bank, scalars, win, par, ctx, dctx, lse, near_first, far_first
    )

    par_got = swap(par_along, "col", 2)
    down_keep, down_send, up_keep, up_send = hidden_grads(after(down_low, par_along), hidden_low, active, upper_low)
    down_near, up_near = swap(down_send, "col", 1), swap(up_send, "col", 1)
    par_got = after(par_got, up_send)
    par_near = jnp.concatenate([par_near, par_got[1:]], axis=0)
    placed = add_parents(segments, here, parents, (par_keep, par_got, swap(par_near, "col", 1)), rows, seg_row)
    down_across = reduce_across(after(down_keep, placed), down_near)
    up_along = reduce_y(after(up_keep, down_across), up_near)
    first_keep, first_send = first_grads(
        tok_window, tok_parent, dwin, dpar, after(first_low, up_along), ctx, up_bias_grad, sums
    )
    placed = lax.psum_scatter(placed, "row", scatter_dimension=0, tiled=False)
    first_near = swap(first_send, "col", 1)
    dtok = token_grads(near_first, far_first, dwin, after(first_low, first_send), window)
    corner = reduce_corner(after(first_keep, dtok), first_near)
    by_leaf, by_col = swap(corner[0], "leaf", 1), swap(corner[1], "col", 2)
    up_got = swap(up_along, "col", 2)
    up_across = reduce_x(after(up_keep, corner), up_near, up_got)
    down_across = swap(down_across, "leaf", 1)
    down_up = reduce_up(after(down_keep, up_across), down_near, down_across)
    edges = reduce_edges(after(first_keep, down_up), first_near, by_leaf, by_col)
    by_leaf, by_col = swap(edges[0], "leaf", 1), swap(edges[1], "col", 2)
    up_across = swap(up_across, "leaf", 1)
    up_rows = reduce_mine(after(up_keep, edges), up_near, up_got[:, 0], up_across)
    down_up = swap(down_up, "col", 2)
    down_rows = reduce_along(after(down_keep, up_rows), down_near, down_across, down_up)
    result_got = after(swap(result_along, "col", 2), down_rows)
    result_near = jnp.concatenate([result_near, result_got[1:]], axis=0)
    result_pieces = result_keep, result_got, swap(result_near, "col", 1)
    first_rows = reduce_mine(after(first_keep, down_rows), first_near, by_leaf, by_col)
    dtok_keep, dtok_along, dtok_near = dtok
    dtok_got = after(swap(after(dtok_along, edges), "col", 2), first_rows, result_near)
    dtok_near = jnp.concatenate([dtok_near, dtok_got[1:]], axis=0)
    layer_output = place(own_blocks, here, result_pieces, row_tokens)
    mem_sum = placed[:, row_tokens : row_tokens + bank].astype(F32)
    memory_grad = jnp.where(parity == 0, mem_sum, jnp.roll(mem_sum, half, axis=0)).T
    tokens_grad = finish_tokens(
        blocks, here, placed, (dtok_keep, dtok_got, swap(dtok_near, "col", 1)), row_tokens
    )
    down_got, up_got, first_got = send_rows(down_rows), send_rows(up_rows), send_rows(first_rows)
    down_rows, up_rows = after((down_rows, up_rows), first_rows)
    second_mine = jnp.concatenate([reduce_rows(down_rows, down_got), reduce_rows(up_rows, up_got)], axis=1)
    second_other = swap(second_mine, "leaf", 1)
    first_mine = reduce_rows(after(first_rows, second_mine, tokens_grad, memory_grad, layer_output), first_got)
    first_other = swap(first_mine, "leaf", 1)

    def in_order(mine, other):
        return jnp.where(
            parity == 0, jnp.concatenate([mine, other], axis=0), jnp.concatenate([other, mine], axis=0)
        ).astype(F32)

    second_total = in_order(second_mine, second_other)
    down_total, up_total = second_total[:, :hidden_width], second_total[:, hidden_width:]
    first_query, first_key, first_value, first_out, query_sum, value_sum, up_sum, *by_col = unpack(
        here, first_mine, first_other, width, hidden_width
    )

    return (
        layer_output,
        tokens_grad,
        memory_grad,
        first_query,
        query_sum,
        first_key,
        first_value,
        value_sum,
        first_out,
        by_col[0],
        by_col[1],
        by_col[2],
        up_total,
        up_sum,
        down_total,
        by_col[3],
        by_col[4],
        by_col[5],
    )


def solution(mesh):
    return jax.shard_map(
        on_device,
        mesh=mesh,
        in_specs=(
            P("col", ("leaf", "row")),
            P("leaf", "col"),
            P("leaf"),
            P("leaf", None),
            P("col", "row"),
            P("row"),
            P("col", "row"),
            P("col", "row"),
            P("row"),
            P("row", "col"),
            P("col"),
            P("col"),
            P("col"),
            P("col", "row"),
            P("row"),
            P("col", "row"),
            P("col"),
            P("col"),
            P("col"),
            P("col", ("leaf", "row")),
        ),
        out_specs=(
            P("col", ("leaf", "row")),
            P("col", ("leaf", "row")),
            P("leaf", "col"),
            P("col", "row"),
            P("row"),
            P("col", "row"),
            P("col", "row"),
            P("row"),
            P("row", "col"),
            P("col"),
            P("col"),
            P("col"),
            P("col", "row"),
            P("row"),
            P("col", "row"),
            P("col"),
            P("col"),
            P("col"),
        ),
        check_vma=False,
    )
```
